32 devices in a mesh: narrow: 2 (over x), wide: 16 (over z, y, core).
Axes of the slice: x: 2, y: 2, z: 4, core: 2. Of those that a mesh axis runs over, the one named last changes fastest.
Arguments:
- patches: bfloat16 [64, 256, 1152], P(('narrow', 'wide')), may hold values from -6 to 6
- condition: float32 [64, 1152], P(('narrow', 'wide')), may hold values from -6 to 6
- image_counts: int32 [32], P(('narrow', 'wide')), may hold values from 1 to 2, as said below
- ada_weight: bfloat16 [1152, 6912], P(None, 'wide'), may hold values from -0.1875 to 0.1875
- ada_bias: bfloat16 [6912], P('wide'), may hold values from -3 to 3
- inproj_weight: bfloat16 [1152, 3456], P('wide'), may hold values from -0.1875 to 0.1875
- inproj_bias: bfloat16 [2304], P('wide'), may hold values from -2 to 2
- outproj_weight: bfloat16 [1152, 1152], P('wide'), may hold values from -0.75 to 0.75
- outproj_bias: bfloat16 [1152], P('wide'), may hold values from -2 to 2
- up_weight: bfloat16 [1152, 4608], P('wide'), may hold values from -0.1875 to 0.1875
- up_bias: bfloat16 [4608], P('wide'), may hold values from -3 to 3
- down_weight: bfloat16 [4608, 1152], P('wide'), may hold values from -0.09375 to 0.09375
- down_bias: bfloat16 [1152], P('wide'), may hold values from -2 to 2
- cotangent: bfloat16 [64, 256, 1152], P(('narrow', 'wide')), may hold values from -6 to 6
Outputs:
- output: bfloat16 [64, 256, 1152], P(('narrow', 'wide'))
- grad_patches: bfloat16 [64, 256, 1152], P(('narrow', 'wide'))
- grad_condition: float32 [64, 1152], P(('narrow', 'wide'))
- grad_ada_weight: float32 [1152, 6912], P(None, 'wide')
- grad_ada_bias: float32 [6912], P('wide')
- grad_inproj_weight: float32 [1152, 3456], P('wide')
- grad_inproj_bias: float32 [2304], P('wide')
- grad_outproj_weight: float32 [1152, 1152], P('wide')
- grad_outproj_bias: float32 [1152], P('wide')
- grad_up_weight: float32 [1152, 4608], P('wide')
- grad_up_bias: float32 [4608], P('wide')
- grad_down_weight: float32 [4608, 1152], P('wide')
- grad_down_bias: float32 [1152], P('wide')
The draws below stay inside these ranges and needn't reach their ends.
Inputs may be any that keep to these rules, and one draw needn't show every extreme that they name: `image_counts`: each device's number of live image slots; a device's live slots are its first ones. In every draw some device has 2 and some device has 1.
All inputs are finite; a program needn't handle non-finite values.
Results may differ from the reference program's by a relative error of at most 0.02.
The reference program's roundings to bfloat16 on the way count: a program that leaves them out, or rounds other values in their place, can miss the bound.
Values may be sent and summed in bfloat16 or wider, within the bound.
A program may use at most 192 MiB of HBM per device.

```python
import math
import jax
import jax.numpy as jnp
from jax import lax

D = 1152
HEADS = 16
FF = 4608
SEQ = 256
SLOTS = 2
IMAGES = 64


def draw_image_counts(key, part):
    device_total = IMAGES // SLOTS
    counts = jax.random.randint(jax.random.fold_in(key, 11), (device_total,), 1, SLOTS + 1)
    fullest = jax.random.randint(jax.random.fold_in(key, 12), (), 0, device_total)
    offset = jax.random.randint(jax.random.fold_in(key, 13), (), 1, device_total)
    emptiest = (fullest + offset) % device_total
    counts = counts.at[fullest].set(SLOTS)
    counts = counts.at[emptiest].set(1)
    return counts.astype(jnp.int32)


def steps_of(stream_key, extent, cuts, low, high):
    def one(axis_at, blocks):
        steps = jax.random.uniform(jax.random.fold_in(jax.random.fold_in(stream_key, 6), axis_at), (blocks,), jnp.float32, low / len(cuts), high / len(cuts))
        return jnp.repeat(jnp.exp(steps), extent[axis_at] // blocks).reshape((-1,) + (1,) * (len(extent) - axis_at - 1))

    gain = one(*cuts[0])
    for cut in cuts[1:]:
        gain = gain * one(*cut)
    return gain


def normal_values(key, dims, width, limit, shards=(), dtype=jnp.bfloat16):
    level = steps_of(key, dims, shards, -0.22, 0.18) if shards else 1.0
    values = jax.random.normal(key, dims, jnp.float32) * width * level
    return jnp.minimum(jnp.maximum(values, -limit), limit).astype(dtype)


def setup_inputs(seed: int = 0) -> dict:
    arg_keys = jax.random.split(jax.random.key(seed), 15)
    patches = normal_values(arg_keys[0], (IMAGES, SEQ, D), 1.0, 6.0, ((0, 32),))
    condition = normal_values(arg_keys[1], (IMAGES, D), 1.0, 6.0, ((0, 32),), jnp.float32)
    image_counts = draw_image_counts(jax.random.fold_in(arg_keys[14], 71), 0)
    ada_weight = normal_values(arg_keys[3], (D, 6 * D), D ** -0.5, 0.1875, ((1, 16),))
    ada_bias = normal_values(arg_keys[4], (6 * D,), 0.5, 3.0, ((0, 16),))
    inproj_weight = normal_values(arg_keys[5], (D, 3 * D), D ** -0.5, 0.1875, ((0, 16),))
    inproj_bias = normal_values(arg_keys[6], (2 * D,), 0.3, 2.0, ((0, 16),))
    outproj_weight = normal_values(arg_keys[7], (D, D), (D // 16) ** -0.5, 0.75, ((0, 16),))
    outproj_bias = normal_values(arg_keys[8], (D,), 0.3, 2.0, ((0, 16),))
    up_weight = normal_values(arg_keys[9], (D, FF), D ** -0.5, 0.1875, ((0, 16),))
    up_bias = normal_values(arg_keys[10], (FF,), 0.5, 3.0, ((0, 16),))
    down_weight = normal_values(arg_keys[11], (FF, D), FF ** -0.5, 0.09375, ((0, 16),))
    down_bias = normal_values(arg_keys[12], (D,), 0.3, 2.0, ((0, 16),))
    cotangent = normal_values(arg_keys[13], (IMAGES, SEQ, D), 1.0, 6.0, ((0, 32),))
    return {"patches": patches, "condition": condition, "image_counts": image_counts, "ada_weight": ada_weight, "ada_bias": ada_bias, "inproj_weight": inproj_weight, "inproj_bias": inproj_bias, "outproj_weight": outproj_weight, "outproj_bias": outproj_bias, "up_weight": up_weight, "up_bias": up_bias, "down_weight": down_weight, "down_bias": down_bias, "cotangent": cotangent}


@jax.custom_vjp
def lower_precision(v):
    return lax.optimization_barrier(v.astype(jnp.bfloat16)).astype(jnp.float32)

@jax.custom_vjp
def low_back(v):
    return v

def low_keep(v):
    return (lower_precision(v), None)

def low_pass(kept, grad):
    return (grad,)

def back_keep(v):
    return (v, None)

def back_low(kept, grad):
    return (lower_precision(grad),)
lower_precision.defvjp(low_keep, low_pass)
low_back.defvjp(back_keep, back_low)
highest = lax.Precision.HIGHEST

def layer_normalize(values):
    center = lax.optimization_barrier(jnp.mean(values, axis=-1, keepdims=True))
    shifted = values - center
    return shifted * lax.rsqrt(lax.optimization_barrier(jnp.mean(shifted * shifted, axis=-1, keepdims=True)) + 1e-06)

def block_group(weights, group_input, group_mod, group_live):
    w_inproj, b_inproj, w_outproj, b_outproj, w_up, b_up, w_down, b_down = weights
    images, seq_len, model_width = group_input.shape
    head_dim = model_width // HEADS
    segment_list = [group_mod[:, None, number * model_width:(number + 1) * model_width] for number in range(6)]
    selfattn_offset, selfattn_scale, selfattn_gate, perceptron_offset, perceptron_scale, perceptron_gate = segment_list
    first_input = lower_precision(layer_normalize(group_input) * (1.0 + selfattn_scale) + selfattn_offset)
    full_bias = jnp.concatenate([b_inproj[:model_width], jnp.zeros((model_width,), jnp.float32), b_inproj[model_width:]])
    projected = jnp.einsum('gsd,de->gse', first_input, w_inproj, precision=highest) + full_bias
    projected = lower_precision(low_back(projected))
    query_rows = projected[..., :model_width].reshape(images, seq_len, HEADS, head_dim)
    key_rows = projected[..., model_width:2 * model_width].reshape(images, seq_len, HEADS, head_dim)
    value_rows = projected[..., 2 * model_width:].reshape(images, seq_len, HEADS, head_dim)
    scores = jnp.einsum('gqhe,gkhe->ghqk', query_rows, key_rows, precision=highest) * head_dim ** (-0.5)
    scores = low_back(scores)
    probs = lower_precision(jax.nn.softmax(scores, axis=-1))
    attended = jnp.einsum('ghqk,gkhe->gqhe', probs, value_rows, precision=highest).reshape(images, seq_len, model_width)
    attended = lower_precision(low_back(attended))
    residual_branch = low_back(jnp.einsum('gsd,de->gse', attended, w_outproj, precision=highest) + b_outproj)
    between_state = group_input + selfattn_gate * residual_branch
    second_in = lower_precision(layer_normalize(between_state) * (1.0 + perceptron_scale) + perceptron_offset)
    hidden = low_back(jnp.einsum('gsd,de->gse', second_in, w_up, precision=highest) + b_up)
    activated = lower_precision(jax.nn.gelu(hidden, approximate=True))
    mlp_out = low_back(jnp.einsum('gsf,fd->gsd', activated, w_down, precision=highest) + b_down)
    return (between_state + perceptron_gate * mlp_out) * group_live[:, None, None]

def forward(patches, condition, ada_weight, ada_bias, w_inproj, b_inproj, w_outproj, b_outproj, w_up, b_up, w_down, b_down, live):
    cond_act = lower_precision(jax.nn.silu(condition))
    modulation = jnp.dot(cond_act, ada_weight, precision=highest) + ada_bias
    modulation = lower_precision(low_back(modulation))
    group = math.gcd(IMAGES, max(1, 4096 // SEQ))
    steps_count = IMAGES // group
    weights = (w_inproj, b_inproj, w_outproj, b_outproj, w_up, b_up, w_down, b_down)
    items = (patches.reshape(steps_count, group, SEQ, D), modulation.reshape(steps_count, group, 6 * D), live.reshape(steps_count, group))

    def step_fn(carry, item):
        return (carry, block_group(weights, item[0], item[1], item[2]))
    _, results = lax.scan(jax.checkpoint(step_fn), jnp.zeros((), jnp.float32), items)
    return results.reshape(IMAGES, SEQ, D)

def reference(patches, condition, image_counts, ada_weight, ada_bias, inproj_weight, inproj_bias, outproj_weight, outproj_bias, up_weight, up_bias, down_weight, down_bias, cotangent):
    slot_number = jnp.arange(IMAGES) % SLOTS
    owner = jnp.arange(IMAGES) // SLOTS
    live = (slot_number < image_counts[owner]).astype(jnp.float32)
    floats = [value.astype(jnp.float32) for value in (patches, condition, ada_weight, ada_bias, inproj_weight, inproj_bias, outproj_weight, outproj_bias, up_weight, up_bias, down_weight, down_bias)]

    def wrapped(*arrays):
        return forward(*arrays, live)
    result, pullback = jax.vjp(wrapped, *floats)
    grads = pullback(cotangent.astype(jnp.float32))
    return (result.astype(jnp.bfloat16), grads[0].astype(jnp.bfloat16), grads[1], grads[2], grads[3], grads[4], grads[5], grads[6], grads[7], grads[8], grads[9], grads[10], grads[11])
```

```python
from functools import partial

import jax
import jax.numpy as jnp
from jax import lax
from jax.sharding import PartitionSpec as P

from jax.experimental import pallas as pl
from jax.experimental.pallas import tpu as pltpu

HEADS = 16
MESH = pl.DeviceIdType.MESH
DEPTH = 2


norm_eps = 1e-06


def normalize(values):
    center = jnp.mean(values, axis=-1, keepdims=True)
    shifted = values - center
    inv_std = lax.rsqrt(jnp.mean(shifted * shifted, axis=-1, keepdims=True) + norm_eps)
    return (shifted * inv_std, inv_std)


def normalize_reverse(normed, inv_std, grad_normed):
    mean_grad = jnp.mean(grad_normed, axis=-1, keepdims=True)
    mean_proj = jnp.mean(grad_normed * normed, axis=-1, keepdims=True)
    return inv_std * (grad_normed - mean_grad - normed * mean_proj)


def matmul_rows(left, right):
    return jnp.dot(left, right, preferred_element_type=jnp.float32)


def matmul_back(left, right):
    return lax.dot_general(
        left, right, (((1,), (1,)), ((), ())), preferred_element_type=jnp.float32
    )


def matmul_outer(left, right):
    return lax.dot_general(
        left, right, (((0,), (0,)), ((), ())), preferred_element_type=jnp.float32
    )


def block_term(factors, count, first, width):
    pieces = []
    for left, right, base in factors:
        lower = max(first, base)
        upper = min(first + width, base + right.shape[1])
        if lower < upper:
            rows_part = lax.slice_in_dim(left, 0, count, axis=1)
            pieces.append(matmul_outer(rows_part, right[:, lower - base : upper - base]))
    return jnp.concatenate(pieces, axis=1)

LANES = 384
PER_HALF = 18


def reduce_kernel(
    at_ref, b_ref, out_ref,
    bbuf, gbuf, sbuf, tbuf, ubuf, fbuf, core_in, one_in, two_in, z_in, far_in,
    bsem, core_sem, one_sem, two_sem, zs_sem, zr_sem, far_sem,
):
    narrow = lax.axis_index("narrow")
    wide = lax.axis_index("wide")
    core = wide % 2
    row = (wide // 2) % 2
    deep = wide // 4
    core_peer = (narrow, wide + 1 - 2 * core)
    x_peer = (1 - narrow, wide)
    y_peer = (narrow, wide + 2 - 4 * row)
    z_to = [(narrow, (deep + o) % 4 * 4 + wide % 4) for o in (1, 2, 3)]

    barrier = pltpu.get_barrier_semaphore()
    for peer in [core_peer, x_peer, y_peer] + z_to:
        pl.semaphore_signal(barrier, inc=1, device_id=peer, device_id_type=MESH)
    pl.semaphore_wait(barrier, 6)

    def fetch(chunk, half):
        number = chunk + half * PER_HALF
        column = number - 3 * ((number - 24) // 3) * (number // 24)
        column = pl.multiple_of(column * LANES, LANES)
        return pltpu.make_async_copy(
            b_ref.at[:, pl.ds(column, LANES)], bbuf.at[half], bsem.at[half]
        )

    def send(src, dst, sems, chunk, peer):
        return pltpu.make_async_remote_copy(
            src_ref=src, dst_ref=dst, send_sem=sems.at[0, chunk], recv_sem=sems.at[1, chunk],
            device_id=peer, device_id_type=MESH,
        )

    def core_copy(chunk):
        return send(gbuf.at[1 - core], core_in.at[chunk], core_sem, chunk, core_peer)

    def one_copy(chunk, even):
        slot = chunk % DEPTH
        if even:
            return send(sbuf.at[slot, 1 - narrow], one_in.at[chunk], one_sem, chunk, x_peer)
        return send(sbuf.at[slot, 1 - row], one_in.at[chunk], one_sem, chunk, y_peer)

    def two_copy(chunk, even):
        slot = chunk % DEPTH
        if even:
            return send(tbuf.at[slot, 1 - row], two_in.at[chunk], two_sem, chunk, y_peer)
        return send(tbuf.at[slot, 1 - narrow], two_in.at[chunk], two_sem, chunk, x_peer)

    def z_copies(chunk):
        slot = chunk % DEPTH
        return [
            pltpu.make_async_remote_copy(
                src_ref=ubuf.at[slot, (deep + o) % 4], dst_ref=z_in.at[chunk, o - 1],
                send_sem=zs_sem.at[chunk, o - 1], recv_sem=zr_sem.at[chunk, o - 1],
                device_id=z_to[o - 1], device_id_type=MESH,
            )
            for o in (1, 2, 3)
        ]

    def far_copy(chunk):
        return send(fbuf.at[chunk], far_in.at[chunk], far_sem, chunk, x_peer)

    def add(left, right):
        return left.astype(jnp.float32) + right.astype(jnp.float32)

    def make(chunk):
        for half in range(2):
            number = chunk + half * PER_HALF
            which = (
                jnp.where(number >= 9, 1, 0) + jnp.where(number >= 12, 1, 0)
                + jnp.where(number >= 24, 1, 0) + jnp.where(number >= 27, 1, 0)
                + jnp.where(number >= 30, 1, 0) + jnp.where(number >= 33, 1, 0)
            )
            fetch(chunk, half).wait()
            for side in range(2):
                product = jnp.dot(
                    at_ref[which, side], bbuf[half], preferred_element_type=jnp.float32
                )
                for unit in range(8):
                    gbuf[side, half, unit] = product[unit * 72 : unit * 72 + 72].astype(jnp.bfloat16)

            @pl.when(chunk + 1 < PER_HALF)
            def _():
                fetch(chunk + 1, half).start()

        core_copy(chunk).start()

    def pair(chunk, even):
        core_copy(chunk).wait()
        slot = chunk % DEPTH

        def body(step, carry):
            half, unit = step // 8, step % 8
            value = add(gbuf[core, half, unit], core_in[chunk, half, unit]).astype(jnp.bfloat16)
            deep_at, row_at = unit // 2, unit % 2
            if even:
                sbuf[slot, half, row_at, deep_at] = value
            else:
                sbuf[slot, row_at, half, deep_at] = value
            return carry

        lax.fori_loop(0, 16, body, 0)
        one_copy(chunk, even).start()

    def first(chunk, even):
        one_copy(chunk, even).wait()
        slot = chunk % DEPTH
        mine = narrow if even else row

        def body(step, carry):
            outer, inner = step // 4, step % 4
            tbuf[slot, outer, inner] = add(
                sbuf[slot, mine, outer, inner], one_in[chunk, outer, inner]
            ).astype(jnp.bfloat16)
            return carry

        lax.fori_loop(0, 8, body, 0)
        two_copy(chunk, even).start()

    def second(chunk, even):
        two_copy(chunk, even).wait()
        slot = chunk % DEPTH
        mine = row if even else narrow

        def body(step, carry):
            ubuf[slot, step] = add(tbuf[slot, mine, step], two_in[chunk, step]).astype(jnp.bfloat16)
            return carry

        lax.fori_loop(0, 4, body, 0)
        for copy in z_copies(chunk):
            copy.start()

    def third(chunk):
        for copy in z_copies(chunk):
            copy.wait()
        total = add(ubuf[chunk % DEPTH, deep], z_in[chunk, 0])
        total = total + add(z_in[chunk, 1], z_in[chunk, 2])
        out_ref[narrow * PER_HALF + chunk] = total
        fbuf[chunk] = total.astype(jnp.bfloat16)
        far_copy(chunk).start()

    for half in range(2):
        fetch(0, half).start()

    def turn(step, carry):
        for parity in range(2):
            now = step * 2 + parity
            for lag, action, fixed in (
                (1 + 3 * DEPTH, third, False),
                (1 + 2 * DEPTH, second, True),
                (1 + DEPTH, first, True),
                (1, pair, True),
                (0, make, False),
            ):
                chunk = now - lag
                even = (parity - lag) % 2 == 0

                @pl.when(jnp.logical_and(chunk >= 0, chunk < PER_HALF))
                def _(action=action, fixed=fixed, chunk=chunk, even=even):
                    action(chunk, even) if fixed else action(chunk)

        return carry

    lax.fori_loop(0, (PER_HALF + 3 * DEPTH + 2) // 2, turn, 0)

    def finish(chunk, carry):
        far_copy(chunk).wait()
        out_ref[(1 - narrow) * PER_HALF + chunk] = far_in[chunk].astype(jnp.float32)
        return carry

    lax.fori_loop(0, PER_HALF, finish, 0)


def reduce_weights(transposed, right):
    bf = jnp.bfloat16
    dma = pltpu.SemaphoreType.DMA
    unit = (72, LANES)
    n = PER_HALF
    return pl.pallas_call(
        reduce_kernel,
        out_shape=jax.ShapeDtypeStruct((2 * n,) + unit, jnp.float32),
        in_specs=[
            pl.BlockSpec(memory_space=pltpu.VMEM),
            pl.BlockSpec(memory_space=pl.ANY),
        ],
        out_specs=pl.BlockSpec(memory_space=pltpu.VMEM),
        scratch_shapes=[
            pltpu.VMEM((2, 512, LANES), bf),
            pltpu.VMEM((2, 2, 8) + unit, bf),
            pltpu.VMEM((DEPTH, 2, 2, 4) + unit, bf),
            pltpu.VMEM((DEPTH, 2, 4) + unit, bf),
            pltpu.VMEM((DEPTH, 4) + unit, bf),
            pltpu.VMEM((n,) + unit, bf),
            pltpu.VMEM((n, 2, 8) + unit, bf),
            pltpu.VMEM((n, 2, 4) + unit, bf),
            pltpu.VMEM((n, 4) + unit, bf),
            pltpu.VMEM((n, 3) + unit, bf),
            pltpu.VMEM((n,) + unit, bf),
            dma((2,)),
            dma((2, n)),
            dma((2, n)),
            dma((2, n)),
            dma((n, 3)),
            dma((n, 3)),
            dma((2, n)),
        ],
        compiler_params=pltpu.CompilerParams(
            collective_id=1, has_side_effects=True, vmem_limit_bytes=66_000_000
        ),
        name="reduce_weights",
    )(transposed, right)


def by_holder(left, parts):
    tokens = left.shape[0]
    rows = left.T.reshape(8, 2, parts, 72, tokens)
    return rows.transpose(2, 1, 0, 3, 4).reshape(parts, 2, 576, tokens)


def weight_grads(first_input, attended, second_in, activated, grad_projected, grad_branch, grad_hidden, grad_mlp):
    transposed = jnp.concatenate(
        [by_holder(first_input, 1), by_holder(attended, 1), by_holder(second_in, 1), by_holder(activated, 4)]
    )
    right = jnp.concatenate([grad_projected, grad_branch, grad_hidden, grad_mlp], axis=1)
    done = reduce_weights(transposed, right)

    def flat(lower, upper):
        return done[lower:upper].transpose(1, 0, 2).reshape(72, (upper - lower) * LANES)

    down = done[24:].reshape(4, 3, 72, LANES).transpose(0, 2, 1, 3).reshape(288, 3 * LANES)
    return flat(0, 9), flat(9, 12), flat(12, 24), down


def per_device(
    patches,
    condition,
    image_counts,
    ada_weight,
    ada_bias,
    inproj_weight,
    inproj_bias,
    outproj_weight,
    outproj_bias,
    up_weight,
    up_bias,
    down_weight,
    down_bias,
    cotangent,
):
    slots, seq_len, model_width = patches.shape
    head_dim = model_width // HEADS
    scale_qk = head_dim ** (-0.5)
    row_total = slots * seq_len
    wide_count = lax.axis_size("wide")
    live = (jnp.arange(slots) < image_counts[0]).astype(jnp.float32)[:, None, None]
    cond_act = jax.nn.silu(condition).astype(jnp.bfloat16)
    cond_all = lax.all_gather(cond_act, "wide", axis=0, tiled=True)
    mod_part = (matmul_rows(cond_all, ada_weight) + ada_bias.astype(jnp.float32)).astype(
        jnp.bfloat16
    )
    modulation = lax.all_to_all(mod_part, "wide", split_axis=0, concat_axis=1, tiled=True).astype(
        jnp.float32
    )
    segment_list = [
        modulation[:, None, number * model_width : (number + 1) * model_width]
        for number in range(6)
    ]
    (
        selfattn_offset,
        selfattn_scale,
        selfattn_gate,
        perceptron_offset,
        perceptron_scale,
        perceptron_gate,
    ) = segment_list
    fetched = (
        lax.all_gather(inproj_weight, "wide", axis=0, tiled=True),
        lax.all_gather(inproj_bias, "wide", axis=0, tiled=True),
        lax.all_gather(outproj_weight, "wide", axis=0, tiled=True),
        lax.all_gather(outproj_bias, "wide", axis=0, tiled=True),
        lax.all_gather(up_weight, "wide", axis=0, tiled=True),
        lax.all_gather(up_bias, "wide", axis=0, tiled=True),
        lax.all_gather(down_weight, "wide", axis=0, tiled=True),
        lax.all_gather(down_bias, "wide", axis=0, tiled=True),
    )
    w_inproj, b_inproj, w_outproj, b_outproj, w_up, b_up, w_down, b_down = fetched
    input_rows = patches.astype(jnp.float32)
    normalized_first, inverse_deviation = normalize(input_rows)
    first_input = (
        (normalized_first * (1.0 + selfattn_scale) + selfattn_offset)
        .astype(jnp.bfloat16)
        .reshape(row_total, model_width)
    )
    proj_bias = b_inproj.astype(jnp.float32)
    full_bias = jnp.concatenate(
        [proj_bias[:model_width], jnp.zeros((model_width,), jnp.float32), proj_bias[model_width:]]
    )
    projected = (matmul_rows(first_input, w_inproj) + full_bias).astype(jnp.bfloat16)
    query_rows = projected[:, :model_width].reshape(slots, seq_len, HEADS, head_dim)
    key_rows = projected[:, model_width : 2 * model_width].reshape(slots, seq_len, HEADS, head_dim)
    value_rows = projected[:, 2 * model_width :].reshape(slots, seq_len, HEADS, head_dim)
    scores = (
        jnp.einsum("sqhe,skhe->shqk", query_rows, key_rows, preferred_element_type=jnp.float32)
        * scale_qk
    )
    log_total = jax.nn.logsumexp(scores, axis=-1, keepdims=True)
    probs = jnp.exp(scores - log_total).astype(jnp.bfloat16)
    attended = jnp.einsum("shqk,skhe->sqhe", probs, value_rows, preferred_element_type=jnp.float32)
    attended = attended.astype(jnp.bfloat16).reshape(row_total, model_width)
    residual_branch = (matmul_rows(attended, w_outproj) + b_outproj.astype(jnp.float32)).reshape(
        slots, seq_len, model_width
    )
    between_state = input_rows + selfattn_gate * residual_branch
    normed_b, inv_b = normalize(between_state)
    second_in = (
        (normed_b * (1.0 + perceptron_scale) + perceptron_offset)
        .astype(jnp.bfloat16)
        .reshape(row_total, model_width)
    )
    hidden = matmul_rows(second_in, w_up) + b_up.astype(jnp.float32)
    gelu_value, gelu_pull = jax.vjp(partial(jax.nn.gelu, approximate=True), hidden)
    activated = gelu_value.astype(jnp.bfloat16)
    mlp_out = (matmul_rows(activated, w_down) + b_down.astype(jnp.float32)).reshape(
        slots, seq_len, model_width
    )
    output = ((between_state + perceptron_gate * mlp_out) * live).astype(jnp.bfloat16)
    back_weights = (
        lax.all_gather(inproj_weight, "wide", axis=0, tiled=True),
        lax.all_gather(inproj_bias, "wide", axis=0, tiled=True),
        lax.all_gather(outproj_weight, "wide", axis=0, tiled=True),
        lax.all_gather(outproj_bias, "wide", axis=0, tiled=True),
        lax.all_gather(up_weight, "wide", axis=0, tiled=True),
        lax.all_gather(up_bias, "wide", axis=0, tiled=True),
        lax.all_gather(down_weight, "wide", axis=0, tiled=True),
        lax.all_gather(down_bias, "wide", axis=0, tiled=True),
    )
    wb_inproj, _, wb_outproj, _, wb_up, _, wb_down, _ = back_weights
    grad_out = cotangent.astype(jnp.float32) * live
    grad_gate_mlp = jnp.sum(grad_out * mlp_out, axis=1)
    grad_mlp = (grad_out * perceptron_gate).astype(jnp.bfloat16).reshape(row_total, model_width)
    grad_down_bias = jnp.sum(grad_mlp.astype(jnp.float32), axis=0)
    grad_act = matmul_back(grad_mlp, wb_down)
    grad_hidden = gelu_pull(grad_act)[0].astype(jnp.bfloat16)
    grad_up_bias = jnp.sum(grad_hidden.astype(jnp.float32), axis=0)
    grad_second = matmul_back(grad_hidden, wb_up).reshape(slots, seq_len, model_width)
    grad_scale_mlp = jnp.sum(grad_second * normed_b, axis=1)
    grad_shift_mlp = jnp.sum(grad_second, axis=1)
    between_gradient = grad_out + normalize_reverse(
        normed_b, inv_b, grad_second * (1.0 + perceptron_scale)
    )
    selfattn_gate_gradient = jnp.sum(between_gradient * residual_branch, axis=1)
    residual_branch_gradient = (
        (between_gradient * selfattn_gate).astype(jnp.bfloat16).reshape(row_total, model_width)
    )
    grad_outproj_bias = jnp.sum(residual_branch_gradient.astype(jnp.float32), axis=0)
    grad_attended = (
        matmul_back(residual_branch_gradient, wb_outproj)
        .astype(jnp.bfloat16)
        .reshape(slots, seq_len, HEADS, head_dim)
    )
    scores_again = (
        jnp.einsum("sqhe,skhe->shqk", query_rows, key_rows, preferred_element_type=jnp.float32)
        * scale_qk
    )
    probs_full = jnp.exp(scores_again - log_total)
    grad_values = jnp.einsum(
        "shqk,sqhe->skhe",
        probs_full.astype(jnp.bfloat16),
        grad_attended,
        preferred_element_type=jnp.float32,
    )
    grad_probs = jnp.einsum(
        "sqhe,skhe->shqk", grad_attended, value_rows, preferred_element_type=jnp.float32
    )
    row_dot = jnp.sum(grad_probs * probs_full, axis=-1, keepdims=True)
    grad_scores = (probs_full * (grad_probs - row_dot)).astype(jnp.bfloat16)
    grad_queries = (
        jnp.einsum("shqk,skhe->sqhe", grad_scores, key_rows, preferred_element_type=jnp.float32)
        * scale_qk
    )
    grad_keys = (
        jnp.einsum("shqk,sqhe->skhe", grad_scores, query_rows, preferred_element_type=jnp.float32)
        * scale_qk
    )
    grad_projected = jnp.concatenate(
        [
            grad_queries.reshape(row_total, model_width),
            grad_keys.reshape(row_total, model_width),
            grad_values.reshape(row_total, model_width),
        ],
        axis=1,
    ).astype(jnp.bfloat16)
    proj_sums = jnp.sum(grad_projected.astype(jnp.float32), axis=0)
    grad_inproj_bias = jnp.concatenate([proj_sums[:model_width], proj_sums[2 * model_width :]])
    first_gradient = matmul_back(grad_projected, wb_inproj).reshape(slots, seq_len, model_width)
    selfattn_scale_gradient = jnp.sum(first_gradient * normalized_first, axis=1)
    selfattn_offset_gradient = jnp.sum(first_gradient, axis=1)
    grad_patches = (
        between_gradient
        + normalize_reverse(
            normalized_first, inverse_deviation, first_gradient * (1.0 + selfattn_scale)
        )
    ).astype(jnp.bfloat16)
    grad_modulation = jnp.concatenate(
        [
            selfattn_offset_gradient,
            selfattn_scale_gradient,
            selfattn_gate_gradient,
            grad_shift_mlp,
            grad_scale_mlp,
            grad_gate_mlp,
        ],
        axis=1,
    ).astype(jnp.bfloat16)
    grad_mod_part = lax.all_to_all(grad_modulation, "wide", split_axis=1, concat_axis=0, tiled=True)
    grad_ada_weight = matmul_outer(cond_all, grad_mod_part)
    grad_ada_bias = jnp.sum(grad_mod_part.astype(jnp.float32), axis=0)
    grad_cond_part = matmul_back(grad_mod_part, ada_weight)
    grad_cond_act = lax.psum_scatter(
        grad_cond_part.astype(jnp.bfloat16), "wide", scatter_dimension=0, tiled=True
    ).astype(jnp.float32)
    _, silu_pull = jax.vjp(jax.nn.silu, condition)
    grad_condition = silu_pull(grad_cond_act)[0]
    bias_shares = (
        lax.psum_scatter(
            grad_inproj_bias.astype(jnp.bfloat16), "wide", scatter_dimension=0, tiled=True
        ).astype(jnp.float32),
        lax.psum_scatter(
            grad_outproj_bias.astype(jnp.bfloat16), "wide", scatter_dimension=0, tiled=True
        ).astype(jnp.float32),
        lax.psum_scatter(
            grad_up_bias.astype(jnp.bfloat16), "wide", scatter_dimension=0, tiled=True
        ).astype(jnp.float32),
        lax.psum_scatter(
            grad_down_bias.astype(jnp.bfloat16), "wide", scatter_dimension=0, tiled=True
        ).astype(jnp.float32),
    )
    ff_width = activated.shape[1]
    input_factors = (
        (first_input, grad_projected, 0),
        (attended, residual_branch_gradient, 3 * model_width),
        (second_in, grad_hidden, 4 * model_width),
    )
    down_factors = ((activated, grad_mlp, 0),)
    input_block = (4 * model_width + ff_width) // 4
    down_block = model_width // 2
    block_jobs = [
        (input_factors, model_width, number * input_block, input_block) for number in range(4)
    ]
    block_jobs = block_jobs + [
        (down_factors, ff_width, number * down_block, down_block) for number in range(2)
    ]

    def reduce_block(factors, rows, first, width):
        return lax.psum_scatter(
            block_term(factors, lax.axis_size("wide") * (rows // wide_count), first, width).astype(
                jnp.bfloat16
            ),
            "wide",
            scatter_dimension=0,
            tiled=True,
        ).astype(jnp.float32)

    if lax.axis_size("narrow") == 2 and wide_count == 16:
        w_grads = weight_grads(
            first_input, attended, second_in, activated,
            grad_projected, residual_branch_gradient, grad_hidden, grad_mlp,
        )
    else:
        shards = [reduce_block(*job) for job in block_jobs]
        input_grads = jnp.concatenate(shards[:4], axis=1)
        w_grads = tuple(
            lax.psum(part.astype(jnp.bfloat16), "narrow").astype(jnp.float32)
            for part in (
                input_grads[:, : 3 * model_width],
                input_grads[:, 3 * model_width : 4 * model_width],
                input_grads[:, 4 * model_width :],
                jnp.concatenate(shards[4:], axis=1),
            )
        )
    small = [
        lax.psum(part.astype(jnp.bfloat16), "narrow").astype(jnp.float32)
        for part in (grad_ada_weight, grad_ada_bias) + bias_shares
    ]
    return (
        output,
        grad_patches,
        grad_condition,
        small[0],
        small[1],
        w_grads[0],
        small[2],
        w_grads[1],
        small[3],
        w_grads[2],
        small[4],
        w_grads[3],
        small[5],
    )


def solution(mesh):
    in_specs = (
        P(("narrow", "wide"), None, None),
        P(("narrow", "wide"), None),
        P(("narrow", "wide")),
        P(None, "wide"),
        P("wide"),
        P("wide", None),
        P("wide"),
        P("wide", None),
        P("wide"),
        P("wide", None),
        P("wide"),
        P("wide", None),
        P("wide"),
        P(("narrow", "wide"), None, None),
    )
    out_specs = (
        P(("narrow", "wide"), None, None),
        P(("narrow", "wide"), None, None),
        P(("narrow", "wide"), None),
        P(None, "wide"),
        P("wide"),
        P("wide", None),
        P("wide"),
        P("wide", None),
        P("wide"),
        P("wide", None),
        P("wide"),
        P("wide", None),
        P("wide"),
    )
    return jax.shard_map(
        per_device, mesh=mesh, in_specs=in_specs, out_specs=out_specs, check_vma=False
    )
```

```python
from functools import partial

import jax
import jax.numpy as jnp
from jax import lax
from jax.sharding import PartitionSpec as P

from jax.experimental import pallas as pl
from jax.experimental.pallas import tpu as pltpu

HEADS = 16
MESH = pl.DeviceIdType.MESH
DEPTH = 2


norm_eps = 1e-06


def normalize(values):
    center = jnp.mean(values, axis=-1, keepdims=True)
    shifted = values - center
    inv_std = lax.rsqrt(jnp.mean(shifted * shifted, axis=-1, keepdims=True) + norm_eps)
    return (shifted * inv_std, inv_std)


def normalize_reverse(normed, inv_std, grad_normed):
    mean_grad = jnp.mean(grad_normed, axis=-1, keepdims=True)
    mean_proj = jnp.mean(grad_normed * normed, axis=-1, keepdims=True)
    return inv_std * (grad_normed - mean_grad - normed * mean_proj)


def matmul_rows(left, right):
    return jnp.dot(left, right, preferred_element_type=jnp.float32)


def matmul_back(left, right):
    return lax.dot_general(
        left, right, (((1,), (1,)), ((), ())), preferred_element_type=jnp.float32
    )


def matmul_outer(left, right):
    return lax.dot_general(
        left, right, (((0,), (0,)), ((), ())), preferred_element_type=jnp.float32
    )


def block_term(factors, count, first, width):
    pieces = []
    for left, right, base in factors:
        lower = max(first, base)
        upper = min(first + width, base + right.shape[1])
        if lower < upper:
            rows_part = lax.slice_in_dim(left, 0, count, axis=1)
            pieces.append(matmul_outer(rows_part, right[:, lower - base : upper - base]))
    return jnp.concatenate(pieces, axis=1)

LANES = 384
PER_HALF = 18


def reduce_kernel(
    at_ref, b_ref, out_ref,
    bbuf, gbuf, sbuf, tbuf, ubuf, fbuf, core_in, one_in, two_in, z_in, far_in,
    bsem, core_sem, one_sem, two_sem, zs_sem, zr_sem, far_sem,
):
    narrow = lax.axis_index("narrow")
    wide = lax.axis_index("wide")
    core = wide % 2
    row = (wide // 2) % 2
    deep = wide // 4
    core_peer = (narrow, wide + 1 - 2 * core)
    x_peer = (1 - narrow, wide)
    y_peer = (narrow, wide + 2 - 4 * row)
    z_to = [(narrow, (deep + o) % 4 * 4 + wide % 4) for o in (1, 2, 3)]

    barrier = pltpu.get_barrier_semaphore()
    for peer in [core_peer, x_peer, y_peer] + z_to:
        pl.semaphore_signal(barrier, inc=1, device_id=peer, device_id_type=MESH)
    pl.semaphore_wait(barrier, 6)

    def fetch(chunk, half):
        number = chunk + half * PER_HALF
        column = number - 3 * ((number - 24) // 3) * (number // 24)
        column = pl.multiple_of(column * LANES, LANES)
        return pltpu.make_async_copy(
            b_ref.at[:, pl.ds(column, LANES)], bbuf.at[half], bsem.at[half]
        )

    def send(src, dst, sems, chunk, peer):
        return pltpu.make_async_remote_copy(
            src_ref=src, dst_ref=dst, send_sem=sems.at[0, chunk], recv_sem=sems.at[1, chunk],
            device_id=peer, device_id_type=MESH,
        )

    def core_copy(chunk):
        return send(gbuf.at[1 - core], core_in.at[chunk], core_sem, chunk, core_peer)

    def one_copy(chunk, even):
        slot = chunk % DEPTH
        if even:
            return send(sbuf.at[slot, 1 - narrow], one_in.at[chunk], one_sem, chunk, x_peer)
        return send(sbuf.at[slot, 1 - row], one_in.at[chunk], one_sem, chunk, y_peer)

    def two_copy(chunk, even):
        slot = chunk % DEPTH
        if even:
            return send(tbuf.at[slot, 1 - row], two_in.at[chunk], two_sem, chunk, y_peer)
        return send(tbuf.at[slot, 1 - narrow], two_in.at[chunk], two_sem, chunk, x_peer)

    def z_copies(chunk):
        slot = chunk % DEPTH
        return [
            pltpu.make_async_remote_copy(
                src_ref=ubuf.at[slot, (deep + o) % 4], dst_ref=z_in.at[chunk, o - 1],
                send_sem=zs_sem.at[chunk, o - 1], recv_sem=zr_sem.at[chunk, o - 1],
                device_id=z_to[o - 1], device_id_type=MESH,
            )
            for o in (1, 2, 3)
        ]

    def far_copy(chunk):
        return send(fbuf.at[chunk], far_in.at[chunk], far_sem, chunk, x_peer)

    def add(left, right):
        return left.astype(jnp.float32) + right.astype(jnp.float32)

    def make(chunk):
        for half in range(2):
            number = chunk + half * PER_HALF
            which = (
                jnp.where(number >= 9, 1, 0) + jnp.where(number >= 12, 1, 0)
                + jnp.where(number >= 24, 1, 0) + jnp.where(number >= 27, 1, 0)
                + jnp.where(number >= 30, 1, 0) + jnp.where(number >= 33, 1, 0)
            )
            fetch(chunk, half).wait()
            for side in range(2):
                product = jnp.dot(
                    at_ref[which, side], bbuf[half], preferred_element_type=jnp.float32
                )
                for unit in range(8):
                    gbuf[side, half, unit] = product[unit * 72 : unit * 72 + 72].astype(jnp.bfloat16)

            @pl.when(chunk + 1 < PER_HALF)
            def _():
                fetch(chunk + 1, half).start()

        core_copy(chunk).start()

    def pair(chunk, even):
        core_copy(chunk).wait()
        slot = chunk % DEPTH

        def body(step, carry):
            half, unit = step // 8, step % 8
            value = add(gbuf[core, half, unit], core_in[chunk, half, unit]).astype(jnp.bfloat16)
            deep_at, row_at = unit // 2, unit % 2
            if even:
                sbuf[slot, half, row_at, deep_at] = value
            else:
                sbuf[slot, row_at, half, deep_at] = value
            return carry

        lax.fori_loop(0, 16, body, 0)
        one_copy(chunk, even).start()

    def first(chunk, even):
        one_copy(chunk, even).wait()
        slot = chunk % DEPTH
        mine = narrow if even else row

        def body(step, carry):
            outer, inner = step // 4, step % 4
            tbuf[slot, outer, inner] = add(
                sbuf[slot, mine, outer, inner], one_in[chunk, outer, inner]
            ).astype(jnp.bfloat16)
            return carry

        lax.fori_loop(0, 8, body, 0)
        two_copy(chunk, even).start()

    def second(chunk, even):
        two_copy(chunk, even).wait()
        slot = chunk % DEPTH
        mine = row if even else narrow

        def body(step, carry):
            ubuf[slot, step] = add(tbuf[slot, mine, step], two_in[chunk, step]).astype(jnp.bfloat16)
            return carry

        lax.fori_loop(0, 4, body, 0)
        for copy in z_copies(chunk):
            copy.start()

    def third(chunk):
        for copy in z_copies(chunk):
            copy.wait()
        total = add(ubuf[chunk % DEPTH, deep], z_in[chunk, 0])
        total = total + add(z_in[chunk, 1], z_in[chunk, 2])
        out_ref[narrow * PER_HALF + chunk] = total
        fbuf[chunk] = total.astype(jnp.bfloat16)
        far_copy(chunk).start()

    for half in range(2):
        fetch(0, half).start()

    def turn(step, carry):
        for parity in range(2):
            now = step * 2 + parity
            for lag, action, fixed in (
                (1 + 3 * DEPTH, third, False),
                (1 + 2 * DEPTH, second, True),
                (1 + DEPTH, first, True),
                (1, pair, True),
                (0, make, False),
            ):
                chunk = now - lag
                even = (parity - lag) % 2 == 0

                @pl.when(jnp.logical_and(chunk >= 0, chunk < PER_HALF))
                def _(action=action, fixed=fixed, chunk=chunk, even=even):
                    action(chunk, even) if fixed else action(chunk)

        return carry

    lax.fori_loop(0, (PER_HALF + 3 * DEPTH + 2) // 2, turn, 0)

    def finish(chunk, carry):
        far_copy(chunk).wait()
        out_ref[(1 - narrow) * PER_HALF + chunk] = far_in[chunk].astype(jnp.float32)
        return carry

    lax.fori_loop(0, PER_HALF, finish, 0)


def reduce_weights(transposed, right):
    bf = jnp.bfloat16
    dma = pltpu.SemaphoreType.DMA
    unit = (72, LANES)
    n = PER_HALF
    return pl.pallas_call(
        reduce_kernel,
        out_shape=jax.ShapeDtypeStruct((2 * n,) + unit, jnp.float32),
        in_specs=[
            pl.BlockSpec(memory_space=pltpu.VMEM),
            pl.BlockSpec(memory_space=pl.ANY),
        ],
        out_specs=pl.BlockSpec(memory_space=pltpu.VMEM),
        scratch_shapes=[
            pltpu.VMEM((2, 512, LANES), bf),
            pltpu.VMEM((2, 2, 8) + unit, bf),
            pltpu.VMEM((DEPTH, 2, 2, 4) + unit, bf),
            pltpu.VMEM((DEPTH, 2, 4) + unit, bf),
            pltpu.VMEM((DEPTH, 4) + unit, bf),
            pltpu.VMEM((n,) + unit, bf),
            pltpu.VMEM((n, 2, 8) + unit, bf),
            pltpu.VMEM((n, 2, 4) + unit, bf),
            pltpu.VMEM((n, 4) + unit, bf),
            pltpu.VMEM((n, 3) + unit, bf),
            pltpu.VMEM((n,) + unit, bf),
            dma((2,)),
            dma((2, n)),
            dma((2, n)),
            dma((2, n)),
            dma((n, 3)),
            dma((n, 3)),
            dma((2, n)),
        ],
        compiler_params=pltpu.CompilerParams(
            collective_id=1, has_side_effects=True, vmem_limit_bytes=66_000_000
        ),
        name="reduce_weights",
    )(transposed, right)


def by_holder(left, parts):
    tokens = left.shape[0]
    rows = left.T.reshape(8, 2, parts, 72, tokens)
    return rows.transpose(2, 1, 0, 3, 4).reshape(parts, 2, 576, tokens)


def weight_grads(first_input, attended, second_in, activated, grad_projected, grad_branch, grad_hidden, grad_mlp):
    transposed = jnp.concatenate(
        [by_holder(first_input, 1), by_holder(attended, 1), by_holder(second_in, 1), by_holder(activated, 4)]
    )
    right = jnp.concatenate([grad_projected, grad_branch, grad_hidden, grad_mlp], axis=1)
    done = reduce_weights(transposed, right)

    def flat(lower, upper):
        return done[lower:upper].transpose(1, 0, 2).reshape(72, (upper - lower) * LANES)

    down = done[24:].reshape(4, 3, 72, LANES).transpose(0, 2, 1, 3).reshape(288, 3 * LANES)
    return flat(0, 9), flat(9, 12), flat(12, 24), down


def place(index, wide_count):
    return (index // wide_count, index % wide_count)


def meet(total, me, wide_count):
    barrier = pltpu.get_barrier_semaphore()

    def greet(step, carry):
        pl.semaphore_signal(
            barrier, inc=1, device_id=place((me + step) % total, wide_count), device_id_type=MESH
        )
        return carry

    lax.fori_loop(1, total, greet, 0)
    pl.semaphore_wait(barrier, total - 1)


def exchange(step, source, landing, send_sems, recv_sems, peer):
    return pltpu.make_async_remote_copy(
        src_ref=source, dst_ref=landing, send_sem=send_sems.at[step], recv_sem=recv_sems.at[step],
        device_id=peer, device_id_type=MESH,
    )


def loop(count, action):
    def body(step, carry):
        action(step)
        return carry

    lax.fori_loop(1, count, body, 0)


def front_kernel(
    narrow_count, wide_count, pack_ref, weight_ref, bias_ref, all_ref, mod_ref,
    part, send_sem, recv_sem, send_two, recv_two,
):
    total = narrow_count * wide_count
    narrow, wide = lax.axis_index("narrow"), lax.axis_index("wide")
    me = narrow * wide_count + wide
    base = narrow * wide_count
    meet(total, me, wide_count)

    def spread(step):
        return exchange(
            step, pack_ref, all_ref.at[me], send_sem, recv_sem, place((me + step) % total, wide_count)
        )

    loop(total, lambda step: spread(step).start())
    all_ref[me] = pack_ref[...]
    loop(total, lambda step: spread(step).wait())
    rows = all_ref[pl.ds(base, wide_count)].astype(jnp.float32)
    rows = rows.reshape(wide_count * 8, rows.shape[2]).astype(jnp.bfloat16)
    product = jnp.dot(rows, weight_ref[...], preferred_element_type=jnp.float32)
    product = product + bias_ref[...].astype(jnp.float32)
    part[...] = product.reshape(part.shape).astype(jnp.bfloat16)

    def deal(step):
        to = (wide + step) % wide_count
        return exchange(step, part.at[to], mod_ref.at[wide], send_two, recv_two, (narrow, to))

    loop(wide_count, lambda step: deal(step).start())
    mod_ref[wide] = part[wide]
    loop(wide_count, lambda step: deal(step).wait())


def tail_kernel(
    narrow_count, wide_count, gift_ref, all_ref, weight_ref, ada_ref, misc_ref, cond_ref,
    gifts, part, shares, send_sem, recv_sem, send_two, recv_two,
):
    total = narrow_count * wide_count
    narrow, wide = lax.axis_index("narrow"), lax.axis_index("wide")
    me = narrow * wide_count + wide
    base = narrow * wide_count
    meet(total, me, wide_count)

    def spread(step):
        to = (me + step) % total
        return exchange(
            step, gift_ref.at[to % wide_count], gifts.at[me], send_sem, recv_sem, place(to, wide_count)
        )

    loop(total, lambda step: spread(step).start())
    gifts[me] = gift_ref[wide]
    loop(total, lambda step: spread(step).wait())
    mine = gifts[pl.ds(base, wide_count)].astype(jnp.float32)
    mine = mine.reshape(wide_count * 8, mine.shape[2]).astype(jnp.bfloat16)
    share = matmul_back(mine, weight_ref[...])
    part[...] = share.reshape(part.shape).astype(jnp.bfloat16)

    def deal(step):
        to = (wide + step) % wide_count
        return exchange(step, part.at[to], shares.at[wide], send_two, recv_two, (narrow, to))

    loop(wide_count, lambda step: deal(step).start())
    shares[wide] = part[wide]
    every = gifts[...].astype(jnp.float32)
    misc_ref[...] = jnp.sum(every, axis=0)
    grads = every.reshape(total * 8, every.shape[2]).astype(jnp.bfloat16)
    conds = all_ref[...].astype(jnp.float32)
    conds = conds.reshape(total * 8, conds.shape[2]).astype(jnp.bfloat16)
    ada_ref[...] = matmul_outer(conds, grads)
    loop(wide_count, lambda step: deal(step).wait())
    cond_ref[...] = jnp.sum(shares[...].astype(jnp.float32), axis=0)


def in_vmem(count):
    return [pl.BlockSpec(memory_space=pltpu.VMEM)] * count


def dmas(*counts):
    return [pltpu.SemaphoreType.DMA((count,)) for count in counts]


def front(cond_act, biases, ada_weight, ada_bias):
    narrow_count, wide_count = lax.axis_size("narrow"), lax.axis_size("wide")
    total = narrow_count * wide_count
    slots, model_width = cond_act.shape
    columns = ada_weight.shape[1]
    bias_row = jnp.concatenate(biases)
    bias_row = jnp.pad(bias_row, (0, model_width - bias_row.shape[0]))[None]
    pack = jnp.concatenate(
        [cond_act, bias_row, jnp.zeros((7 - slots, model_width), jnp.bfloat16)]
    )
    return pl.pallas_call(
        partial(front_kernel, narrow_count, wide_count),
        out_shape=(
            jax.ShapeDtypeStruct((total, 8, model_width), jnp.bfloat16),
            jax.ShapeDtypeStruct((wide_count, 8, columns), jnp.bfloat16),
        ),
        in_specs=in_vmem(3),
        out_specs=tuple(in_vmem(2)),
        scratch_shapes=[pltpu.VMEM((wide_count, 8, columns), jnp.bfloat16)]
        + dmas(total, total, wide_count, wide_count),
        compiler_params=pltpu.CompilerParams(collective_id=2, has_side_effects=True),
        name="front",
    )(pack, ada_weight, ada_bias[None])


def tail(grad_modulation, bias_grads, gathered, ada_weight):
    narrow_count, wide_count = lax.axis_size("narrow"), lax.axis_size("wide")
    total = narrow_count * wide_count
    slots = grad_modulation.shape[0]
    model_width, columns = ada_weight.shape
    blocks = grad_modulation.reshape(slots, wide_count, columns).transpose(1, 0, 2)
    held = jnp.concatenate(
        [grad.reshape(wide_count, -1) for grad in bias_grads], axis=1
    ).astype(jnp.bfloat16)
    lines = -(-held.shape[1] // columns)
    held_rows = jnp.pad(held, ((0, 0), (0, lines * columns - held.shape[1])))
    held_rows = held_rows.reshape(wide_count, lines, columns)
    gap = jnp.zeros((wide_count, 4 - slots, columns), jnp.bfloat16)
    end = jnp.zeros((wide_count, 4 - lines, columns), jnp.bfloat16)
    gift = jnp.concatenate([blocks, gap, held_rows, end], axis=1)
    ada, misc, cond = pl.pallas_call(
        partial(tail_kernel, narrow_count, wide_count),
        out_shape=(
            jax.ShapeDtypeStruct((model_width, columns), jnp.float32),
            jax.ShapeDtypeStruct((8, columns), jnp.float32),
            jax.ShapeDtypeStruct((8, model_width), jnp.float32),
        ),
        in_specs=in_vmem(3),
        out_specs=tuple(in_vmem(3)),
        scratch_shapes=[
            pltpu.VMEM((total, 8, columns), jnp.bfloat16),
            pltpu.VMEM((wide_count, 8, model_width), jnp.bfloat16),
            pltpu.VMEM((wide_count, 8, model_width), jnp.bfloat16),
        ]
        + dmas(total, total, wide_count, wide_count),
        compiler_params=pltpu.CompilerParams(collective_id=3, has_side_effects=True),
        name="tail",
    )(gift, gathered, ada_weight)
    flat = misc[4:].reshape(-1)
    grads, at = [], 0
    for grad in bias_grads:
        width = grad.shape[0] // wide_count
        grads.append(flat[at : at + width])
        at += width
    return ada, misc[:slots].sum(axis=0), cond[:slots], grads


def per_device(
    patches,
    condition,
    image_counts,
    ada_weight,
    ada_bias,
    inproj_weight,
    inproj_bias,
    outproj_weight,
    outproj_bias,
    up_weight,
    up_bias,
    down_weight,
    down_bias,
    cotangent,
):
    slots, seq_len, model_width = patches.shape
    head_dim = model_width // HEADS
    scale_qk = head_dim ** (-0.5)
    row_total = slots * seq_len
    wide_count = lax.axis_size("wide")
    live = (jnp.arange(slots) < image_counts[0]).astype(jnp.float32)[:, None, None]
    cond_act = jax.nn.silu(condition).astype(jnp.bfloat16)
    gathered, mod_blocks = front(
        cond_act, (inproj_bias, outproj_bias, up_bias, down_bias), ada_weight, ada_bias
    )
    modulation = (
        mod_blocks[:, :slots].transpose(1, 0, 2).reshape(slots, 6 * model_width).astype(jnp.float32)
    )
    group = lax.dynamic_slice_in_dim(
        gathered[:, slots], lax.axis_index("narrow") * wide_count, wide_count
    )
    all_biases, bias_at = [], 0
    for bias in (inproj_bias, outproj_bias, up_bias, down_bias):
        all_biases.append(group[:, bias_at : bias_at + bias.shape[0]].reshape(-1))
        bias_at += bias.shape[0]
    b_inproj, b_outproj, b_up, b_down = all_biases
    segment_list = [
        modulation[:, None, number * model_width : (number + 1) * model_width]
        for number in range(6)
    ]
    (
        selfattn_offset,
        selfattn_scale,
        selfattn_gate,
        perceptron_offset,
        perceptron_scale,
        perceptron_gate,
    ) = segment_list
    fetched = (
        lax.all_gather(inproj_weight, "wide", axis=0, tiled=True),
        lax.all_gather(outproj_weight, "wide", axis=0, tiled=True),
        lax.all_gather(up_weight, "wide", axis=0, tiled=True),
        lax.all_gather(down_weight, "wide", axis=0, tiled=True),
    )
    w_inproj, w_outproj, w_up, w_down = fetched
    input_rows = patches.astype(jnp.float32)
    normalized_first, inverse_deviation = normalize(input_rows)
    first_input = (
        (normalized_first * (1.0 + selfattn_scale) + selfattn_offset)
        .astype(jnp.bfloat16)
        .reshape(row_total, model_width)
    )
    proj_bias = b_inproj.astype(jnp.float32)
    full_bias = jnp.concatenate(
        [proj_bias[:model_width], jnp.zeros((model_width,), jnp.float32), proj_bias[model_width:]]
    )
    projected = (matmul_rows(first_input, w_inproj) + full_bias).astype(jnp.bfloat16)
    query_rows = projected[:, :model_width].reshape(slots, seq_len, HEADS, head_dim)
    key_rows = projected[:, model_width : 2 * model_width].reshape(slots, seq_len, HEADS, head_dim)
    value_rows = projected[:, 2 * model_width :].reshape(slots, seq_len, HEADS, head_dim)
    scores = (
        jnp.einsum("sqhe,skhe->shqk", query_rows, key_rows, preferred_element_type=jnp.float32)
        * scale_qk
    )
    log_total = jax.nn.logsumexp(scores, axis=-1, keepdims=True)
    probs = jnp.exp(scores - log_total).astype(jnp.bfloat16)
    attended = jnp.einsum("shqk,skhe->sqhe", probs, value_rows, preferred_element_type=jnp.float32)
    attended = attended.astype(jnp.bfloat16).reshape(row_total, model_width)
    residual_branch = (matmul_rows(attended, w_outproj) + b_outproj.astype(jnp.float32)).reshape(
        slots, seq_len, model_width
    )
    between_state = input_rows + selfattn_gate * residual_branch
    normed_b, inv_b = normalize(between_state)
    second_in = (
        (normed_b * (1.0 + perceptron_scale) + perceptron_offset)
        .astype(jnp.bfloat16)
        .reshape(row_total, model_width)
    )
    hidden = matmul_rows(second_in, w_up) + b_up.astype(jnp.float32)
    gelu_value, gelu_pull = jax.vjp(partial(jax.nn.gelu, approximate=True), hidden)
    activated = gelu_value.astype(jnp.bfloat16)
    mlp_out = (matmul_rows(activated, w_down) + b_down.astype(jnp.float32)).reshape(
        slots, seq_len, model_width
    )
    output = ((between_state + perceptron_gate * mlp_out) * live).astype(jnp.bfloat16)
    back_weights = (
        lax.all_gather(inproj_weight, "wide", axis=0, tiled=True),
        lax.all_gather(outproj_weight, "wide", axis=0, tiled=True),
        lax.all_gather(up_weight, "wide", axis=0, tiled=True),
        lax.all_gather(down_weight, "wide", axis=0, tiled=True),
    )
    wb_inproj, wb_outproj, wb_up, wb_down = back_weights
    grad_out = cotangent.astype(jnp.float32) * live
    grad_gate_mlp = jnp.sum(grad_out * mlp_out, axis=1)
    grad_mlp = (grad_out * perceptron_gate).astype(jnp.bfloat16).reshape(row_total, model_width)
    grad_down_bias = jnp.sum(grad_mlp.astype(jnp.float32), axis=0)
    grad_act = matmul_back(grad_mlp, wb_down)
    grad_hidden = gelu_pull(grad_act)[0].astype(jnp.bfloat16)
    grad_up_bias = jnp.sum(grad_hidden.astype(jnp.float32), axis=0)
    grad_second = matmul_back(grad_hidden, wb_up).reshape(slots, seq_len, model_width)
    grad_scale_mlp = jnp.sum(grad_second * normed_b, axis=1)
    grad_shift_mlp = jnp.sum(grad_second, axis=1)
    between_gradient = grad_out + normalize_reverse(
        normed_b, inv_b, grad_second * (1.0 + perceptron_scale)
    )
    selfattn_gate_gradient = jnp.sum(between_gradient * residual_branch, axis=1)
    residual_branch_gradient = (
        (between_gradient * selfattn_gate).astype(jnp.bfloat16).reshape(row_total, model_width)
    )
    grad_outproj_bias = jnp.sum(residual_branch_gradient.astype(jnp.float32), axis=0)
    grad_attended = (
        matmul_back(residual_branch_gradient, wb_outproj)
        .astype(jnp.bfloat16)
        .reshape(slots, seq_len, HEADS, head_dim)
    )
    scores_again = (
        jnp.einsum("sqhe,skhe->shqk", query_rows, key_rows, preferred_element_type=jnp.float32)
        * scale_qk
    )
    probs_full = jnp.exp(scores_again - log_total)
    grad_values = jnp.einsum(
        "shqk,sqhe->skhe",
        probs_full.astype(jnp.bfloat16),
        grad_attended,
        preferred_element_type=jnp.float32,
    )
    grad_probs = jnp.einsum(
        "sqhe,skhe->shqk", grad_attended, value_rows, preferred_element_type=jnp.float32
    )
    row_dot = jnp.sum(grad_probs * probs_full, axis=-1, keepdims=True)
    grad_scores = (probs_full * (grad_probs - row_dot)).astype(jnp.bfloat16)
    grad_queries = (
        jnp.einsum("shqk,skhe->sqhe", grad_scores, key_rows, preferred_element_type=jnp.float32)
        * scale_qk
    )
    grad_keys = (
        jnp.einsum("shqk,sqhe->skhe", grad_scores, query_rows, preferred_element_type=jnp.float32)
        * scale_qk
    )
    grad_projected = jnp.concatenate(
        [
            grad_queries.reshape(row_total, model_width),
            grad_keys.reshape(row_total, model_width),
            grad_values.reshape(row_total, model_width),
        ],
        axis=1,
    ).astype(jnp.bfloat16)
    proj_sums = jnp.sum(grad_projected.astype(jnp.float32), axis=0)
    grad_inproj_bias = jnp.concatenate([proj_sums[:model_width], proj_sums[2 * model_width :]])
    first_gradient = matmul_back(grad_projected, wb_inproj).reshape(slots, seq_len, model_width)
    selfattn_scale_gradient = jnp.sum(first_gradient * normalized_first, axis=1)
    selfattn_offset_gradient = jnp.sum(first_gradient, axis=1)
    grad_patches = (
        between_gradient
        + normalize_reverse(
            normalized_first, inverse_deviation, first_gradient * (1.0 + selfattn_scale)
        )
    ).astype(jnp.bfloat16)
    grad_modulation = jnp.concatenate(
        [
            selfattn_offset_gradient,
            selfattn_scale_gradient,
            selfattn_gate_gradient,
            grad_shift_mlp,
            grad_scale_mlp,
            grad_gate_mlp,
        ],
        axis=1,
    ).astype(jnp.bfloat16)
    grad_ada_weight, grad_ada_bias, grad_cond_act, bias_shares = tail(
        grad_modulation,
        (grad_inproj_bias, grad_outproj_bias, grad_up_bias, grad_down_bias),
        gathered,
        ada_weight,
    )
    _, silu_pull = jax.vjp(jax.nn.silu, condition)
    grad_condition = silu_pull(grad_cond_act)[0]
    ff_width = activated.shape[1]
    input_factors = (
        (first_input, grad_projected, 0),
        (attended, residual_branch_gradient, 3 * model_width),
        (second_in, grad_hidden, 4 * model_width),
    )
    down_factors = ((activated, grad_mlp, 0),)
    input_block = (4 * model_width + ff_width) // 4
    down_block = model_width // 2
    block_jobs = [
        (input_factors, model_width, number * input_block, input_block) for number in range(4)
    ]
    block_jobs = block_jobs + [
        (down_factors, ff_width, number * down_block, down_block) for number in range(2)
    ]

    def reduce_block(factors, rows, first, width):
        return lax.psum_scatter(
            block_term(factors, lax.axis_size("wide") * (rows // wide_count), first, width).astype(
                jnp.bfloat16
            ),
            "wide",
            scatter_dimension=0,
            tiled=True,
        ).astype(jnp.float32)

    if lax.axis_size("narrow") == 2 and wide_count == 16:
        w_grads = weight_grads(
            first_input, attended, second_in, activated,
            grad_projected, residual_branch_gradient, grad_hidden, grad_mlp,
        )
    else:
        shards = [reduce_block(*job) for job in block_jobs]
        input_grads = jnp.concatenate(shards[:4], axis=1)
        w_grads = tuple(
            lax.psum(part.astype(jnp.bfloat16), "narrow").astype(jnp.float32)
            for part in (
                input_grads[:, : 3 * model_width],
                input_grads[:, 3 * model_width : 4 * model_width],
                input_grads[:, 4 * model_width :],
                jnp.concatenate(shards[4:], axis=1),
            )
        )
    return (
        output,
        grad_patches,
        grad_condition,
        grad_ada_weight,
        grad_ada_bias,
        w_grads[0],
        bias_shares[0],
        w_grads[1],
        bias_shares[1],
        w_grads[2],
        bias_shares[2],
        w_grads[3],
        bias_shares[3],
    )


def solution(mesh):
    in_specs = (
        P(("narrow", "wide"), None, None),
        P(("narrow", "wide"), None),
        P(("narrow", "wide")),
        P(None, "wide"),
        P("wide"),
        P("wide", None),
        P("wide"),
        P("wide", None),
        P("wide"),
        P("wide", None),
        P("wide"),
        P("wide", None),
        P("wide"),
        P(("narrow", "wide"), None, None),
    )
    out_specs = (
        P(("narrow", "wide"), None, None),
        P(("narrow", "wide"), None, None),
        P(("narrow", "wide"), None),
        P(None, "wide"),
        P("wide"),
        P("wide", None),
        P("wide"),
        P("wide", None),
        P("wide"),
        P("wide", None),
        P("wide"),
        P("wide", None),
        P("wide"),
    )
    return jax.shard_map(
        per_device, mesh=mesh, in_specs=in_specs, out_specs=out_specs, check_vma=False
    )
```

```python
from functools import partial

import jax
import jax.numpy as jnp
from jax import lax
from jax.sharding import PartitionSpec as P

from jax.experimental import pallas as pl
from jax.experimental.pallas import tpu as pltpu

HEADS = 16
MESH = pl.DeviceIdType.MESH
DEPTH = 2


norm_eps = 1e-06


def normalize(values):
    center = jnp.mean(values, axis=-1, keepdims=True)
    shifted = values - center
    inv_std = lax.rsqrt(jnp.mean(shifted * shifted, axis=-1, keepdims=True) + norm_eps)
    return (shifted * inv_std, inv_std)


def normalize_reverse(normed, inv_std, grad_normed):
    mean_grad = jnp.mean(grad_normed, axis=-1, keepdims=True)
    mean_proj = jnp.mean(grad_normed * normed, axis=-1, keepdims=True)
    return inv_std * (grad_normed - mean_grad - normed * mean_proj)


def matmul_rows(left, right):
    return jnp.dot(left, right, preferred_element_type=jnp.float32)


def matmul_back(left, right):
    return lax.dot_general(
        left, right, (((1,), (1,)), ((), ())), preferred_element_type=jnp.float32
    )


def matmul_outer(left, right):
    return lax.dot_general(
        left, right, (((0,), (0,)), ((), ())), preferred_element_type=jnp.float32
    )


def block_term(factors, count, first, width):
    pieces = []
    for left, right, base in factors:
        lower = max(first, base)
        upper = min(first + width, base + right.shape[1])
        if lower < upper:
            rows_part = lax.slice_in_dim(left, 0, count, axis=1)
            pieces.append(matmul_outer(rows_part, right[:, lower - base : upper - base]))
    return jnp.concatenate(pieces, axis=1)

LANES = 384
PER_HALF = 18


def reduce_kernel(
    at_ref, b_ref, out_ref,
    bbuf, gbuf, sbuf, tbuf, ubuf, fbuf, core_in, one_in, two_in, z_in, far_in,
    bsem, core_sem, one_sem, two_sem, zs_sem, zr_sem, far_sem,
):
    narrow = lax.axis_index("narrow")
    wide = lax.axis_index("wide")
    core = wide % 2
    row = (wide // 2) % 2
    deep = wide // 4
    core_peer = (narrow, wide + 1 - 2 * core)
    x_peer = (1 - narrow, wide)
    y_peer = (narrow, wide + 2 - 4 * row)
    z_to = [(narrow, (deep + o) % 4 * 4 + wide % 4) for o in (1, 2, 3)]

    barrier = pltpu.get_barrier_semaphore()
    for peer in [core_peer, x_peer, y_peer] + z_to:
        pl.semaphore_signal(barrier, inc=1, device_id=peer, device_id_type=MESH)
    pl.semaphore_wait(barrier, 6)

    def fetch(chunk, half):
        number = chunk + half * PER_HALF
        column = number - 3 * ((number - 24) // 3) * (number // 24)
        column = pl.multiple_of(column * LANES, LANES)
        return pltpu.make_async_copy(
            b_ref.at[:, pl.ds(column, LANES)], bbuf.at[half], bsem.at[half]
        )

    def send(src, dst, sems, chunk, peer):
        return pltpu.make_async_remote_copy(
            src_ref=src, dst_ref=dst, send_sem=sems.at[0, chunk], recv_sem=sems.at[1, chunk],
            device_id=peer, device_id_type=MESH,
        )

    def core_copy(chunk):
        return send(gbuf.at[1 - core], core_in.at[chunk], core_sem, chunk, core_peer)

    def one_copy(chunk, even):
        slot = chunk % DEPTH
        if even:
            return send(sbuf.at[slot, 1 - narrow], one_in.at[chunk], one_sem, chunk, x_peer)
        return send(sbuf.at[slot, 1 - row], one_in.at[chunk], one_sem, chunk, y_peer)

    def two_copy(chunk, even):
        slot = chunk % DEPTH
        if even:
            return send(tbuf.at[slot, 1 - row], two_in.at[chunk], two_sem, chunk, y_peer)
        return send(tbuf.at[slot, 1 - narrow], two_in.at[chunk], two_sem, chunk, x_peer)

    def z_copies(chunk):
        slot = chunk % DEPTH
        return [
            pltpu.make_async_remote_copy(
                src_ref=ubuf.at[slot, (deep + o) % 4], dst_ref=z_in.at[chunk, o - 1],
                send_sem=zs_sem.at[chunk, o - 1], recv_sem=zr_sem.at[chunk, o - 1],
                device_id=z_to[o - 1], device_id_type=MESH,
            )
            for o in (1, 2, 3)
        ]

    def far_copy(chunk):
        return send(fbuf.at[chunk], far_in.at[chunk], far_sem, chunk, x_peer)

    def add(left, right):
        return left.astype(jnp.float32) + right.astype(jnp.float32)

    def make(chunk):
        for half in range(2):
            number = chunk + half * PER_HALF
            which = (
                jnp.where(number >= 9, 1, 0) + jnp.where(number >= 12, 1, 0)
                + jnp.where(number >= 24, 1, 0) + jnp.where(number >= 27, 1, 0)
                + jnp.where(number >= 30, 1, 0) + jnp.where(number >= 33, 1, 0)
            )
            fetch(chunk, half).wait()
            for side in range(2):
                product = jnp.dot(
                    at_ref[which, side], bbuf[half], preferred_element_type=jnp.float32
                )
                for unit in range(8):
                    gbuf[side, half, unit] = product[unit * 72 : unit * 72 + 72].astype(jnp.bfloat16)

            @pl.when(chunk + 1 < PER_HALF)
            def _():
                fetch(chunk + 1, half).start()

        core_copy(chunk).start()

    def pair(chunk, even):
        core_copy(chunk).wait()
        slot = chunk % DEPTH

        def body(step, carry):
            half, unit = step // 8, step % 8
            value = add(gbuf[core, half, unit], core_in[chunk, half, unit]).astype(jnp.bfloat16)
            deep_at, row_at = unit // 2, unit % 2
            if even:
                sbuf[slot, half, row_at, deep_at] = value
            else:
                sbuf[slot, row_at, half, deep_at] = value
            return carry

        lax.fori_loop(0, 16, body, 0)
        one_copy(chunk, even).start()

    def first(chunk, even):
        one_copy(chunk, even).wait()
        slot = chunk % DEPTH
        mine = narrow if even else row

        def body(step, carry):
            outer, inner = step // 4, step % 4
            tbuf[slot, outer, inner] = add(
                sbuf[slot, mine, outer, inner], one_in[chunk, outer, inner]
            ).astype(jnp.bfloat16)
            return carry

        lax.fori_loop(0, 8, body, 0)
        two_copy(chunk, even).start()

    def second(chunk, even):
        two_copy(chunk, even).wait()
        slot = chunk % DEPTH
        mine = row if even else narrow

        def body(step, carry):
            ubuf[slot, step] = add(tbuf[slot, mine, step], two_in[chunk, step]).astype(jnp.bfloat16)
            return carry

        lax.fori_loop(0, 4, body, 0)
        for copy in z_copies(chunk):
            copy.start()

    def third(chunk):
        for copy in z_copies(chunk):
            copy.wait()
        total = add(ubuf[chunk % DEPTH, deep], z_in[chunk, 0])
        total = total + add(z_in[chunk, 1], z_in[chunk, 2])
        out_ref[narrow * PER_HALF + chunk] = total
        fbuf[chunk] = total.astype(jnp.bfloat16)
        far_copy(chunk).start()

    for half in range(2):
        fetch(0, half).start()

    def turn(step, carry):
        for parity in range(2):
            now = step * 2 + parity
            for lag, action, fixed in (
                (1 + 3 * DEPTH, third, False),
                (1 + 2 * DEPTH, second, True),
                (1 + DEPTH, first, True),
                (1, pair, True),
                (0, make, False),
            ):
                chunk = now - lag
                even = (parity - lag) % 2 == 0

                @pl.when(jnp.logical_and(chunk >= 0, chunk < PER_HALF))
                def _(action=action, fixed=fixed, chunk=chunk, even=even):
                    action(chunk, even) if fixed else action(chunk)

        return carry

    lax.fori_loop(0, (PER_HALF + 3 * DEPTH + 2) // 2, turn, 0)

    def finish(chunk, carry):
        far_copy(chunk).wait()
        out_ref[(1 - narrow) * PER_HALF + chunk] = far_in[chunk].astype(jnp.float32)
        return carry

    lax.fori_loop(0, PER_HALF, finish, 0)


def reduce_weights(transposed, right):
    bf = jnp.bfloat16
    dma = pltpu.SemaphoreType.DMA
    unit = (72, LANES)
    n = PER_HALF
    return pl.pallas_call(
        reduce_kernel,
        out_shape=jax.ShapeDtypeStruct((2 * n,) + unit, jnp.float32),
        in_specs=[
            pl.BlockSpec(memory_space=pltpu.VMEM),
            pl.BlockSpec(memory_space=pl.ANY),
        ],
        out_specs=pl.BlockSpec(memory_space=pltpu.VMEM),
        scratch_shapes=[
            pltpu.VMEM((2, 512, LANES), bf),
            pltpu.VMEM((2, 2, 8) + unit, bf),
            pltpu.VMEM((DEPTH, 2, 2, 4) + unit, bf),
            pltpu.VMEM((DEPTH, 2, 4) + unit, bf),
            pltpu.VMEM((DEPTH, 4) + unit, bf),
            pltpu.VMEM((n,) + unit, bf),
            pltpu.VMEM((n, 2, 8) + unit, bf),
            pltpu.VMEM((n, 2, 4) + unit, bf),
            pltpu.VMEM((n, 4) + unit, bf),
            pltpu.VMEM((n, 3) + unit, bf),
            pltpu.VMEM((n,) + unit, bf),
            dma((2,)),
            dma((2, n)),
            dma((2, n)),
            dma((2, n)),
            dma((n, 3)),
            dma((n, 3)),
            dma((2, n)),
        ],
        compiler_params=pltpu.CompilerParams(
            collective_id=1, has_side_effects=True, vmem_limit_bytes=66_000_000
        ),
        name="reduce_weights",
    )(transposed, right)


def by_holder(left, parts):
    tokens = left.shape[0]
    rows = left.T.reshape(8, 2, parts, 72, tokens)
    return rows.transpose(2, 1, 0, 3, 4).reshape(parts, 2, 576, tokens)


def weight_grads(first_input, attended, second_in, activated, grad_projected, grad_branch, grad_hidden, grad_mlp):
    transposed = jnp.concatenate(
        [by_holder(first_input, 1), by_holder(attended, 1), by_holder(second_in, 1), by_holder(activated, 4)]
    )
    right = jnp.concatenate([grad_projected, grad_branch, grad_hidden, grad_mlp], axis=1)
    done = reduce_weights(transposed, right)

    def flat(lower, upper):
        return done[lower:upper].transpose(1, 0, 2).reshape(72, (upper - lower) * LANES)

    down = done[24:].reshape(4, 3, 72, LANES).transpose(0, 2, 1, 3).reshape(288, 3 * LANES)
    return flat(0, 9), flat(9, 12), flat(12, 24), down


def place(index, wide_count):
    return (index // wide_count, index % wide_count)


def meet(total, me, wide_count):
    barrier = pltpu.get_barrier_semaphore()

    def greet(step, carry):
        pl.semaphore_signal(
            barrier, inc=1, device_id=place((me + step) % total, wide_count), device_id_type=MESH
        )
        return carry

    lax.fori_loop(1, total, greet, 0)
    pl.semaphore_wait(barrier, total - 1)


def exchange(step, source, landing, send_sems, recv_sems, peer):
    return pltpu.make_async_remote_copy(
        src_ref=source, dst_ref=landing, send_sem=send_sems.at[step], recv_sem=recv_sems.at[step],
        device_id=peer, device_id_type=MESH,
    )


def loop(count, action):
    def body(step, carry):
        action(step)
        return carry

    lax.fori_loop(1, count, body, 0)


GATHER_CHUNKS = 6


def gather_steps(shard_ref, full_ref, own_sem, zs_sem, zr_sem, one_sem, two_sem, core_sem):
    narrow, wide = lax.axis_index("narrow"), lax.axis_index("wide")
    core, row, deep = wide % 2, (wide // 2) % 2, wide // 4
    core_peer = (narrow, wide + 1 - 2 * core)
    x_peer = (1 - narrow, wide)
    y_peer = (narrow, wide + 2 - 4 * row)

    def span(chunk, half):
        return pl.ds(pl.multiple_of((chunk + half * GATHER_CHUNKS) * LANES, LANES), LANES)

    def send(view, sems, chunk, number, peer):
        return pltpu.make_async_remote_copy(
            src_ref=view, dst_ref=view, send_sem=sems.at[0, chunk, number],
            recv_sem=sems.at[1, chunk, number], device_id=peer, device_id_type=MESH,
        )

    def own(chunk):
        return pltpu.make_async_copy(
            shard_ref.at[:, span(chunk, narrow)],
            full_ref.at[deep, row, core, :, span(chunk, narrow)],
            own_sem.at[chunk],
        )

    def along_z(chunk):
        return [
            pltpu.make_async_remote_copy(
                src_ref=shard_ref.at[:, span(chunk, narrow)],
                dst_ref=full_ref.at[deep, row, core, :, span(chunk, narrow)],
                send_sem=zs_sem.at[chunk, o - 1], recv_sem=zr_sem.at[chunk, o - 1],
                device_id=(narrow, (deep + o) % 4 * 4 + wide % 4), device_id_type=MESH,
            )
            for o in (1, 2, 3)
        ]

    def one(chunk):
        view = full_ref.at[:, row, core, :, span(chunk, narrow)]
        return [send(view, one_sem, chunk, 0, x_peer if chunk % 2 else y_peer)]

    def two(chunk):
        if chunk % 2:
            return [
                send(full_ref.at[:, row, core, :, span(chunk, half)], two_sem, chunk, half, y_peer)
                for half in range(2)
            ]
        return [
            send(full_ref.at[:, side, core, :, span(chunk, narrow)], two_sem, chunk, side, x_peer)
            for side in range(2)
        ]

    def across(chunk):
        return [
            send(full_ref.at[:, :, core, :, span(chunk, half)], core_sem, chunk, half, core_peer)
            for half in range(2)
        ]

    def begin():
        for chunk in range(GATHER_CHUNKS):
            own(chunk).start()
            for copy in along_z(chunk):
                copy.start()

    def run():
        stages = (lambda chunk: [own(chunk)] + along_z(chunk), one, two, across)
        for turn in range(GATHER_CHUNKS + 3):
            for stage in (3, 2, 1, 0):
                chunk = turn - stage
                if 0 <= chunk < GATHER_CHUNKS:
                    for copy in stages[stage](chunk):
                        copy.wait()
                    if stage < 3:
                        for copy in stages[stage + 1](chunk):
                            copy.start()

    return begin, run


def front_kernel(narrow_count, wide_count, with_weights, *refs):
    if with_weights:
        pack_ref, weight_ref, bias_ref, shard_ref, all_ref, mod_ref, full_ref = refs[:7]
        part, send_sem, recv_sem, send_two, recv_two = refs[7:12]
        begin, run = gather_steps(shard_ref, full_ref, *refs[12:])
    else:
        pack_ref, weight_ref, bias_ref, all_ref, mod_ref = refs[:5]
        part, send_sem, recv_sem, send_two, recv_two = refs[5:]
    total = narrow_count * wide_count
    narrow, wide = lax.axis_index("narrow"), lax.axis_index("wide")
    me = narrow * wide_count + wide
    base = narrow * wide_count
    meet(total, me, wide_count)

    def spread(step):
        return exchange(
            step, pack_ref, all_ref.at[me], send_sem, recv_sem, place((me + step) % total, wide_count)
        )

    loop(total, lambda step: spread(step).start())
    if with_weights:
        begin()
    all_ref[me] = pack_ref[...]
    loop(total, lambda step: spread(step).wait())
    rows = all_ref[pl.ds(base, wide_count)].astype(jnp.float32)
    rows = rows.reshape(wide_count * 8, rows.shape[2]).astype(jnp.bfloat16)
    product = jnp.dot(rows, weight_ref[...], preferred_element_type=jnp.float32)
    product = product + bias_ref[...].astype(jnp.float32)
    part[...] = product.reshape(part.shape).astype(jnp.bfloat16)

    def deal(step):
        to = (wide + step) % wide_count
        return exchange(step, part.at[to], mod_ref.at[wide], send_two, recv_two, (narrow, to))

    loop(wide_count, lambda step: deal(step).start())
    mod_ref[wide] = part[wide]
    if with_weights:
        run()
    loop(wide_count, lambda step: deal(step).wait())


def tail_kernel(
    narrow_count, wide_count, gift_ref, all_ref, weight_ref, ada_ref, misc_ref, cond_ref,
    gifts, part, shares, send_sem, recv_sem, send_two, recv_two,
):
    total = narrow_count * wide_count
    narrow, wide = lax.axis_index("narrow"), lax.axis_index("wide")
    me = narrow * wide_count + wide
    base = narrow * wide_count
    meet(total, me, wide_count)

    def spread(step):
        to = (me + step) % total
        return exchange(
            step, gift_ref.at[to % wide_count], gifts.at[me], send_sem, recv_sem, place(to, wide_count)
        )

    loop(total, lambda step: spread(step).start())
    gifts[me] = gift_ref[wide]
    loop(total, lambda step: spread(step).wait())
    mine = gifts[pl.ds(base, wide_count)].astype(jnp.float32)
    mine = mine.reshape(wide_count * 8, mine.shape[2]).astype(jnp.bfloat16)
    share = matmul_back(mine, weight_ref[...])
    part[...] = share.reshape(part.shape).astype(jnp.bfloat16)

    def deal(step):
        to = (wide + step) % wide_count
        return exchange(step, part.at[to], shares.at[wide], send_two, recv_two, (narrow, to))

    loop(wide_count, lambda step: deal(step).start())
    shares[wide] = part[wide]
    every = gifts[...].astype(jnp.float32)
    misc_ref[...] = jnp.sum(every, axis=0)
    grads = every.reshape(total * 8, every.shape[2]).astype(jnp.bfloat16)
    conds = all_ref[...].astype(jnp.float32)
    conds = conds.reshape(total * 8, conds.shape[2]).astype(jnp.bfloat16)
    ada_ref[...] = matmul_outer(conds, grads)
    loop(wide_count, lambda step: deal(step).wait())
    cond_ref[...] = jnp.sum(shares[...].astype(jnp.float32), axis=0)


def in_vmem(count):
    return [pl.BlockSpec(memory_space=pltpu.VMEM)] * count


def dmas(*counts):
    return [pltpu.SemaphoreType.DMA((count,)) for count in counts]


def front(cond_act, biases, ada_weight, ada_bias, shards):
    narrow_count, wide_count = lax.axis_size("narrow"), lax.axis_size("wide")
    total = narrow_count * wide_count
    slots, model_width = cond_act.shape
    columns = ada_weight.shape[1]
    bias_row = jnp.concatenate(biases)
    bias_row = jnp.pad(bias_row, (0, model_width - bias_row.shape[0]))[None]
    pack = jnp.concatenate(
        [cond_act, bias_row, jnp.zeros((7 - slots, model_width), jnp.bfloat16)]
    )
    with_weights = narrow_count == 2 and wide_count == 16
    operands = [pack, ada_weight, ada_bias[None]]
    shapes = [
        jax.ShapeDtypeStruct((total, 8, model_width), jnp.bfloat16),
        jax.ShapeDtypeStruct((wide_count, 8, columns), jnp.bfloat16),
    ]
    out_specs = in_vmem(2)
    scratch = [pltpu.VMEM((wide_count, 8, columns), jnp.bfloat16)]
    scratch += dmas(total, total, wide_count, wide_count)
    if with_weights:
        shard = jnp.concatenate(shards, axis=1)
        operands.append(shard)
        shapes.append(jax.ShapeDtypeStruct((4, 2, 2) + shard.shape, jnp.bfloat16))
        out_specs.append(pl.BlockSpec(memory_space=pl.ANY))
        n = GATHER_CHUNKS
        for dims in ((n,), (n, 3), (n, 3), (2, n, 1), (2, n, 2), (2, n, 2)):
            scratch.append(pltpu.SemaphoreType.DMA(dims))
    results = pl.pallas_call(
        partial(front_kernel, narrow_count, wide_count, with_weights),
        out_shape=tuple(shapes),
        in_specs=in_vmem(len(operands)),
        out_specs=tuple(out_specs),
        scratch_shapes=scratch,
        compiler_params=pltpu.CompilerParams(collective_id=2, has_side_effects=True),
        name="front",
    )(*operands)
    if not with_weights:
        return results + tuple(lax.all_gather(shard, "wide", axis=0, tiled=True) for shard in shards)
    full = results[2].reshape(wide_count * shard.shape[0], shard.shape[1])
    cut = shards[0].shape[1]
    return results[0], results[1], full[:, :cut], full[:, cut:]


def tail(grad_modulation, bias_grads, gathered, ada_weight):
    narrow_count, wide_count = lax.axis_size("narrow"), lax.axis_size("wide")
    total = narrow_count * wide_count
    slots = grad_modulation.shape[0]
    model_width, columns = ada_weight.shape
    blocks = grad_modulation.reshape(slots, wide_count, columns).transpose(1, 0, 2)
    held = jnp.concatenate(
        [grad.reshape(wide_count, -1) for grad in bias_grads], axis=1
    ).astype(jnp.bfloat16)
    lines = -(-held.shape[1] // columns)
    held_rows = jnp.pad(held, ((0, 0), (0, lines * columns - held.shape[1])))
    held_rows = held_rows.reshape(wide_count, lines, columns)
    gap = jnp.zeros((wide_count, 4 - slots, columns), jnp.bfloat16)
    end = jnp.zeros((wide_count, 4 - lines, columns), jnp.bfloat16)
    gift = jnp.concatenate([blocks, gap, held_rows, end], axis=1)
    ada, misc, cond = pl.pallas_call(
        partial(tail_kernel, narrow_count, wide_count),
        out_shape=(
            jax.ShapeDtypeStruct((model_width, columns), jnp.float32),
            jax.ShapeDtypeStruct((8, columns), jnp.float32),
            jax.ShapeDtypeStruct((8, model_width), jnp.float32),
        ),
        in_specs=in_vmem(3),
        out_specs=tuple(in_vmem(3)),
        scratch_shapes=[
            pltpu.VMEM((total, 8, columns), jnp.bfloat16),
            pltpu.VMEM((wide_count, 8, model_width), jnp.bfloat16),
            pltpu.VMEM((wide_count, 8, model_width), jnp.bfloat16),
        ]
        + dmas(total, total, wide_count, wide_count),
        compiler_params=pltpu.CompilerParams(collective_id=3, has_side_effects=True),
        name="tail",
    )(gift, gathered, ada_weight)
    flat = misc[4:].reshape(-1)
    grads, at = [], 0
    for grad in bias_grads:
        width = grad.shape[0] // wide_count
        grads.append(flat[at : at + width])
        at += width
    return ada, misc[:slots].sum(axis=0), cond[:slots], grads


def per_device(
    patches,
    condition,
    image_counts,
    ada_weight,
    ada_bias,
    inproj_weight,
    inproj_bias,
    outproj_weight,
    outproj_bias,
    up_weight,
    up_bias,
    down_weight,
    down_bias,
    cotangent,
):
    slots, seq_len, model_width = patches.shape
    head_dim = model_width // HEADS
    scale_qk = head_dim ** (-0.5)
    row_total = slots * seq_len
    wide_count = lax.axis_size("wide")
    live = (jnp.arange(slots) < image_counts[0]).astype(jnp.float32)[:, None, None]
    cond_act = jax.nn.silu(condition).astype(jnp.bfloat16)
    gathered, mod_blocks, w_inproj, w_outproj = front(
        cond_act, (inproj_bias, outproj_bias, up_bias, down_bias), ada_weight, ada_bias,
        (inproj_weight, outproj_weight),
    )
    modulation = (
        mod_blocks[:, :slots].transpose(1, 0, 2).reshape(slots, 6 * model_width).astype(jnp.float32)
    )
    group = lax.dynamic_slice_in_dim(
        gathered[:, slots], lax.axis_index("narrow") * wide_count, wide_count
    )
    all_biases, bias_at = [], 0
    for bias in (inproj_bias, outproj_bias, up_bias, down_bias):
        all_biases.append(group[:, bias_at : bias_at + bias.shape[0]].reshape(-1))
        bias_at += bias.shape[0]
    b_inproj, b_outproj, b_up, b_down = all_biases
    segment_list = [
        modulation[:, None, number * model_width : (number + 1) * model_width]
        for number in range(6)
    ]
    (
        selfattn_offset,
        selfattn_scale,
        selfattn_gate,
        perceptron_offset,
        perceptron_scale,
        perceptron_gate,
    ) = segment_list
    w_up = lax.all_gather(up_weight, "wide", axis=0, tiled=True)
    w_down = lax.all_gather(down_weight, "wide", axis=0, tiled=True)
    input_rows = patches.astype(jnp.float32)
    normalized_first, inverse_deviation = normalize(input_rows)
    first_input = (
        (normalized_first * (1.0 + selfattn_scale) + selfattn_offset)
        .astype(jnp.bfloat16)
        .reshape(row_total, model_width)
    )
    proj_bias = b_inproj.astype(jnp.float32)
    full_bias = jnp.concatenate(
        [proj_bias[:model_width], jnp.zeros((model_width,), jnp.float32), proj_bias[model_width:]]
    )
    projected = (matmul_rows(first_input, w_inproj) + full_bias).astype(jnp.bfloat16)
    query_rows = projected[:, :model_width].reshape(slots, seq_len, HEADS, head_dim)
    key_rows = projected[:, model_width : 2 * model_width].reshape(slots, seq_len, HEADS, head_dim)
    value_rows = projected[:, 2 * model_width :].reshape(slots, seq_len, HEADS, head_dim)
    scores = (
        jnp.einsum("sqhe,skhe->shqk", query_rows, key_rows, preferred_element_type=jnp.float32)
        * scale_qk
    )
    log_total = jax.nn.logsumexp(scores, axis=-1, keepdims=True)
    probs = jnp.exp(scores - log_total).astype(jnp.bfloat16)
    attended = jnp.einsum("shqk,skhe->sqhe", probs, value_rows, preferred_element_type=jnp.float32)
    attended = attended.astype(jnp.bfloat16).reshape(row_total, model_width)
    residual_branch = (matmul_rows(attended, w_outproj) + b_outproj.astype(jnp.float32)).reshape(
        slots, seq_len, model_width
    )
    between_state = input_rows + selfattn_gate * residual_branch
    normed_b, inv_b = normalize(between_state)
    second_in = (
        (normed_b * (1.0 + perceptron_scale) + perceptron_offset)
        .astype(jnp.bfloat16)
        .reshape(row_total, model_width)
    )
    hidden = matmul_rows(second_in, w_up) + b_up.astype(jnp.float32)
    gelu_value, gelu_pull = jax.vjp(partial(jax.nn.gelu, approximate=True), hidden)
    activated = gelu_value.astype(jnp.bfloat16)
    mlp_out = (matmul_rows(activated, w_down) + b_down.astype(jnp.float32)).reshape(
        slots, seq_len, model_width
    )
    output = ((between_state + perceptron_gate * mlp_out) * live).astype(jnp.bfloat16)
    wb_inproj, wb_outproj, wb_up, wb_down = w_inproj, w_outproj, w_up, w_down
    grad_out = cotangent.astype(jnp.float32) * live
    grad_gate_mlp = jnp.sum(grad_out * mlp_out, axis=1)
    grad_mlp = (grad_out * perceptron_gate).astype(jnp.bfloat16).reshape(row_total, model_width)
    grad_down_bias = jnp.sum(grad_mlp.astype(jnp.float32), axis=0)
    grad_act = matmul_back(grad_mlp, wb_down)
    grad_hidden = gelu_pull(grad_act)[0].astype(jnp.bfloat16)
    grad_up_bias = jnp.sum(grad_hidden.astype(jnp.float32), axis=0)
    grad_second = matmul_back(grad_hidden, wb_up).reshape(slots, seq_len, model_width)
    grad_scale_mlp = jnp.sum(grad_second * normed_b, axis=1)
    grad_shift_mlp = jnp.sum(grad_second, axis=1)
    between_gradient = grad_out + normalize_reverse(
        normed_b, inv_b, grad_second * (1.0 + perceptron_scale)
    )
    selfattn_gate_gradient = jnp.sum(between_gradient * residual_branch, axis=1)
    residual_branch_gradient = (
        (between_gradient * selfattn_gate).astype(jnp.bfloat16).reshape(row_total, model_width)
    )
    grad_outproj_bias = jnp.sum(residual_branch_gradient.astype(jnp.float32), axis=0)
    grad_attended = (
        matmul_back(residual_branch_gradient, wb_outproj)
        .astype(jnp.bfloat16)
        .reshape(slots, seq_len, HEADS, head_dim)
    )
    scores_again = (
        jnp.einsum("sqhe,skhe->shqk", query_rows, key_rows, preferred_element_type=jnp.float32)
        * scale_qk
    )
    probs_full = jnp.exp(scores_again - log_total)
    grad_values = jnp.einsum(
        "shqk,sqhe->skhe",
        probs_full.astype(jnp.bfloat16),
        grad_attended,
        preferred_element_type=jnp.float32,
    )
    grad_probs = jnp.einsum(
        "sqhe,skhe->shqk", grad_attended, value_rows, preferred_element_type=jnp.float32
    )
    row_dot = jnp.sum(grad_probs * probs_full, axis=-1, keepdims=True)
    grad_scores = (probs_full * (grad_probs - row_dot)).astype(jnp.bfloat16)
    grad_queries = (
        jnp.einsum("shqk,skhe->sqhe", grad_scores, key_rows, preferred_element_type=jnp.float32)
        * scale_qk
    )
    grad_keys = (
        jnp.einsum("shqk,sqhe->skhe", grad_scores, query_rows, preferred_element_type=jnp.float32)
        * scale_qk
    )
    grad_projected = jnp.concatenate(
        [
            grad_queries.reshape(row_total, model_width),
            grad_keys.reshape(row_total, model_width),
            grad_values.reshape(row_total, model_width),
        ],
        axis=1,
    ).astype(jnp.bfloat16)
    proj_sums = jnp.sum(grad_projected.astype(jnp.float32), axis=0)
    grad_inproj_bias = jnp.concatenate([proj_sums[:model_width], proj_sums[2 * model_width :]])
    first_gradient = matmul_back(grad_projected, wb_inproj).reshape(slots, seq_len, model_width)
    selfattn_scale_gradient = jnp.sum(first_gradient * normalized_first, axis=1)
    selfattn_offset_gradient = jnp.sum(first_gradient, axis=1)
    grad_patches = (
        between_gradient
        + normalize_reverse(
            normalized_first, inverse_deviation, first_gradient * (1.0 + selfattn_scale)
        )
    ).astype(jnp.bfloat16)
    grad_modulation = jnp.concatenate(
        [
            selfattn_offset_gradient,
            selfattn_scale_gradient,
            selfattn_gate_gradient,
            grad_shift_mlp,
            grad_scale_mlp,
            grad_gate_mlp,
        ],
        axis=1,
    ).astype(jnp.bfloat16)
    grad_ada_weight, grad_ada_bias, grad_cond_act, bias_shares = tail(
        grad_modulation,
        (grad_inproj_bias, grad_outproj_bias, grad_up_bias, grad_down_bias),
        gathered,
        ada_weight,
    )
    _, silu_pull = jax.vjp(jax.nn.silu, condition)
    grad_condition = silu_pull(grad_cond_act)[0]
    ff_width = activated.shape[1]
    input_factors = (
        (first_input, grad_projected, 0),
        (attended, residual_branch_gradient, 3 * model_width),
        (second_in, grad_hidden, 4 * model_width),
    )
    down_factors = ((activated, grad_mlp, 0),)
    input_block = (4 * model_width + ff_width) // 4
    down_block = model_width // 2
    block_jobs = [
        (input_factors, model_width, number * input_block, input_block) for number in range(4)
    ]
    block_jobs = block_jobs + [
        (down_factors, ff_width, number * down_block, down_block) for number in range(2)
    ]

    def reduce_block(factors, rows, first, width):
        return lax.psum_scatter(
            block_term(factors, lax.axis_size("wide") * (rows // wide_count), first, width).astype(
                jnp.bfloat16
            ),
            "wide",
            scatter_dimension=0,
            tiled=True,
        ).astype(jnp.float32)

    if lax.axis_size("narrow") == 2 and wide_count == 16:
        w_grads = weight_grads(
            first_input, attended, second_in, activated,
            grad_projected, residual_branch_gradient, grad_hidden, grad_mlp,
        )
    else:
        shards = [reduce_block(*job) for job in block_jobs]
        input_grads = jnp.concatenate(shards[:4], axis=1)
        w_grads = tuple(
            lax.psum(part.astype(jnp.bfloat16), "narrow").astype(jnp.float32)
            for part in (
                input_grads[:, : 3 * model_width],
                input_grads[:, 3 * model_width : 4 * model_width],
                input_grads[:, 4 * model_width :],
                jnp.concatenate(shards[4:], axis=1),
            )
        )
    return (
        output,
        grad_patches,
        grad_condition,
        grad_ada_weight,
        grad_ada_bias,
        w_grads[0],
        bias_shares[0],
        w_grads[1],
        bias_shares[1],
        w_grads[2],
        bias_shares[2],
        w_grads[3],
        bias_shares[3],
    )


def solution(mesh):
    in_specs = (
        P(("narrow", "wide"), None, None),
        P(("narrow", "wide"), None),
        P(("narrow", "wide")),
        P(None, "wide"),
        P("wide"),
        P("wide", None),
        P("wide"),
        P("wide", None),
        P("wide"),
        P("wide", None),
        P("wide"),
        P("wide", None),
        P("wide"),
        P(("narrow", "wide"), None, None),
    )
    out_specs = (
        P(("narrow", "wide"), None, None),
        P(("narrow", "wide"), None, None),
        P(("narrow", "wide"), None),
        P(None, "wide"),
        P("wide"),
        P("wide", None),
        P("wide"),
        P("wide", None),
        P("wide"),
        P("wide", None),
        P("wide"),
        P("wide", None),
        P("wide"),
    )
    return jax.shard_map(
        per_device, mesh=mesh, in_specs=in_specs, out_specs=out_specs, check_vma=False
    )
```

```python
from functools import partial

import jax
import jax.numpy as jnp
from jax import lax
from jax.sharding import PartitionSpec as P

from jax.experimental import pallas as pl
from jax.experimental.pallas import tpu as pltpu

HEADS = 16
MESH = pl.DeviceIdType.MESH
DEPTH = 2


norm_eps = 1e-06


def normalize(values):
    center = jnp.mean(values, axis=-1, keepdims=True)
    shifted = values - center
    inv_std = lax.rsqrt(jnp.mean(shifted * shifted, axis=-1, keepdims=True) + norm_eps)
    return (shifted * inv_std, inv_std)


def normalize_reverse(normed, inv_std, grad_normed):
    mean_grad = jnp.mean(grad_normed, axis=-1, keepdims=True)
    mean_proj = jnp.mean(grad_normed * normed, axis=-1, keepdims=True)
    return inv_std * (grad_normed - mean_grad - normed * mean_proj)


def matmul_rows(left, right):
    return jnp.dot(left, right, preferred_element_type=jnp.float32)


def matmul_back(left, right):
    return lax.dot_general(
        left, right, (((1,), (1,)), ((), ())), preferred_element_type=jnp.float32
    )


def matmul_outer(left, right):
    return lax.dot_general(
        left, right, (((0,), (0,)), ((), ())), preferred_element_type=jnp.float32
    )


def block_term(factors, count, first, width):
    pieces = []
    for left, right, base in factors:
        lower = max(first, base)
        upper = min(first + width, base + right.shape[1])
        if lower < upper:
            rows_part = lax.slice_in_dim(left, 0, count, axis=1)
            pieces.append(matmul_outer(rows_part, right[:, lower - base : upper - base]))
    return jnp.concatenate(pieces, axis=1)

LANES = 384
PER_HALF = 18


def reduce_kernel(
    at_ref, b_ref, out_ref,
    bbuf, gbuf, sbuf, tbuf, ubuf, fbuf, core_in, one_in, two_in, z_in, far_in,
    bsem, core_sem, one_sem, two_sem, zs_sem, zr_sem, far_sem,
):
    narrow = lax.axis_index("narrow")
    wide = lax.axis_index("wide")
    core = wide % 2
    row = (wide // 2) % 2
    deep = wide // 4
    core_peer = (narrow, wide + 1 - 2 * core)
    x_peer = (1 - narrow, wide)
    y_peer = (narrow, wide + 2 - 4 * row)
    z_to = [(narrow, (deep + o) % 4 * 4 + wide % 4) for o in (1, 2, 3)]

    barrier = pltpu.get_barrier_semaphore()
    for peer in [core_peer, x_peer, y_peer] + z_to:
        pl.semaphore_signal(barrier, inc=1, device_id=peer, device_id_type=MESH)
    pl.semaphore_wait(barrier, 6)

    def fetch(chunk, half):
        number = chunk + half * PER_HALF
        column = number - 3 * ((number - 24) // 3) * (number // 24)
        column = pl.multiple_of(column * LANES, LANES)
        return pltpu.make_async_copy(
            b_ref.at[:, pl.ds(column, LANES)], bbuf.at[half], bsem.at[half]
        )

    def send(src, dst, sems, chunk, peer):
        return pltpu.make_async_remote_copy(
            src_ref=src, dst_ref=dst, send_sem=sems.at[0, chunk], recv_sem=sems.at[1, chunk],
            device_id=peer, device_id_type=MESH,
        )

    def core_copy(chunk):
        return send(gbuf.at[1 - core], core_in.at[chunk], core_sem, chunk, core_peer)

    def one_copy(chunk, even):
        slot = chunk % DEPTH
        if even:
            return send(sbuf.at[slot, 1 - narrow], one_in.at[chunk], one_sem, chunk, x_peer)
        return send(sbuf.at[slot, 1 - row], one_in.at[chunk], one_sem, chunk, y_peer)

    def two_copy(chunk, even):
        slot = chunk % DEPTH
        if even:
            return send(tbuf.at[slot, 1 - row], two_in.at[chunk], two_sem, chunk, y_peer)
        return send(tbuf.at[slot, 1 - narrow], two_in.at[chunk], two_sem, chunk, x_peer)

    def z_copies(chunk):
        slot = chunk % DEPTH
        return [
            pltpu.make_async_remote_copy(
                src_ref=ubuf.at[slot, (deep + o) % 4], dst_ref=z_in.at[chunk, o - 1],
                send_sem=zs_sem.at[chunk, o - 1], recv_sem=zr_sem.at[chunk, o - 1],
                device_id=z_to[o - 1], device_id_type=MESH,
            )
            for o in (1, 2, 3)
        ]

    def far_copy(chunk):
        return send(fbuf.at[chunk], far_in.at[chunk], far_sem, chunk, x_peer)

    def add(left, right):
        return left.astype(jnp.float32) + right.astype(jnp.float32)

    def make(chunk):
        for half in range(2):
            number = chunk + half * PER_HALF
            which = (
                jnp.where(number >= 9, 1, 0) + jnp.where(number >= 12, 1, 0)
                + jnp.where(number >= 24, 1, 0) + jnp.where(number >= 27, 1, 0)
                + jnp.where(number >= 30, 1, 0) + jnp.where(number >= 33, 1, 0)
            )
            fetch(chunk, half).wait()
            for side in range(2):
                product = jnp.dot(
                    at_ref[which, side], bbuf[half], preferred_element_type=jnp.float32
                )
                for unit in range(8):
                    gbuf[side, half, unit] = product[unit * 72 : unit * 72 + 72].astype(jnp.bfloat16)

            @pl.when(chunk + 1 < PER_HALF)
            def _():
                fetch(chunk + 1, half).start()

        core_copy(chunk).start()

    def pair(chunk, even):
        core_copy(chunk).wait()
        slot = chunk % DEPTH

        def body(step, carry):
            half, unit = step // 8, step % 8
            value = add(gbuf[core, half, unit], core_in[chunk, half, unit]).astype(jnp.bfloat16)
            deep_at, row_at = unit // 2, unit % 2
            if even:
                sbuf[slot, half, row_at, deep_at] = value
            else:
                sbuf[slot, row_at, half, deep_at] = value
            return carry

        lax.fori_loop(0, 16, body, 0)
        one_copy(chunk, even).start()

    def first(chunk, even):
        one_copy(chunk, even).wait()
        slot = chunk % DEPTH
        mine = narrow if even else row

        def body(step, carry):
            outer, inner = step // 4, step % 4
            tbuf[slot, outer, inner] = add(
                sbuf[slot, mine, outer, inner], one_in[chunk, outer, inner]
            ).astype(jnp.bfloat16)
            return carry

        lax.fori_loop(0, 8, body, 0)
        two_copy(chunk, even).start()

    def second(chunk, even):
        two_copy(chunk, even).wait()
        slot = chunk % DEPTH
        mine = row if even else narrow

        def body(step, carry):
            ubuf[slot, step] = add(tbuf[slot, mine, step], two_in[chunk, step]).astype(jnp.bfloat16)
            return carry

        lax.fori_loop(0, 4, body, 0)
        for copy in z_copies(chunk):
            copy.start()

    def third(chunk):
        for copy in z_copies(chunk):
            copy.wait()
        total = add(ubuf[chunk % DEPTH, deep], z_in[chunk, 0])
        total = total + add(z_in[chunk, 1], z_in[chunk, 2])
        out_ref[narrow * PER_HALF + chunk] = total
        fbuf[chunk] = total.astype(jnp.bfloat16)
        far_copy(chunk).start()

    for half in range(2):
        fetch(0, half).start()

    def turn(step, carry):
        for parity in range(2):
            now = step * 2 + parity
            for lag, action, fixed in (
                (1 + 3 * DEPTH, third, False),
                (1 + 2 * DEPTH, second, True),
                (1 + DEPTH, first, True),
                (1, pair, True),
                (0, make, False),
            ):
                chunk = now - lag
                even = (parity - lag) % 2 == 0

                @pl.when(jnp.logical_and(chunk >= 0, chunk < PER_HALF))
                def _(action=action, fixed=fixed, chunk=chunk, even=even):
                    action(chunk, even) if fixed else action(chunk)

        return carry

    lax.fori_loop(0, (PER_HALF + 3 * DEPTH + 2) // 2, turn, 0)

    def finish(chunk, carry):
        far_copy(chunk).wait()
        out_ref[(1 - narrow) * PER_HALF + chunk] = far_in[chunk].astype(jnp.float32)
        return carry

    lax.fori_loop(0, PER_HALF, finish, 0)


def reduce_weights(transposed, right):
    bf = jnp.bfloat16
    dma = pltpu.SemaphoreType.DMA
    unit = (72, LANES)
    n = PER_HALF
    return pl.pallas_call(
        reduce_kernel,
        out_shape=jax.ShapeDtypeStruct((2 * n,) + unit, jnp.float32),
        in_specs=[
            pl.BlockSpec(memory_space=pltpu.VMEM),
            pl.BlockSpec(memory_space=pl.ANY),
        ],
        out_specs=pl.BlockSpec(memory_space=pltpu.VMEM),
        scratch_shapes=[
            pltpu.VMEM((2, 512, LANES), bf),
            pltpu.VMEM((2, 2, 8) + unit, bf),
            pltpu.VMEM((DEPTH, 2, 2, 4) + unit, bf),
            pltpu.VMEM((DEPTH, 2, 4) + unit, bf),
            pltpu.VMEM((DEPTH, 4) + unit, bf),
            pltpu.VMEM((n,) + unit, bf),
            pltpu.VMEM((n, 2, 8) + unit, bf),
            pltpu.VMEM((n, 2, 4) + unit, bf),
            pltpu.VMEM((n, 4) + unit, bf),
            pltpu.VMEM((n, 3) + unit, bf),
            pltpu.VMEM((n,) + unit, bf),
            dma((2,)),
            dma((2, n)),
            dma((2, n)),
            dma((2, n)),
            dma((n, 3)),
            dma((n, 3)),
            dma((2, n)),
        ],
        compiler_params=pltpu.CompilerParams(
            collective_id=1, has_side_effects=True, vmem_limit_bytes=66_000_000
        ),
        name="reduce_weights",
    )(transposed, right)


def by_holder(left, parts):
    tokens = left.shape[0]
    rows = left.T.reshape(8, 2, parts, 72, tokens)
    return rows.transpose(2, 1, 0, 3, 4).reshape(parts, 2, 576, tokens)


def weight_grads(first_input, attended, second_in, activated, grad_projected, grad_branch, grad_hidden, grad_mlp):
    transposed = jnp.concatenate(
        [by_holder(first_input, 1), by_holder(attended, 1), by_holder(second_in, 1), by_holder(activated, 4)]
    )
    right = jnp.concatenate([grad_projected, grad_branch, grad_hidden, grad_mlp], axis=1)
    done = reduce_weights(transposed, right)

    def flat(lower, upper):
        return done[lower:upper].transpose(1, 0, 2).reshape(72, (upper - lower) * LANES)

    down = done[24:].reshape(4, 3, 72, LANES).transpose(0, 2, 1, 3).reshape(288, 3 * LANES)
    return flat(0, 9), flat(9, 12), flat(12, 24), down


def place(index, wide_count):
    return (index // wide_count, index % wide_count)


def meet(total, me, wide_count):
    barrier = pltpu.get_barrier_semaphore()

    def greet(step, carry):
        pl.semaphore_signal(
            barrier, inc=1, device_id=place((me + step) % total, wide_count), device_id_type=MESH
        )
        return carry

    lax.fori_loop(1, total, greet, 0)
    pl.semaphore_wait(barrier, total - 1)


def exchange(step, source, landing, send_sems, recv_sems, peer):
    return pltpu.make_async_remote_copy(
        src_ref=source, dst_ref=landing, send_sem=send_sems.at[step], recv_sem=recv_sems.at[step],
        device_id=peer, device_id_type=MESH,
    )


def loop(count, action):
    def body(step, carry):
        action(step)
        return carry

    lax.fori_loop(1, count, body, 0)


def gather_steps(shard_ref, full_ref, own_sem, zs_sem, zr_sem, one_sem, two_sem, core_sem):
    narrow, wide = lax.axis_index("narrow"), lax.axis_index("wide")
    core, row, deep = wide % 2, (wide // 2) % 2, wide // 4
    core_peer = (narrow, wide + 1 - 2 * core)
    x_peer = (1 - narrow, wide)
    y_peer = (narrow, wide + 2 - 4 * row)
    chunks = shard_ref.shape[1] // (2 * LANES)

    def span(chunk, half):
        return pl.ds(pl.multiple_of((chunk + half * chunks) * LANES, LANES), LANES)

    def send(view, sems, chunk, number, peer):
        return pltpu.make_async_remote_copy(
            src_ref=view, dst_ref=view, send_sem=sems.at[0, chunk, number],
            recv_sem=sems.at[1, chunk, number], device_id=peer, device_id_type=MESH,
        )

    def own(chunk):
        return pltpu.make_async_copy(
            shard_ref.at[:, span(chunk, narrow)],
            full_ref.at[deep, row, core, :, span(chunk, narrow)],
            own_sem.at[chunk],
        )

    def along_z(chunk):
        return [
            pltpu.make_async_remote_copy(
                src_ref=shard_ref.at[:, span(chunk, narrow)],
                dst_ref=full_ref.at[deep, row, core, :, span(chunk, narrow)],
                send_sem=zs_sem.at[chunk, o - 1], recv_sem=zr_sem.at[chunk, o - 1],
                device_id=(narrow, (deep + o) % 4 * 4 + wide % 4), device_id_type=MESH,
            )
            for o in (1, 2, 3)
        ]

    def one(chunk):
        view = full_ref.at[:, row, core, :, span(chunk, narrow)]
        return [send(view, one_sem, chunk, 0, x_peer if chunk % 2 else y_peer)]

    def two(chunk):
        if chunk % 2:
            return [
                send(full_ref.at[:, row, core, :, span(chunk, half)], two_sem, chunk, half, y_peer)
                for half in range(2)
            ]
        return [
            send(full_ref.at[:, side, core, :, span(chunk, narrow)], two_sem, chunk, side, x_peer)
            for side in range(2)
        ]

    def across(chunk):
        return [
            send(full_ref.at[:, :, core, :, span(chunk, half)], core_sem, chunk, half, core_peer)
            for half in range(2)
        ]

    def begin():
        for chunk in range(chunks):
            own(chunk).start()
            for copy in along_z(chunk):
                copy.start()

    def run():
        stages = (lambda chunk: [own(chunk)] + along_z(chunk), one, two, across)
        for turn in range(chunks + 3):
            for stage in (3, 2, 1, 0):
                chunk = turn - stage
                if 0 <= chunk < chunks:
                    for copy in stages[stage](chunk):
                        copy.wait()
                    if stage < 3:
                        for copy in stages[stage + 1](chunk):
                            copy.start()

    return begin, run


def front_kernel(narrow_count, wide_count, with_weights, *refs):
    if with_weights:
        pack_ref, weight_ref, bias_ref, shard_ref, all_ref, mod_ref, full_ref = refs[:7]
        part, send_sem, recv_sem, send_two, recv_two = refs[7:12]
        begin, run = gather_steps(shard_ref, full_ref, *refs[12:])
    else:
        pack_ref, weight_ref, bias_ref, all_ref, mod_ref = refs[:5]
        part, send_sem, recv_sem, send_two, recv_two = refs[5:]
    total = narrow_count * wide_count
    narrow, wide = lax.axis_index("narrow"), lax.axis_index("wide")
    me = narrow * wide_count + wide
    base = narrow * wide_count
    meet(total, me, wide_count)

    def spread(step):
        return exchange(
            step, pack_ref, all_ref.at[me], send_sem, recv_sem, place((me + step) % total, wide_count)
        )

    loop(total, lambda step: spread(step).start())
    if with_weights:
        begin()
    all_ref[me] = pack_ref[...]
    loop(total, lambda step: spread(step).wait())
    rows = all_ref[pl.ds(base, wide_count)].astype(jnp.float32)
    rows = rows.reshape(wide_count * 8, rows.shape[2]).astype(jnp.bfloat16)
    product = jnp.dot(rows, weight_ref[...], preferred_element_type=jnp.float32)
    product = product + bias_ref[...].astype(jnp.float32)
    part[...] = product.reshape(part.shape).astype(jnp.bfloat16)

    def deal(step):
        to = (wide + step) % wide_count
        return exchange(step, part.at[to], mod_ref.at[wide], send_two, recv_two, (narrow, to))

    loop(wide_count, lambda step: deal(step).start())
    mod_ref[wide] = part[wide]
    if with_weights:
        run()
    loop(wide_count, lambda step: deal(step).wait())


def tail_kernel(
    narrow_count, wide_count, gift_ref, all_ref, weight_ref, ada_ref, misc_ref, cond_ref,
    gifts, part, shares, send_sem, recv_sem, send_two, recv_two,
):
    total = narrow_count * wide_count
    narrow, wide = lax.axis_index("narrow"), lax.axis_index("wide")
    me = narrow * wide_count + wide
    base = narrow * wide_count
    meet(total, me, wide_count)

    def spread(step):
        to = (me + step) % total
        return exchange(
            step, gift_ref.at[to % wide_count], gifts.at[me], send_sem, recv_sem, place(to, wide_count)
        )

    loop(total, lambda step: spread(step).start())
    gifts[me] = gift_ref[wide]
    loop(total, lambda step: spread(step).wait())
    mine = gifts[pl.ds(base, wide_count)].astype(jnp.float32)
    mine = mine.reshape(wide_count * 8, mine.shape[2]).astype(jnp.bfloat16)
    share = matmul_back(mine, weight_ref[...])
    part[...] = share.reshape(part.shape).astype(jnp.bfloat16)

    def deal(step):
        to = (wide + step) % wide_count
        return exchange(step, part.at[to], shares.at[wide], send_two, recv_two, (narrow, to))

    loop(wide_count, lambda step: deal(step).start())
    shares[wide] = part[wide]
    every = gifts[...].astype(jnp.float32)
    misc_ref[...] = jnp.sum(every, axis=0)
    grads = every.reshape(total * 8, every.shape[2]).astype(jnp.bfloat16)
    conds = all_ref[...].astype(jnp.float32)
    conds = conds.reshape(total * 8, conds.shape[2]).astype(jnp.bfloat16)
    ada_ref[...] = matmul_outer(conds, grads)
    loop(wide_count, lambda step: deal(step).wait())
    cond_ref[...] = jnp.sum(shares[...].astype(jnp.float32), axis=0)


def in_vmem(count):
    return [pl.BlockSpec(memory_space=pltpu.VMEM)] * count


def dmas(*counts):
    return [pltpu.SemaphoreType.DMA((count,)) for count in counts]


def front(cond_act, biases, ada_weight, ada_bias, shards):
    narrow_count, wide_count = lax.axis_size("narrow"), lax.axis_size("wide")
    total = narrow_count * wide_count
    slots, model_width = cond_act.shape
    columns = ada_weight.shape[1]
    bias_row = jnp.concatenate(biases)
    bias_row = jnp.pad(bias_row, (0, model_width - bias_row.shape[0]))[None]
    pack = jnp.concatenate(
        [cond_act, bias_row, jnp.zeros((7 - slots, model_width), jnp.bfloat16)]
    )
    with_weights = narrow_count == 2 and wide_count == 16
    operands = [pack, ada_weight, ada_bias[None]]
    shapes = [
        jax.ShapeDtypeStruct((total, 8, model_width), jnp.bfloat16),
        jax.ShapeDtypeStruct((wide_count, 8, columns), jnp.bfloat16),
    ]
    out_specs = in_vmem(2)
    scratch = [pltpu.VMEM((wide_count, 8, columns), jnp.bfloat16)]
    scratch += dmas(total, total, wide_count, wide_count)
    if with_weights:
        shard = jnp.concatenate(shards, axis=1)
        operands.append(shard)
        shapes.append(jax.ShapeDtypeStruct((4, 2, 2) + shard.shape, jnp.bfloat16))
        out_specs.append(pl.BlockSpec(memory_space=pl.ANY))
        n = shard.shape[1] // (2 * LANES)
        for dims in ((n,), (n, 3), (n, 3), (2, n, 1), (2, n, 2), (2, n, 2)):
            scratch.append(pltpu.SemaphoreType.DMA(dims))
    results = pl.pallas_call(
        partial(front_kernel, narrow_count, wide_count, with_weights),
        out_shape=tuple(shapes),
        in_specs=in_vmem(len(operands)),
        out_specs=tuple(out_specs),
        scratch_shapes=scratch,
        compiler_params=pltpu.CompilerParams(collective_id=2, has_side_effects=True),
        name="front",
    )(*operands)
    if not with_weights:
        return tuple(results) + tuple(lax.all_gather(shard, "wide", axis=0, tiled=True) for shard in shards)
    full = results[2].reshape(wide_count * shard.shape[0], shard.shape[1])
    weights, at = [], 0
    for piece in shards:
        weights.append(full[:, at : at + piece.shape[1]])
        at += piece.shape[1]
    return tuple(results[:2]) + tuple(weights)


def tail(grad_modulation, bias_grads, gathered, ada_weight):
    narrow_count, wide_count = lax.axis_size("narrow"), lax.axis_size("wide")
    total = narrow_count * wide_count
    slots = grad_modulation.shape[0]
    model_width, columns = ada_weight.shape
    blocks = grad_modulation.reshape(slots, wide_count, columns).transpose(1, 0, 2)
    held = jnp.concatenate(
        [grad.reshape(wide_count, -1) for grad in bias_grads], axis=1
    ).astype(jnp.bfloat16)
    lines = -(-held.shape[1] // columns)
    held_rows = jnp.pad(held, ((0, 0), (0, lines * columns - held.shape[1])))
    held_rows = held_rows.reshape(wide_count, lines, columns)
    gap = jnp.zeros((wide_count, 4 - slots, columns), jnp.bfloat16)
    end = jnp.zeros((wide_count, 4 - lines, columns), jnp.bfloat16)
    gift = jnp.concatenate([blocks, gap, held_rows, end], axis=1)
    ada, misc, cond = pl.pallas_call(
        partial(tail_kernel, narrow_count, wide_count),
        out_shape=(
            jax.ShapeDtypeStruct((model_width, columns), jnp.float32),
            jax.ShapeDtypeStruct((8, columns), jnp.float32),
            jax.ShapeDtypeStruct((8, model_width), jnp.float32),
        ),
        in_specs=in_vmem(3),
        out_specs=tuple(in_vmem(3)),
        scratch_shapes=[
            pltpu.VMEM((total, 8, columns), jnp.bfloat16),
            pltpu.VMEM((wide_count, 8, model_width), jnp.bfloat16),
            pltpu.VMEM((wide_count, 8, model_width), jnp.bfloat16),
        ]
        + dmas(total, total, wide_count, wide_count),
        compiler_params=pltpu.CompilerParams(collective_id=3, has_side_effects=True),
        name="tail",
    )(gift, gathered, ada_weight)
    flat = misc[4:].reshape(-1)
    grads, at = [], 0
    for grad in bias_grads:
        width = grad.shape[0] // wide_count
        grads.append(flat[at : at + width])
        at += width
    return ada, misc[:slots].sum(axis=0), cond[:slots], grads


def per_device(
    patches,
    condition,
    image_counts,
    ada_weight,
    ada_bias,
    inproj_weight,
    inproj_bias,
    outproj_weight,
    outproj_bias,
    up_weight,
    up_bias,
    down_weight,
    down_bias,
    cotangent,
):
    slots, seq_len, model_width = patches.shape
    head_dim = model_width // HEADS
    scale_qk = head_dim ** (-0.5)
    row_total = slots * seq_len
    wide_count = lax.axis_size("wide")
    live = (jnp.arange(slots) < image_counts[0]).astype(jnp.float32)[:, None, None]
    cond_act = jax.nn.silu(condition).astype(jnp.bfloat16)
    gathered, mod_blocks, w_inproj, w_outproj, w_up = front(
        cond_act, (inproj_bias, outproj_bias, up_bias, down_bias), ada_weight, ada_bias,
        (inproj_weight, outproj_weight, up_weight),
    )
    down_weight, mod_blocks = lax.optimization_barrier((down_weight, mod_blocks))
    modulation = (
        mod_blocks[:, :slots].transpose(1, 0, 2).reshape(slots, 6 * model_width).astype(jnp.float32)
    )
    group = lax.dynamic_slice_in_dim(
        gathered[:, slots], lax.axis_index("narrow") * wide_count, wide_count
    )
    all_biases, bias_at = [], 0
    for bias in (inproj_bias, outproj_bias, up_bias, down_bias):
        all_biases.append(group[:, bias_at : bias_at + bias.shape[0]].reshape(-1))
        bias_at += bias.shape[0]
    b_inproj, b_outproj, b_up, b_down = all_biases
    segment_list = [
        modulation[:, None, number * model_width : (number + 1) * model_width]
        for number in range(6)
    ]
    (
        selfattn_offset,
        selfattn_scale,
        selfattn_gate,
        perceptron_offset,
        perceptron_scale,
        perceptron_gate,
    ) = segment_list
    w_down = lax.all_gather(down_weight, "wide", axis=0, tiled=True)
    input_rows = patches.astype(jnp.float32)
    normalized_first, inverse_deviation = normalize(input_rows)
    first_input = (
        (normalized_first * (1.0 + selfattn_scale) + selfattn_offset)
        .astype(jnp.bfloat16)
        .reshape(row_total, model_width)
    )
    proj_bias = b_inproj.astype(jnp.float32)
    full_bias = jnp.concatenate(
        [proj_bias[:model_width], jnp.zeros((model_width,), jnp.float32), proj_bias[model_width:]]
    )
    projected = (matmul_rows(first_input, w_inproj) + full_bias).astype(jnp.bfloat16)
    query_rows = projected[:, :model_width].reshape(slots, seq_len, HEADS, head_dim)
    key_rows = projected[:, model_width : 2 * model_width].reshape(slots, seq_len, HEADS, head_dim)
    value_rows = projected[:, 2 * model_width :].reshape(slots, seq_len, HEADS, head_dim)
    scores = (
        jnp.einsum("sqhe,skhe->shqk", query_rows, key_rows, preferred_element_type=jnp.float32)
        * scale_qk
    )
    log_total = jax.nn.logsumexp(scores, axis=-1, keepdims=True)
    probs = jnp.exp(scores - log_total).astype(jnp.bfloat16)
    attended = jnp.einsum("shqk,skhe->sqhe", probs, value_rows, preferred_element_type=jnp.float32)
    attended = attended.astype(jnp.bfloat16).reshape(row_total, model_width)
    residual_branch = (matmul_rows(attended, w_outproj) + b_outproj.astype(jnp.float32)).reshape(
        slots, seq_len, model_width
    )
    between_state = input_rows + selfattn_gate * residual_branch
    normed_b, inv_b = normalize(between_state)
    second_in = (
        (normed_b * (1.0 + perceptron_scale) + perceptron_offset)
        .astype(jnp.bfloat16)
        .reshape(row_total, model_width)
    )
    hidden = matmul_rows(second_in, w_up) + b_up.astype(jnp.float32)
    gelu_value, gelu_pull = jax.vjp(partial(jax.nn.gelu, approximate=True), hidden)
    activated = gelu_value.astype(jnp.bfloat16)
    w_down, activated = lax.optimization_barrier((w_down, activated))
    mlp_out = (matmul_rows(activated, w_down) + b_down.astype(jnp.float32)).reshape(
        slots, seq_len, model_width
    )
    output = ((between_state + perceptron_gate * mlp_out) * live).astype(jnp.bfloat16)
    wb_inproj, wb_outproj, wb_up, wb_down = w_inproj, w_outproj, w_up, w_down
    grad_out = cotangent.astype(jnp.float32) * live
    grad_gate_mlp = jnp.sum(grad_out * mlp_out, axis=1)
    grad_mlp = (grad_out * perceptron_gate).astype(jnp.bfloat16).reshape(row_total, model_width)
    grad_down_bias = jnp.sum(grad_mlp.astype(jnp.float32), axis=0)
    grad_act = matmul_back(grad_mlp, wb_down)
    grad_hidden = gelu_pull(grad_act)[0].astype(jnp.bfloat16)
    grad_up_bias = jnp.sum(grad_hidden.astype(jnp.float32), axis=0)
    grad_second = matmul_back(grad_hidden, wb_up).reshape(slots, seq_len, model_width)
    grad_scale_mlp = jnp.sum(grad_second * normed_b, axis=1)
    grad_shift_mlp = jnp.sum(grad_second, axis=1)
    between_gradient = grad_out + normalize_reverse(
        normed_b, inv_b, grad_second * (1.0 + perceptron_scale)
    )
    selfattn_gate_gradient = jnp.sum(between_gradient * residual_branch, axis=1)
    residual_branch_gradient = (
        (between_gradient * selfattn_gate).astype(jnp.bfloat16).reshape(row_total, model_width)
    )
    grad_outproj_bias = jnp.sum(residual_branch_gradient.astype(jnp.float32), axis=0)
    grad_attended = (
        matmul_back(residual_branch_gradient, wb_outproj)
        .astype(jnp.bfloat16)
        .reshape(slots, seq_len, HEADS, head_dim)
    )
    scores_again = (
        jnp.einsum("sqhe,skhe->shqk", query_rows, key_rows, preferred_element_type=jnp.float32)
        * scale_qk
    )
    probs_full = jnp.exp(scores_again - log_total)
    grad_values = jnp.einsum(
        "shqk,sqhe->skhe",
        probs_full.astype(jnp.bfloat16),
        grad_attended,
        preferred_element_type=jnp.float32,
    )
    grad_probs = jnp.einsum(
        "sqhe,skhe->shqk", grad_attended, value_rows, preferred_element_type=jnp.float32
    )
    row_dot = jnp.sum(grad_probs * probs_full, axis=-1, keepdims=True)
    grad_scores = (probs_full * (grad_probs - row_dot)).astype(jnp.bfloat16)
    grad_queries = (
        jnp.einsum("shqk,skhe->sqhe", grad_scores, key_rows, preferred_element_type=jnp.float32)
        * scale_qk
    )
    grad_keys = (
        jnp.einsum("shqk,sqhe->skhe", grad_scores, query_rows, preferred_element_type=jnp.float32)
        * scale_qk
    )
    grad_projected = jnp.concatenate(
        [
            grad_queries.reshape(row_total, model_width),
            grad_keys.reshape(row_total, model_width),
            grad_values.reshape(row_total, model_width),
        ],
        axis=1,
    ).astype(jnp.bfloat16)
    proj_sums = jnp.sum(grad_projected.astype(jnp.float32), axis=0)
    grad_inproj_bias = jnp.concatenate([proj_sums[:model_width], proj_sums[2 * model_width :]])
    first_gradient = matmul_back(grad_projected, wb_inproj).reshape(slots, seq_len, model_width)
    selfattn_scale_gradient = jnp.sum(first_gradient * normalized_first, axis=1)
    selfattn_offset_gradient = jnp.sum(first_gradient, axis=1)
    grad_patches = (
        between_gradient
        + normalize_reverse(
            normalized_first, inverse_deviation, first_gradient * (1.0 + selfattn_scale)
        )
    ).astype(jnp.bfloat16)
    grad_modulation = jnp.concatenate(
        [
            selfattn_offset_gradient,
            selfattn_scale_gradient,
            selfattn_gate_gradient,
            grad_shift_mlp,
            grad_scale_mlp,
            grad_gate_mlp,
        ],
        axis=1,
    ).astype(jnp.bfloat16)
    grad_ada_weight, grad_ada_bias, grad_cond_act, bias_shares = tail(
        grad_modulation,
        (grad_inproj_bias, grad_outproj_bias, grad_up_bias, grad_down_bias),
        gathered,
        ada_weight,
    )
    _, silu_pull = jax.vjp(jax.nn.silu, condition)
    grad_condition = silu_pull(grad_cond_act)[0]
    ff_width = activated.shape[1]
    input_factors = (
        (first_input, grad_projected, 0),
        (attended, residual_branch_gradient, 3 * model_width),
        (second_in, grad_hidden, 4 * model_width),
    )
    down_factors = ((activated, grad_mlp, 0),)
    input_block = (4 * model_width + ff_width) // 4
    down_block = model_width // 2
    block_jobs = [
        (input_factors, model_width, number * input_block, input_block) for number in range(4)
    ]
    block_jobs = block_jobs + [
        (down_factors, ff_width, number * down_block, down_block) for number in range(2)
    ]

    def reduce_block(factors, rows, first, width):
        return lax.psum_scatter(
            block_term(factors, lax.axis_size("wide") * (rows // wide_count), first, width).astype(
                jnp.bfloat16
            ),
            "wide",
            scatter_dimension=0,
            tiled=True,
        ).astype(jnp.float32)

    if lax.axis_size("narrow") == 2 and wide_count == 16:
        w_grads = weight_grads(
            first_input, attended, second_in, activated,
            grad_projected, residual_branch_gradient, grad_hidden, grad_mlp,
        )
    else:
        shards = [reduce_block(*job) for job in block_jobs]
        input_grads = jnp.concatenate(shards[:4], axis=1)
        w_grads = tuple(
            lax.psum(part.astype(jnp.bfloat16), "narrow").astype(jnp.float32)
            for part in (
                input_grads[:, : 3 * model_width],
                input_grads[:, 3 * model_width : 4 * model_width],
                input_grads[:, 4 * model_width :],
                jnp.concatenate(shards[4:], axis=1),
            )
        )
    return (
        output,
        grad_patches,
        grad_condition,
        grad_ada_weight,
        grad_ada_bias,
        w_grads[0],
        bias_shares[0],
        w_grads[1],
        bias_shares[1],
        w_grads[2],
        bias_shares[2],
        w_grads[3],
        bias_shares[3],
    )


def solution(mesh):
    in_specs = (
        P(("narrow", "wide"), None, None),
        P(("narrow", "wide"), None),
        P(("narrow", "wide")),
        P(None, "wide"),
        P("wide"),
        P("wide", None),
        P("wide"),
        P("wide", None),
        P("wide"),
        P("wide", None),
        P("wide"),
        P("wide", None),
        P("wide"),
        P(("narrow", "wide"), None, None),
    )
    out_specs = (
        P(("narrow", "wide"), None, None),
        P(("narrow", "wide"), None, None),
        P(("narrow", "wide"), None),
        P(None, "wide"),
        P("wide"),
        P("wide", None),
        P("wide"),
        P("wide", None),
        P("wide"),
        P("wide", None),
        P("wide"),
        P("wide", None),
        P("wide"),
    )
    return jax.shard_map(
        per_device, mesh=mesh, in_specs=in_specs, out_specs=out_specs, check_vma=False
    )
```

```python
from functools import partial

import jax
import jax.numpy as jnp
from jax import lax
from jax.sharding import PartitionSpec as P

from jax.experimental import pallas as pl
from jax.experimental.pallas import tpu as pltpu

HEADS = 16
MESH = pl.DeviceIdType.MESH
DEPTH = 4


norm_eps = 1e-06


def normalize(values):
    center = jnp.mean(values, axis=-1, keepdims=True)
    shifted = values - center
    inv_std = lax.rsqrt(jnp.mean(shifted * shifted, axis=-1, keepdims=True) + norm_eps)
    return (shifted * inv_std, inv_std)


def normalize_reverse(normed, inv_std, grad_normed):
    mean_grad = jnp.mean(grad_normed, axis=-1, keepdims=True)
    mean_proj = jnp.mean(grad_normed * normed, axis=-1, keepdims=True)
    return inv_std * (grad_normed - mean_grad - normed * mean_proj)


def matmul_rows(left, right):
    return jnp.dot(left, right, preferred_element_type=jnp.float32)


def matmul_back(left, right):
    return lax.dot_general(
        left, right, (((1,), (1,)), ((), ())), preferred_element_type=jnp.float32
    )


def matmul_outer(left, right):
    return lax.dot_general(
        left, right, (((0,), (0,)), ((), ())), preferred_element_type=jnp.float32
    )


def block_term(factors, count, first, width):
    pieces = []
    for left, right, base in factors:
        lower = max(first, base)
        upper = min(first + width, base + right.shape[1])
        if lower < upper:
            rows_part = lax.slice_in_dim(left, 0, count, axis=1)
            pieces.append(matmul_outer(rows_part, right[:, lower - base : upper - base]))
    return jnp.concatenate(pieces, axis=1)

LANES = 384
PER_HALF = 18


def reduce_kernel(
    at_ref, b_ref, out_ref,
    bbuf, gbuf, sbuf, tbuf, ubuf, fbuf, core_in, one_in, two_in, z_in, far_in,
    bsem, core_sem, one_sem, two_sem, zs_sem, zr_sem, far_sem,
):
    narrow = lax.axis_index("narrow")
    wide = lax.axis_index("wide")
    core = wide % 2
    row = (wide // 2) % 2
    deep = wide // 4
    core_peer = (narrow, wide + 1 - 2 * core)
    x_peer = (1 - narrow, wide)
    y_peer = (narrow, wide + 2 - 4 * row)
    z_to = [(narrow, (deep + o) % 4 * 4 + wide % 4) for o in (1, 2, 3)]

    barrier = pltpu.get_barrier_semaphore()
    for peer in [core_peer, x_peer, y_peer] + z_to:
        pl.semaphore_signal(barrier, inc=1, device_id=peer, device_id_type=MESH)
    pl.semaphore_wait(barrier, 6)

    def fetch(chunk, half):
        number = chunk + half * PER_HALF
        column = number - 3 * ((number - 24) // 3) * (number // 24)
        column = pl.multiple_of(column * LANES, LANES)
        return pltpu.make_async_copy(
            b_ref.at[:, pl.ds(column, LANES)], bbuf.at[half], bsem.at[half]
        )

    def send(src, dst, sems, chunk, peer):
        return pltpu.make_async_remote_copy(
            src_ref=src, dst_ref=dst, send_sem=sems.at[0, chunk], recv_sem=sems.at[1, chunk],
            device_id=peer, device_id_type=MESH,
        )

    def core_copy(chunk):
        return send(gbuf.at[1 - core], core_in.at[chunk], core_sem, chunk, core_peer)

    def one_copy(chunk, even):
        slot = chunk % DEPTH
        if even:
            return send(sbuf.at[slot, 1 - narrow], one_in.at[chunk], one_sem, chunk, x_peer)
        return send(sbuf.at[slot, 1 - row], one_in.at[chunk], one_sem, chunk, y_peer)

    def two_copy(chunk, even):
        slot = chunk % DEPTH
        if even:
            return send(tbuf.at[slot, 1 - row], two_in.at[chunk], two_sem, chunk, y_peer)
        return send(tbuf.at[slot, 1 - narrow], two_in.at[chunk], two_sem, chunk, x_peer)

    def z_copies(chunk):
        slot = chunk % DEPTH
        return [
            pltpu.make_async_remote_copy(
                src_ref=ubuf.at[slot, (deep + o) % 4], dst_ref=z_in.at[chunk, o - 1],
                send_sem=zs_sem.at[chunk, o - 1], recv_sem=zr_sem.at[chunk, o - 1],
                device_id=z_to[o - 1], device_id_type=MESH,
            )
            for o in (1, 2, 3)
        ]

    def far_copy(chunk):
        return send(fbuf.at[chunk], far_in.at[chunk], far_sem, chunk, x_peer)

    def add(left, right):
        return left.astype(jnp.float32) + right.astype(jnp.float32)

    def make(chunk):
        for half in range(2):
            number = chunk + half * PER_HALF
            which = (
                jnp.where(number >= 9, 1, 0) + jnp.where(number >= 12, 1, 0)
                + jnp.where(number >= 24, 1, 0) + jnp.where(number >= 27, 1, 0)
                + jnp.where(number >= 30, 1, 0) + jnp.where(number >= 33, 1, 0)
            )
            fetch(chunk, half).wait()
            for side in range(2):
                product = jnp.dot(
                    at_ref[which, side], bbuf[half], preferred_element_type=jnp.float32
                )
                for unit in range(8):
                    gbuf[side, half, unit] = product[unit * 72 : unit * 72 + 72].astype(jnp.bfloat16)

            @pl.when(chunk + 1 < PER_HALF)
            def _():
                fetch(chunk + 1, half).start()

        core_copy(chunk).start()

    def pair(chunk, even):
        core_copy(chunk).wait()
        slot = chunk % DEPTH

        def body(step, carry):
            half, unit = step // 8, step % 8
            value = add(gbuf[core, half, unit], core_in[chunk, half, unit]).astype(jnp.bfloat16)
            deep_at, row_at = unit // 2, unit % 2
            if even:
                sbuf[slot, half, row_at, deep_at] = value
            else:
                sbuf[slot, row_at, half, deep_at] = value
            return carry

        lax.fori_loop(0, 16, body, 0)
        one_copy(chunk, even).start()

    def first(chunk, even):
        one_copy(chunk, even).wait()
        slot = chunk % DEPTH
        mine = narrow if even else row

        def body(step, carry):
            outer, inner = step // 4, step % 4
            tbuf[slot, outer, inner] = add(
                sbuf[slot, mine, outer, inner], one_in[chunk, outer, inner]
            ).astype(jnp.bfloat16)
            return carry

        lax.fori_loop(0, 8, body, 0)
        two_copy(chunk, even).start()

    def second(chunk, even):
        two_copy(chunk, even).wait()
        slot = chunk % DEPTH
        mine = row if even else narrow

        def body(step, carry):
            ubuf[slot, step] = add(tbuf[slot, mine, step], two_in[chunk, step]).astype(jnp.bfloat16)
            return carry

        lax.fori_loop(0, 4, body, 0)
        for copy in z_copies(chunk):
            copy.start()

    def third(chunk):
        for copy in z_copies(chunk):
            copy.wait()
        total = add(ubuf[chunk % DEPTH, deep], z_in[chunk, 0])
        total = total + add(z_in[chunk, 1], z_in[chunk, 2])
        out_ref[narrow * PER_HALF + chunk] = total
        fbuf[chunk] = total.astype(jnp.bfloat16)
        far_copy(chunk).start()

    for half in range(2):
        fetch(0, half).start()

    def turn(step, carry):
        for parity in range(2):
            now = step * 2 + parity
            for lag, action, fixed in (
                (1 + 3 * DEPTH, third, False),
                (1 + 2 * DEPTH, second, True),
                (1 + DEPTH, first, True),
                (1, pair, True),
                (0, make, False),
            ):
                chunk = now - lag
                even = (parity - lag) % 2 == 0

                @pl.when(jnp.logical_and(chunk >= 0, chunk < PER_HALF))
                def _(action=action, fixed=fixed, chunk=chunk, even=even):
                    action(chunk, even) if fixed else action(chunk)

        return carry

    lax.fori_loop(0, (PER_HALF + 3 * DEPTH + 2) // 2, turn, 0)

    def finish(chunk, carry):
        far_copy(chunk).wait()
        out_ref[(1 - narrow) * PER_HALF + chunk] = far_in[chunk].astype(jnp.float32)
        return carry

    lax.fori_loop(0, PER_HALF, finish, 0)


def reduce_weights(transposed, right):
    bf = jnp.bfloat16
    dma = pltpu.SemaphoreType.DMA
    unit = (72, LANES)
    n = PER_HALF
    return pl.pallas_call(
        reduce_kernel,
        out_shape=jax.ShapeDtypeStruct((2 * n,) + unit, jnp.float32),
        in_specs=[
            pl.BlockSpec(memory_space=pltpu.VMEM),
            pl.BlockSpec(memory_space=pl.ANY),
        ],
        out_specs=pl.BlockSpec(memory_space=pltpu.VMEM),
        scratch_shapes=[
            pltpu.VMEM((2, 512, LANES), bf),
            pltpu.VMEM((2, 2, 8) + unit, bf),
            pltpu.VMEM((DEPTH, 2, 2, 4) + unit, bf),
            pltpu.VMEM((DEPTH, 2, 4) + unit, bf),
            pltpu.VMEM((DEPTH, 4) + unit, bf),
            pltpu.VMEM((n,) + unit, bf),
            pltpu.VMEM((n, 2, 8) + unit, bf),
            pltpu.VMEM((n, 2, 4) + unit, bf),
            pltpu.VMEM((n, 4) + unit, bf),
            pltpu.VMEM((n, 3) + unit, bf),
            pltpu.VMEM((n,) + unit, bf),
            dma((2,)),
            dma((2, n)),
            dma((2, n)),
            dma((2, n)),
            dma((n, 3)),
            dma((n, 3)),
            dma((2, n)),
        ],
        compiler_params=pltpu.CompilerParams(
            collective_id=1, has_side_effects=True, vmem_limit_bytes=66_000_000
        ),
        name="reduce_weights",
    )(transposed, right)


def by_holder(left, parts):
    tokens = left.shape[0]
    rows = left.T.reshape(8, 2, parts, 72, tokens)
    return rows.transpose(2, 1, 0, 3, 4).reshape(parts, 2, 576, tokens)


def weight_grads(first_input, attended, second_in, activated, grad_projected, grad_branch, grad_hidden, grad_mlp):
    transposed = jnp.concatenate(
        [by_holder(first_input, 1), by_holder(attended, 1), by_holder(second_in, 1), by_holder(activated, 4)]
    )
    right = jnp.concatenate([grad_projected, grad_branch, grad_hidden, grad_mlp], axis=1)
    done = reduce_weights(transposed, right)

    def flat(lower, upper):
        return done[lower:upper].transpose(1, 0, 2).reshape(72, (upper - lower) * LANES)

    down = done[24:].reshape(4, 3, 72, LANES).transpose(0, 2, 1, 3).reshape(288, 3 * LANES)
    return flat(0, 9), flat(9, 12), flat(12, 24), down


def place(index, wide_count):
    return (index // wide_count, index % wide_count)


def meet(total, me, wide_count):
    barrier = pltpu.get_barrier_semaphore()

    def greet(step, carry):
        pl.semaphore_signal(
            barrier, inc=1, device_id=place((me + step) % total, wide_count), device_id_type=MESH
        )
        return carry

    lax.fori_loop(1, total, greet, 0)
    pl.semaphore_wait(barrier, total - 1)


def exchange(step, source, landing, send_sems, recv_sems, peer):
    return pltpu.make_async_remote_copy(
        src_ref=source, dst_ref=landing, send_sem=send_sems.at[step], recv_sem=recv_sems.at[step],
        device_id=peer, device_id_type=MESH,
    )


def loop(count, action):
    def body(step, carry):
        action(step)
        return carry

    lax.fori_loop(1, count, body, 0)


def gather_steps(shard_ref, full_ref, own_sem, zs_sem, zr_sem, one_sem, two_sem, core_sem):
    narrow, wide = lax.axis_index("narrow"), lax.axis_index("wide")
    core, row, deep = wide % 2, (wide // 2) % 2, wide // 4
    core_peer = (narrow, wide + 1 - 2 * core)
    x_peer = (1 - narrow, wide)
    y_peer = (narrow, wide + 2 - 4 * row)
    chunks = shard_ref.shape[1] // (2 * LANES)

    def span(chunk, half):
        return pl.ds(pl.multiple_of((chunk + half * chunks) * LANES, LANES), LANES)

    def send(view, sems, chunk, number, peer):
        return pltpu.make_async_remote_copy(
            src_ref=view, dst_ref=view, send_sem=sems.at[0, chunk, number],
            recv_sem=sems.at[1, chunk, number], device_id=peer, device_id_type=MESH,
        )

    def own(chunk):
        return pltpu.make_async_copy(
            shard_ref.at[:, span(chunk, narrow)],
            full_ref.at[deep, row, core, :, span(chunk, narrow)],
            own_sem.at[chunk],
        )

    def along_z(chunk):
        return [
            pltpu.make_async_remote_copy(
                src_ref=shard_ref.at[:, span(chunk, narrow)],
                dst_ref=full_ref.at[deep, row, core, :, span(chunk, narrow)],
                send_sem=zs_sem.at[chunk, o - 1], recv_sem=zr_sem.at[chunk, o - 1],
                device_id=(narrow, (deep + o) % 4 * 4 + wide % 4), device_id_type=MESH,
            )
            for o in (1, 2, 3)
        ]

    def one(chunk):
        view = full_ref.at[:, row, core, :, span(chunk, narrow)]
        return [send(view, one_sem, chunk, 0, x_peer if chunk % 2 else y_peer)]

    def two(chunk):
        if chunk % 2:
            return [
                send(full_ref.at[:, row, core, :, span(chunk, half)], two_sem, chunk, half, y_peer)
                for half in range(2)
            ]
        return [
            send(full_ref.at[:, side, core, :, span(chunk, narrow)], two_sem, chunk, side, x_peer)
            for side in range(2)
        ]

    def across(chunk):
        return [
            send(full_ref.at[:, :, core, :, span(chunk, half)], core_sem, chunk, half, core_peer)
            for half in range(2)
        ]

    def begin():
        for chunk in range(chunks):
            own(chunk).start()
            for copy in along_z(chunk):
                copy.start()

    def run():
        stages = (lambda chunk: [own(chunk)] + along_z(chunk), one, two, across)
        for turn in range(chunks + 4):
            for stage in (2, 1, 0):
                chunk = turn - 2 * stage
                if 0 <= chunk < chunks:
                    for copy in stages[stage](chunk):
                        copy.wait()
                    for copy in stages[stage + 1](chunk):
                        copy.start()
        for chunk in range(chunks):
            for copy in across(chunk):
                copy.wait()

    return begin, run


def front_kernel(narrow_count, wide_count, with_weights, *refs):
    if with_weights:
        pack_ref, weight_ref, bias_ref, shard_ref, all_ref, mod_ref, full_ref = refs[:7]
        part, send_sem, recv_sem, send_two, recv_two = refs[7:12]
        begin, run = gather_steps(shard_ref, full_ref, *refs[12:])
    else:
        pack_ref, weight_ref, bias_ref, all_ref, mod_ref = refs[:5]
        part, send_sem, recv_sem, send_two, recv_two = refs[5:]
    total = narrow_count * wide_count
    narrow, wide = lax.axis_index("narrow"), lax.axis_index("wide")
    me = narrow * wide_count + wide
    base = narrow * wide_count
    meet(total, me, wide_count)

    def spread(step):
        return exchange(
            step, pack_ref, all_ref.at[me], send_sem, recv_sem, place((me + step) % total, wide_count)
        )

    loop(total, lambda step: spread(step).start())
    if with_weights:
        begin()
    all_ref[me] = pack_ref[...]
    loop(total, lambda step: spread(step).wait())
    rows = all_ref[pl.ds(base, wide_count)].astype(jnp.float32)
    rows = rows.reshape(wide_count * 8, rows.shape[2]).astype(jnp.bfloat16)
    product = jnp.dot(rows, weight_ref[...], preferred_element_type=jnp.float32)
    product = product + bias_ref[...].astype(jnp.float32)
    part[...] = product.reshape(part.shape).astype(jnp.bfloat16)

    def deal(step):
        to = (wide + step) % wide_count
        return exchange(step, part.at[to], mod_ref.at[wide], send_two, recv_two, (narrow, to))

    loop(wide_count, lambda step: deal(step).start())
    mod_ref[wide] = part[wide]
    if with_weights:
        run()
    loop(wide_count, lambda step: deal(step).wait())


def tail_kernel(
    narrow_count, wide_count, gift_ref, all_ref, weight_ref, ada_ref, misc_ref, cond_ref,
    gifts, part, shares, send_sem, recv_sem, send_two, recv_two,
):
    total = narrow_count * wide_count
    narrow, wide = lax.axis_index("narrow"), lax.axis_index("wide")
    me = narrow * wide_count + wide
    base = narrow * wide_count
    meet(total, me, wide_count)

    def spread(step):
        to = (me + step) % total
        return exchange(
            step, gift_ref.at[to % wide_count], gifts.at[me], send_sem, recv_sem, place(to, wide_count)
        )

    loop(total, lambda step: spread(step).start())
    gifts[me] = gift_ref[wide]
    loop(total, lambda step: spread(step).wait())
    mine = gifts[pl.ds(base, wide_count)].astype(jnp.float32)
    mine = mine.reshape(wide_count * 8, mine.shape[2]).astype(jnp.bfloat16)
    share = matmul_back(mine, weight_ref[...])
    part[...] = share.reshape(part.shape).astype(jnp.bfloat16)

    def deal(step):
        to = (wide + step) % wide_count
        return exchange(step, part.at[to], shares.at[wide], send_two, recv_two, (narrow, to))

    loop(wide_count, lambda step: deal(step).start())
    shares[wide] = part[wide]
    every = gifts[...].astype(jnp.float32)
    misc_ref[...] = jnp.sum(every, axis=0)
    grads = every.reshape(total * 8, every.shape[2]).astype(jnp.bfloat16)
    conds = all_ref[...].astype(jnp.float32)
    conds = conds.reshape(total * 8, conds.shape[2]).astype(jnp.bfloat16)
    ada_ref[...] = matmul_outer(conds, grads)
    loop(wide_count, lambda step: deal(step).wait())
    cond_ref[...] = jnp.sum(shares[...].astype(jnp.float32), axis=0)


def in_vmem(count):
    return [pl.BlockSpec(memory_space=pltpu.VMEM)] * count


def dmas(*counts):
    return [pltpu.SemaphoreType.DMA((count,)) for count in counts]


def front(cond_act, biases, ada_weight, ada_bias, shards):
    narrow_count, wide_count = lax.axis_size("narrow"), lax.axis_size("wide")
    total = narrow_count * wide_count
    slots, model_width = cond_act.shape
    columns = ada_weight.shape[1]
    bias_row = jnp.concatenate(biases)
    bias_row = jnp.pad(bias_row, (0, model_width - bias_row.shape[0]))[None]
    pack = jnp.concatenate(
        [cond_act, bias_row, jnp.zeros((7 - slots, model_width), jnp.bfloat16)]
    )
    with_weights = narrow_count == 2 and wide_count == 16
    operands = [pack, ada_weight, ada_bias[None]]
    shapes = [
        jax.ShapeDtypeStruct((total, 8, model_width), jnp.bfloat16),
        jax.ShapeDtypeStruct((wide_count, 8, columns), jnp.bfloat16),
    ]
    out_specs = in_vmem(2)
    scratch = [pltpu.VMEM((wide_count, 8, columns), jnp.bfloat16)]
    scratch += dmas(total, total, wide_count, wide_count)
    if with_weights:
        shard = jnp.concatenate(shards, axis=1)
        operands.append(shard)
        shapes.append(jax.ShapeDtypeStruct((4, 2, 2) + shard.shape, jnp.bfloat16))
        out_specs.append(pl.BlockSpec(memory_space=pl.ANY))
        n = shard.shape[1] // (2 * LANES)
        for dims in ((n,), (n, 3), (n, 3), (2, n, 1), (2, n, 2), (2, n, 2)):
            scratch.append(pltpu.SemaphoreType.DMA(dims))
    results = pl.pallas_call(
        partial(front_kernel, narrow_count, wide_count, with_weights),
        out_shape=tuple(shapes),
        in_specs=in_vmem(len(operands)),
        out_specs=tuple(out_specs),
        scratch_shapes=scratch,
        compiler_params=pltpu.CompilerParams(collective_id=2, has_side_effects=True),
        name="front",
    )(*operands)
    if not with_weights:
        return tuple(results) + tuple(lax.all_gather(shard, "wide", axis=0, tiled=True) for shard in shards)
    full = results[2].reshape(wide_count * shard.shape[0], shard.shape[1])
    weights, at = [], 0
    for piece in shards:
        weights.append(full[:, at : at + piece.shape[1]])
        at += piece.shape[1]
    return tuple(results[:2]) + tuple(weights)


def tail(grad_modulation, bias_grads, gathered, ada_weight):
    narrow_count, wide_count = lax.axis_size("narrow"), lax.axis_size("wide")
    total = narrow_count * wide_count
    slots = grad_modulation.shape[0]
    model_width, columns = ada_weight.shape
    blocks = grad_modulation.reshape(slots, wide_count, columns).transpose(1, 0, 2)
    held = jnp.concatenate(
        [grad.reshape(wide_count, -1) for grad in bias_grads], axis=1
    ).astype(jnp.bfloat16)
    lines = -(-held.shape[1] // columns)
    held_rows = jnp.pad(held, ((0, 0), (0, lines * columns - held.shape[1])))
    held_rows = held_rows.reshape(wide_count, lines, columns)
    gap = jnp.zeros((wide_count, 4 - slots, columns), jnp.bfloat16)
    end = jnp.zeros((wide_count, 4 - lines, columns), jnp.bfloat16)
    gift = jnp.concatenate([blocks, gap, held_rows, end], axis=1)
    ada, misc, cond = pl.pallas_call(
        partial(tail_kernel, narrow_count, wide_count),
        out_shape=(
            jax.ShapeDtypeStruct((model_width, columns), jnp.float32),
            jax.ShapeDtypeStruct((8, columns), jnp.float32),
            jax.ShapeDtypeStruct((8, model_width), jnp.float32),
        ),
        in_specs=in_vmem(3),
        out_specs=tuple(in_vmem(3)),
        scratch_shapes=[
            pltpu.VMEM((total, 8, columns), jnp.bfloat16),
            pltpu.VMEM((wide_count, 8, model_width), jnp.bfloat16),
            pltpu.VMEM((wide_count, 8, model_width), jnp.bfloat16),
        ]
        + dmas(total, total, wide_count, wide_count),
        compiler_params=pltpu.CompilerParams(collective_id=3, has_side_effects=True),
        name="tail",
    )(gift, gathered, ada_weight)
    flat = misc[4:].reshape(-1)
    grads, at = [], 0
    for grad in bias_grads:
        width = grad.shape[0] // wide_count
        grads.append(flat[at : at + width])
        at += width
    return ada, misc[:slots].sum(axis=0), cond[:slots], grads


def per_device(
    patches,
    condition,
    image_counts,
    ada_weight,
    ada_bias,
    inproj_weight,
    inproj_bias,
    outproj_weight,
    outproj_bias,
    up_weight,
    up_bias,
    down_weight,
    down_bias,
    cotangent,
):
    slots, seq_len, model_width = patches.shape
    head_dim = model_width // HEADS
    scale_qk = head_dim ** (-0.5)
    row_total = slots * seq_len
    wide_count = lax.axis_size("wide")
    live = (jnp.arange(slots) < image_counts[0]).astype(jnp.float32)[:, None, None]
    cond_act = jax.nn.silu(condition).astype(jnp.bfloat16)
    gathered, mod_blocks, w_inproj, w_outproj, w_up = front(
        cond_act, (inproj_bias, outproj_bias, up_bias, down_bias), ada_weight, ada_bias,
        (inproj_weight, outproj_weight, up_weight),
    )
    down_weight, mod_blocks = lax.optimization_barrier((down_weight, mod_blocks))
    modulation = (
        mod_blocks[:, :slots].transpose(1, 0, 2).reshape(slots, 6 * model_width).astype(jnp.float32)
    )
    group = lax.dynamic_slice_in_dim(
        gathered[:, slots], lax.axis_index("narrow") * wide_count, wide_count
    )
    all_biases, bias_at = [], 0
    for bias in (inproj_bias, outproj_bias, up_bias, down_bias):
        all_biases.append(group[:, bias_at : bias_at + bias.shape[0]].reshape(-1))
        bias_at += bias.shape[0]
    b_inproj, b_outproj, b_up, b_down = all_biases
    segment_list = [
        modulation[:, None, number * model_width : (number + 1) * model_width]
        for number in range(6)
    ]
    (
        selfattn_offset,
        selfattn_scale,
        selfattn_gate,
        perceptron_offset,
        perceptron_scale,
        perceptron_gate,
    ) = segment_list
    w_down = lax.all_gather(down_weight, "wide", axis=0, tiled=True)
    input_rows = patches.astype(jnp.float32)
    normalized_first, inverse_deviation = normalize(input_rows)
    first_input = (
        (normalized_first * (1.0 + selfattn_scale) + selfattn_offset)
        .astype(jnp.bfloat16)
        .reshape(row_total, model_width)
    )
    proj_bias = b_inproj.astype(jnp.float32)
    full_bias = jnp.concatenate(
        [proj_bias[:model_width], jnp.zeros((model_width,), jnp.float32), proj_bias[model_width:]]
    )
    projected = (matmul_rows(first_input, w_inproj) + full_bias).astype(jnp.bfloat16)
    query_rows = projected[:, :model_width].reshape(slots, seq_len, HEADS, head_dim)
    key_rows = projected[:, model_width : 2 * model_width].reshape(slots, seq_len, HEADS, head_dim)
    value_rows = projected[:, 2 * model_width :].reshape(slots, seq_len, HEADS, head_dim)
    scores = (
        jnp.einsum("sqhe,skhe->shqk", query_rows, key_rows, preferred_element_type=jnp.float32)
        * scale_qk
    )
    log_total = jax.nn.logsumexp(scores, axis=-1, keepdims=True)
    probs = jnp.exp(scores - log_total).astype(jnp.bfloat16)
    attended = jnp.einsum("shqk,skhe->sqhe", probs, value_rows, preferred_element_type=jnp.float32)
    attended = attended.astype(jnp.bfloat16).reshape(row_total, model_width)
    residual_branch = (matmul_rows(attended, w_outproj) + b_outproj.astype(jnp.float32)).reshape(
        slots, seq_len, model_width
    )
    between_state = input_rows + selfattn_gate * residual_branch
    normed_b, inv_b = normalize(between_state)
    second_in = (
        (normed_b * (1.0 + perceptron_scale) + perceptron_offset)
        .astype(jnp.bfloat16)
        .reshape(row_total, model_width)
    )
    hidden = matmul_rows(second_in, w_up) + b_up.astype(jnp.float32)
    gelu_value, gelu_pull = jax.vjp(partial(jax.nn.gelu, approximate=True), hidden)
    activated = gelu_value.astype(jnp.bfloat16)
    w_down, activated = lax.optimization_barrier((w_down, activated))
    mlp_out = (matmul_rows(activated, w_down) + b_down.astype(jnp.float32)).reshape(
        slots, seq_len, model_width
    )
    output = ((between_state + perceptron_gate * mlp_out) * live).astype(jnp.bfloat16)
    wb_inproj, wb_outproj, wb_up, wb_down = w_inproj, w_outproj, w_up, w_down
    grad_out = cotangent.astype(jnp.float32) * live
    grad_gate_mlp = jnp.sum(grad_out * mlp_out, axis=1)
    grad_mlp = (grad_out * perceptron_gate).astype(jnp.bfloat16).reshape(row_total, model_width)
    grad_down_bias = jnp.sum(grad_mlp.astype(jnp.float32), axis=0)
    grad_act = matmul_back(grad_mlp, wb_down)
    grad_hidden = gelu_pull(grad_act)[0].astype(jnp.bfloat16)
    grad_up_bias = jnp.sum(grad_hidden.astype(jnp.float32), axis=0)
    grad_second = matmul_back(grad_hidden, wb_up).reshape(slots, seq_len, model_width)
    grad_scale_mlp = jnp.sum(grad_second * normed_b, axis=1)
    grad_shift_mlp = jnp.sum(grad_second, axis=1)
    between_gradient = grad_out + normalize_reverse(
        normed_b, inv_b, grad_second * (1.0 + perceptron_scale)
    )
    selfattn_gate_gradient = jnp.sum(between_gradient * residual_branch, axis=1)
    residual_branch_gradient = (
        (between_gradient * selfattn_gate).astype(jnp.bfloat16).reshape(row_total, model_width)
    )
    grad_outproj_bias = jnp.sum(residual_branch_gradient.astype(jnp.float32), axis=0)
    grad_attended = (
        matmul_back(residual_branch_gradient, wb_outproj)
        .astype(jnp.bfloat16)
        .reshape(slots, seq_len, HEADS, head_dim)
    )
    scores_again = (
        jnp.einsum("sqhe,skhe->shqk", query_rows, key_rows, preferred_element_type=jnp.float32)
        * scale_qk
    )
    probs_full = jnp.exp(scores_again - log_total)
    grad_values = jnp.einsum(
        "shqk,sqhe->skhe",
        probs_full.astype(jnp.bfloat16),
        grad_attended,
        preferred_element_type=jnp.float32,
    )
    grad_probs = jnp.einsum(
        "sqhe,skhe->shqk", grad_attended, value_rows, preferred_element_type=jnp.float32
    )
    row_dot = jnp.sum(grad_probs * probs_full, axis=-1, keepdims=True)
    grad_scores = (probs_full * (grad_probs - row_dot)).astype(jnp.bfloat16)
    grad_queries = (
        jnp.einsum("shqk,skhe->sqhe", grad_scores, key_rows, preferred_element_type=jnp.float32)
        * scale_qk
    )
    grad_keys = (
        jnp.einsum("shqk,sqhe->skhe", grad_scores, query_rows, preferred_element_type=jnp.float32)
        * scale_qk
    )
    grad_projected = jnp.concatenate(
        [
            grad_queries.reshape(row_total, model_width),
            grad_keys.reshape(row_total, model_width),
            grad_values.reshape(row_total, model_width),
        ],
        axis=1,
    ).astype(jnp.bfloat16)
    proj_sums = jnp.sum(grad_projected.astype(jnp.float32), axis=0)
    grad_inproj_bias = jnp.concatenate([proj_sums[:model_width], proj_sums[2 * model_width :]])
    first_gradient = matmul_back(grad_projected, wb_inproj).reshape(slots, seq_len, model_width)
    selfattn_scale_gradient = jnp.sum(first_gradient * normalized_first, axis=1)
    selfattn_offset_gradient = jnp.sum(first_gradient, axis=1)
    grad_patches = (
        between_gradient
        + normalize_reverse(
            normalized_first, inverse_deviation, first_gradient * (1.0 + selfattn_scale)
        )
    ).astype(jnp.bfloat16)
    grad_modulation = jnp.concatenate(
        [
            selfattn_offset_gradient,
            selfattn_scale_gradient,
            selfattn_gate_gradient,
            grad_shift_mlp,
            grad_scale_mlp,
            grad_gate_mlp,
        ],
        axis=1,
    ).astype(jnp.bfloat16)
    grad_ada_weight, grad_ada_bias, grad_cond_act, bias_shares = tail(
        grad_modulation,
        (grad_inproj_bias, grad_outproj_bias, grad_up_bias, grad_down_bias),
        gathered,
        ada_weight,
    )
    _, silu_pull = jax.vjp(jax.nn.silu, condition)
    grad_condition = silu_pull(grad_cond_act)[0]
    ff_width = activated.shape[1]
    input_factors = (
        (first_input, grad_projected, 0),
        (attended, residual_branch_gradient, 3 * model_width),
        (second_in, grad_hidden, 4 * model_width),
    )
    down_factors = ((activated, grad_mlp, 0),)
    input_block = (4 * model_width + ff_width) // 4
    down_block = model_width // 2
    block_jobs = [
        (input_factors, model_width, number * input_block, input_block) for number in range(4)
    ]
    block_jobs = block_jobs + [
        (down_factors, ff_width, number * down_block, down_block) for number in range(2)
    ]

    def reduce_block(factors, rows, first, width):
        return lax.psum_scatter(
            block_term(factors, lax.axis_size("wide") * (rows // wide_count), first, width).astype(
                jnp.bfloat16
            ),
            "wide",
            scatter_dimension=0,
            tiled=True,
        ).astype(jnp.float32)

    if lax.axis_size("narrow") == 2 and wide_count == 16:
        w_grads = weight_grads(
            first_input, attended, second_in, activated,
            grad_projected, residual_branch_gradient, grad_hidden, grad_mlp,
        )
    else:
        shards = [reduce_block(*job) for job in block_jobs]
        input_grads = jnp.concatenate(shards[:4], axis=1)
        w_grads = tuple(
            lax.psum(part.astype(jnp.bfloat16), "narrow").astype(jnp.float32)
            for part in (
                input_grads[:, : 3 * model_width],
                input_grads[:, 3 * model_width : 4 * model_width],
                input_grads[:, 4 * model_width :],
                jnp.concatenate(shards[4:], axis=1),
            )
        )
    return (
        output,
        grad_patches,
        grad_condition,
        grad_ada_weight,
        grad_ada_bias,
        w_grads[0],
        bias_shares[0],
        w_grads[1],
        bias_shares[1],
        w_grads[2],
        bias_shares[2],
        w_grads[3],
        bias_shares[3],
    )


def solution(mesh):
    in_specs = (
        P(("narrow", "wide"), None, None),
        P(("narrow", "wide"), None),
        P(("narrow", "wide")),
        P(None, "wide"),
        P("wide"),
        P("wide", None),
        P("wide"),
        P("wide", None),
        P("wide"),
        P("wide", None),
        P("wide"),
        P("wide", None),
        P("wide"),
        P(("narrow", "wide"), None, None),
    )
    out_specs = (
        P(("narrow", "wide"), None, None),
        P(("narrow", "wide"), None, None),
        P(("narrow", "wide"), None),
        P(None, "wide"),
        P("wide"),
        P("wide", None),
        P("wide"),
        P("wide", None),
        P("wide"),
        P("wide", None),
        P("wide"),
        P("wide", None),
        P("wide"),
    )
    return jax.shard_map(
        per_device, mesh=mesh, in_specs=in_specs, out_specs=out_specs, check_vma=False
    )
```

```python
from functools import partial

import jax
import jax.numpy as jnp
from jax import lax
from jax.sharding import PartitionSpec as P

from jax.experimental import pallas as pl
from jax.experimental.pallas import tpu as pltpu

HEADS = 16
MESH = pl.DeviceIdType.MESH
DEPTH = 4


norm_eps = 1e-06


def normalize(values):
    center = jnp.mean(values, axis=-1, keepdims=True)
    shifted = values - center
    inv_std = lax.rsqrt(jnp.mean(shifted * shifted, axis=-1, keepdims=True) + norm_eps)
    return (shifted * inv_std, inv_std)


def normalize_reverse(normed, inv_std, grad_normed):
    mean_grad = jnp.mean(grad_normed, axis=-1, keepdims=True)
    mean_proj = jnp.mean(grad_normed * normed, axis=-1, keepdims=True)
    return inv_std * (grad_normed - mean_grad - normed * mean_proj)


def matmul_rows(left, right):
    return jnp.dot(left, right, preferred_element_type=jnp.float32)


def matmul_back(left, right):
    return lax.dot_general(
        left, right, (((1,), (1,)), ((), ())), preferred_element_type=jnp.float32
    )


def matmul_outer(left, right):
    return lax.dot_general(
        left, right, (((0,), (0,)), ((), ())), preferred_element_type=jnp.float32
    )


def block_term(factors, count, first, width):
    pieces = []
    for left, right, base in factors:
        lower = max(first, base)
        upper = min(first + width, base + right.shape[1])
        if lower < upper:
            rows_part = lax.slice_in_dim(left, 0, count, axis=1)
            pieces.append(matmul_outer(rows_part, right[:, lower - base : upper - base]))
    return jnp.concatenate(pieces, axis=1)

LANES = 384
PER_HALF = 18


def reduce_kernel(
    at_ref, b_ref, out_ref,
    bbuf, gbuf, sbuf, tbuf, ubuf, fbuf, core_in, one_in, two_in, z_in, far_in,
    bsem, core_sem, one_sem, two_sem, zs_sem, zr_sem, far_sem,
):
    narrow = lax.axis_index("narrow")
    wide = lax.axis_index("wide")
    core = wide % 2
    row = (wide // 2) % 2
    deep = wide // 4
    core_peer = (narrow, wide + 1 - 2 * core)
    x_peer = (1 - narrow, wide)
    y_peer = (narrow, wide + 2 - 4 * row)
    z_to = [(narrow, (deep + o) % 4 * 4 + wide % 4) for o in (1, 2, 3)]

    barrier = pltpu.get_barrier_semaphore()
    for peer in [core_peer, x_peer, y_peer] + z_to:
        pl.semaphore_signal(barrier, inc=1, device_id=peer, device_id_type=MESH)
    pl.semaphore_wait(barrier, 6)

    def fetch(chunk, half):
        number = chunk + half * PER_HALF
        column = number - 3 * ((number - 24) // 3) * (number // 24)
        column = pl.multiple_of(column * LANES, LANES)
        return pltpu.make_async_copy(
            b_ref.at[:, pl.ds(column, LANES)], bbuf.at[half], bsem.at[half]
        )

    def send(src, dst, sems, chunk, peer):
        return pltpu.make_async_remote_copy(
            src_ref=src, dst_ref=dst, send_sem=sems.at[0, chunk], recv_sem=sems.at[1, chunk],
            device_id=peer, device_id_type=MESH,
        )

    def core_copy(chunk):
        return send(gbuf.at[1 - core], core_in.at[chunk], core_sem, chunk, core_peer)

    def one_copy(chunk, even):
        slot = chunk % DEPTH
        if even:
            return send(sbuf.at[slot, 1 - narrow], one_in.at[chunk], one_sem, chunk, x_peer)
        return send(sbuf.at[slot, 1 - row], one_in.at[chunk], one_sem, chunk, y_peer)

    def two_copy(chunk, even):
        slot = chunk % DEPTH
        if even:
            return send(tbuf.at[slot, 1 - row], two_in.at[chunk], two_sem, chunk, y_peer)
        return send(tbuf.at[slot, 1 - narrow], two_in.at[chunk], two_sem, chunk, x_peer)

    def z_copies(chunk):
        slot = chunk % DEPTH
        return [
            pltpu.make_async_remote_copy(
                src_ref=ubuf.at[slot, (deep + o) % 4], dst_ref=z_in.at[chunk, o - 1],
                send_sem=zs_sem.at[chunk, o - 1], recv_sem=zr_sem.at[chunk, o - 1],
                device_id=z_to[o - 1], device_id_type=MESH,
            )
            for o in (1, 2, 3)
        ]

    def far_copy(chunk):
        return send(fbuf.at[chunk], far_in.at[chunk], far_sem, chunk, x_peer)

    def add(left, right):
        return left.astype(jnp.float32) + right.astype(jnp.float32)

    def make(chunk):
        for half in range(2):
            number = chunk + half * PER_HALF
            which = (
                jnp.where(number >= 9, 1, 0) + jnp.where(number >= 12, 1, 0)
                + jnp.where(number >= 24, 1, 0) + jnp.where(number >= 27, 1, 0)
                + jnp.where(number >= 30, 1, 0) + jnp.where(number >= 33, 1, 0)
            )
            fetch(chunk, half).wait()
            for side in range(2):
                product = jnp.dot(
                    at_ref[which, side], bbuf[half], preferred_element_type=jnp.float32
                )
                for unit in range(8):
                    gbuf[side, half, unit] = product[unit * 72 : unit * 72 + 72].astype(jnp.bfloat16)

            @pl.when(chunk + 1 < PER_HALF)
            def _():
                fetch(chunk + 1, half).start()

        core_copy(chunk).start()

    def pair(chunk, even):
        core_copy(chunk).wait()
        slot = chunk % DEPTH

        def body(step, carry):
            half, unit = step // 8, step % 8
            value = add(gbuf[core, half, unit], core_in[chunk, half, unit]).astype(jnp.bfloat16)
            deep_at, row_at = unit // 2, unit % 2
            if even:
                sbuf[slot, half, row_at, deep_at] = value
            else:
                sbuf[slot, row_at, half, deep_at] = value
            return carry

        lax.fori_loop(0, 16, body, 0)
        one_copy(chunk, even).start()

    def first(chunk, even):
        one_copy(chunk, even).wait()
        slot = chunk % DEPTH
        mine = narrow if even else row

        def body(step, carry):
            outer, inner = step // 4, step % 4
            tbuf[slot, outer, inner] = add(
                sbuf[slot, mine, outer, inner], one_in[chunk, outer, inner]
            ).astype(jnp.bfloat16)
            return carry

        lax.fori_loop(0, 8, body, 0)
        two_copy(chunk, even).start()

    def second(chunk, even):
        two_copy(chunk, even).wait()
        slot = chunk % DEPTH
        mine = row if even else narrow

        def body(step, carry):
            ubuf[slot, step] = add(tbuf[slot, mine, step], two_in[chunk, step]).astype(jnp.bfloat16)
            return carry

        lax.fori_loop(0, 4, body, 0)
        for copy in z_copies(chunk):
            copy.start()

    def third(chunk):
        for copy in z_copies(chunk):
            copy.wait()
        total = add(ubuf[chunk % DEPTH, deep], z_in[chunk, 0])
        total = total + add(z_in[chunk, 1], z_in[chunk, 2])
        out_ref[narrow * PER_HALF + chunk] = total
        fbuf[chunk] = total.astype(jnp.bfloat16)
        far_copy(chunk).start()

    for half in range(2):
        fetch(0, half).start()

    def turn(step, carry):
        for parity in range(2):
            now = step * 2 + parity
            for lag, action, fixed in (
                (1 + 3 * DEPTH, third, False),
                (1 + 2 * DEPTH, second, True),
                (1 + DEPTH, first, True),
                (1, pair, True),
                (0, make, False),
            ):
                chunk = now - lag
                even = (parity - lag) % 2 == 0

                @pl.when(jnp.logical_and(chunk >= 0, chunk < PER_HALF))
                def _(action=action, fixed=fixed, chunk=chunk, even=even):
                    action(chunk, even) if fixed else action(chunk)

        return carry

    lax.fori_loop(0, (PER_HALF + 3 * DEPTH + 2) // 2, turn, 0)

    def finish(chunk, carry):
        far_copy(chunk).wait()
        out_ref[(1 - narrow) * PER_HALF + chunk] = far_in[chunk].astype(jnp.float32)
        return carry

    lax.fori_loop(0, PER_HALF, finish, 0)


def reduce_weights(transposed, right):
    bf = jnp.bfloat16
    dma = pltpu.SemaphoreType.DMA
    unit = (72, LANES)
    n = PER_HALF
    return pl.pallas_call(
        reduce_kernel,
        out_shape=jax.ShapeDtypeStruct((2 * n,) + unit, jnp.float32),
        in_specs=[
            pl.BlockSpec(memory_space=pltpu.VMEM),
            pl.BlockSpec(memory_space=pl.ANY),
        ],
        out_specs=pl.BlockSpec(memory_space=pltpu.VMEM),
        scratch_shapes=[
            pltpu.VMEM((2, 512, LANES), bf),
            pltpu.VMEM((2, 2, 8) + unit, bf),
            pltpu.VMEM((DEPTH, 2, 2, 4) + unit, bf),
            pltpu.VMEM((DEPTH, 2, 4) + unit, bf),
            pltpu.VMEM((DEPTH, 4) + unit, bf),
            pltpu.VMEM((n,) + unit, bf),
            pltpu.VMEM((n, 2, 8) + unit, bf),
            pltpu.VMEM((n, 2, 4) + unit, bf),
            pltpu.VMEM((n, 4) + unit, bf),
            pltpu.VMEM((n, 3) + unit, bf),
            pltpu.VMEM((n,) + unit, bf),
            dma((2,)),
            dma((2, n)),
            dma((2, n)),
            dma((2, n)),
            dma((n, 3)),
            dma((n, 3)),
            dma((2, n)),
        ],
        compiler_params=pltpu.CompilerParams(
            collective_id=1, has_side_effects=True, vmem_limit_bytes=66_000_000
        ),
        name="reduce_weights",
    )(transposed, right)


def by_holder(left, parts):
    tokens = left.shape[0]
    rows = left.T.reshape(8, 2, parts, 72, tokens)
    return rows.transpose(2, 1, 0, 3, 4).reshape(parts, 2, 576, tokens)


def weight_grads(first_input, attended, second_in, activated, grad_projected, grad_branch, grad_hidden, grad_mlp):
    transposed = jnp.concatenate(
        [by_holder(first_input, 1), by_holder(attended, 1), by_holder(second_in, 1), by_holder(activated, 4)]
    )
    right = jnp.concatenate([grad_projected, grad_branch, grad_hidden, grad_mlp], axis=1)
    done = reduce_weights(transposed, right)

    def flat(lower, upper):
        return done[lower:upper].transpose(1, 0, 2).reshape(72, (upper - lower) * LANES)

    down = done[24:].reshape(4, 3, 72, LANES).transpose(0, 2, 1, 3).reshape(288, 3 * LANES)
    return flat(0, 9), flat(9, 12), flat(12, 24), down


def place(index, wide_count):
    return (index // wide_count, index % wide_count)


def meet(total, me, wide_count):
    barrier = pltpu.get_barrier_semaphore()

    def greet(step, carry):
        pl.semaphore_signal(
            barrier, inc=1, device_id=place((me + step) % total, wide_count), device_id_type=MESH
        )
        return carry

    lax.fori_loop(1, total, greet, 0)
    pl.semaphore_wait(barrier, total - 1)


def exchange(step, source, landing, send_sems, recv_sems, peer):
    return pltpu.make_async_remote_copy(
        src_ref=source, dst_ref=landing, send_sem=send_sems.at[step], recv_sem=recv_sems.at[step],
        device_id=peer, device_id_type=MESH,
    )


def loop(count, action):
    def body(step, carry):
        action(step)
        return carry

    lax.fori_loop(1, count, body, 0)


def gather_steps(shard_ref, full_ref, own_sem, zs_sem, zr_sem, one_sem, two_sem, core_sem):
    narrow, wide = lax.axis_index("narrow"), lax.axis_index("wide")
    core, row, deep = wide % 2, (wide // 2) % 2, wide // 4
    core_peer = (narrow, wide + 1 - 2 * core)
    x_peer = (1 - narrow, wide)
    y_peer = (narrow, wide + 2 - 4 * row)
    chunks = shard_ref.shape[1] // (2 * LANES)

    def span(chunk, half):
        return pl.ds(pl.multiple_of((chunk + half * chunks) * LANES, LANES), LANES)

    def send(view, sems, chunk, number, peer):
        return pltpu.make_async_remote_copy(
            src_ref=view, dst_ref=view, send_sem=sems.at[0, chunk, number],
            recv_sem=sems.at[1, chunk, number], device_id=peer, device_id_type=MESH,
        )

    def own(chunk):
        return pltpu.make_async_copy(
            shard_ref.at[:, span(chunk, narrow)],
            full_ref.at[deep, row, core, :, span(chunk, narrow)],
            own_sem.at[chunk],
        )

    def along_z(chunk):
        return [
            pltpu.make_async_remote_copy(
                src_ref=shard_ref.at[:, span(chunk, narrow)],
                dst_ref=full_ref.at[deep, row, core, :, span(chunk, narrow)],
                send_sem=zs_sem.at[chunk, o - 1], recv_sem=zr_sem.at[chunk, o - 1],
                device_id=(narrow, (deep + o) % 4 * 4 + wide % 4), device_id_type=MESH,
            )
            for o in (1, 2, 3)
        ]

    def one(chunk):
        view = full_ref.at[:, row, core, :, span(chunk, narrow)]
        return [send(view, one_sem, chunk, 0, x_peer if chunk % 2 else y_peer)]

    def two(chunk):
        if chunk % 2:
            return [
                send(full_ref.at[:, row, core, :, span(chunk, half)], two_sem, chunk, half, y_peer)
                for half in range(2)
            ]
        return [
            send(full_ref.at[:, side, core, :, span(chunk, narrow)], two_sem, chunk, side, x_peer)
            for side in range(2)
        ]

    def across(chunk):
        return [
            send(full_ref.at[:, :, core, :, span(chunk, half)], core_sem, chunk, half, core_peer)
            for half in range(2)
        ]

    def begin():
        for chunk in range(chunks):
            own(chunk).start()
            for copy in along_z(chunk):
                copy.start()

    def run():
        stages = (lambda chunk: [own(chunk)] + along_z(chunk), one, two, across)
        for turn in range(chunks + 4):
            for stage in (2, 1, 0):
                chunk = turn - 2 * stage
                if 0 <= chunk < chunks:
                    for copy in stages[stage](chunk):
                        copy.wait()
                    for copy in stages[stage + 1](chunk):
                        copy.start()
        for chunk in range(chunks):
            for copy in across(chunk):
                copy.wait()

    return begin, run


def front_kernel(narrow_count, wide_count, with_weights, *refs):
    if with_weights:
        pack_ref, weight_ref, bias_ref, shard_ref, all_ref, mod_ref, full_ref = refs[:7]
        part, send_sem, recv_sem, send_two, recv_two = refs[7:12]
        begin, run = gather_steps(shard_ref, full_ref, *refs[12:])
    else:
        pack_ref, weight_ref, bias_ref, all_ref, mod_ref = refs[:5]
        part, send_sem, recv_sem, send_two, recv_two = refs[5:]
    total = narrow_count * wide_count
    narrow, wide = lax.axis_index("narrow"), lax.axis_index("wide")
    me = narrow * wide_count + wide
    base = narrow * wide_count
    meet(total, me, wide_count)

    def spread(step):
        return exchange(
            step, pack_ref, all_ref.at[me], send_sem, recv_sem, place((me + step) % total, wide_count)
        )

    loop(total, lambda step: spread(step).start())
    if with_weights:
        begin()
    all_ref[me] = pack_ref[...]
    loop(total, lambda step: spread(step).wait())
    rows = all_ref[pl.ds(base, wide_count)].astype(jnp.float32)
    rows = rows.reshape(wide_count * 8, rows.shape[2]).astype(jnp.bfloat16)
    product = jnp.dot(rows, weight_ref[...], preferred_element_type=jnp.float32)
    product = product + bias_ref[...].astype(jnp.float32)
    part[...] = product.reshape(part.shape).astype(jnp.bfloat16)

    def deal(step):
        to = (wide + step) % wide_count
        return exchange(step, part.at[to], mod_ref.at[wide], send_two, recv_two, (narrow, to))

    loop(wide_count, lambda step: deal(step).start())
    mod_ref[wide] = part[wide]
    if with_weights:
        run()
    loop(wide_count, lambda step: deal(step).wait())


def tail_kernel(
    narrow_count, wide_count, gift_ref, all_ref, weight_ref, ada_ref, misc_ref, cond_ref,
    gifts, part, shares, send_sem, recv_sem, send_two, recv_two,
):
    total = narrow_count * wide_count
    narrow, wide = lax.axis_index("narrow"), lax.axis_index("wide")
    me = narrow * wide_count + wide
    base = narrow * wide_count
    meet(total, me, wide_count)

    def spread(step):
        to = (me + step) % total
        return exchange(
            step, gift_ref.at[to % wide_count], gifts.at[me], send_sem, recv_sem, place(to, wide_count)
        )

    loop(total, lambda step: spread(step).start())
    gifts[me] = gift_ref[wide]
    loop(total, lambda step: spread(step).wait())
    mine = gifts[pl.ds(base, wide_count)].astype(jnp.float32)
    mine = mine.reshape(wide_count * 8, mine.shape[2]).astype(jnp.bfloat16)
    share = matmul_back(mine, weight_ref[...])
    part[...] = share.reshape(part.shape).astype(jnp.bfloat16)

    def deal(step):
        to = (wide + step) % wide_count
        return exchange(step, part.at[to], shares.at[wide], send_two, recv_two, (narrow, to))

    loop(wide_count, lambda step: deal(step).start())
    shares[wide] = part[wide]
    every = gifts[...].astype(jnp.float32)
    misc_ref[...] = jnp.sum(every, axis=0)
    grads = every.reshape(total * 8, every.shape[2]).astype(jnp.bfloat16)
    conds = all_ref[...].astype(jnp.float32)
    conds = conds.reshape(total * 8, conds.shape[2]).astype(jnp.bfloat16)
    ada_ref[...] = matmul_outer(conds, grads)
    loop(wide_count, lambda step: deal(step).wait())
    cond_ref[...] = jnp.sum(shares[...].astype(jnp.float32), axis=0)


def in_vmem(count):
    return [pl.BlockSpec(memory_space=pltpu.VMEM)] * count


def dmas(*counts):
    return [pltpu.SemaphoreType.DMA((count,)) for count in counts]


def front(cond_act, biases, ada_weight, ada_bias, shards):
    narrow_count, wide_count = lax.axis_size("narrow"), lax.axis_size("wide")
    total = narrow_count * wide_count
    slots, model_width = cond_act.shape
    columns = ada_weight.shape[1]
    bias_row = jnp.concatenate(biases)
    bias_row = jnp.pad(bias_row, (0, model_width - bias_row.shape[0]))[None]
    pack = jnp.concatenate(
        [cond_act, bias_row, jnp.zeros((7 - slots, model_width), jnp.bfloat16)]
    )
    with_weights = narrow_count == 2 and wide_count == 16
    operands = [pack, ada_weight, ada_bias[None]]
    shapes = [
        jax.ShapeDtypeStruct((total, 8, model_width), jnp.bfloat16),
        jax.ShapeDtypeStruct((wide_count, 8, columns), jnp.bfloat16),
    ]
    out_specs = in_vmem(2)
    scratch = [pltpu.VMEM((wide_count, 8, columns), jnp.bfloat16)]
    scratch += dmas(total, total, wide_count, wide_count)
    if with_weights:
        shard = jnp.concatenate(shards, axis=1)
        operands.append(shard)
        shapes.append(jax.ShapeDtypeStruct((4, 2, 2) + shard.shape, jnp.bfloat16))
        out_specs.append(pl.BlockSpec(memory_space=pl.ANY))
        n = shard.shape[1] // (2 * LANES)
        for dims in ((n,), (n, 3), (n, 3), (2, n, 1), (2, n, 2), (2, n, 2)):
            scratch.append(pltpu.SemaphoreType.DMA(dims))
    results = pl.pallas_call(
        partial(front_kernel, narrow_count, wide_count, with_weights),
        out_shape=tuple(shapes),
        in_specs=in_vmem(len(operands)),
        out_specs=tuple(out_specs),
        scratch_shapes=scratch,
        compiler_params=pltpu.CompilerParams(collective_id=2, has_side_effects=True),
        name="front",
    )(*operands)
    if not with_weights:
        return tuple(results) + tuple(lax.all_gather(shard, "wide", axis=0, tiled=True) for shard in shards)
    full = results[2].reshape(wide_count * shard.shape[0], shard.shape[1])
    weights, at = [], 0
    for piece in shards:
        weights.append(full[:, at : at + piece.shape[1]])
        at += piece.shape[1]
    return tuple(results[:2]) + tuple(weights)


def tail(grad_modulation, bias_grads, gathered, ada_weight):
    narrow_count, wide_count = lax.axis_size("narrow"), lax.axis_size("wide")
    total = narrow_count * wide_count
    slots = grad_modulation.shape[0]
    model_width, columns = ada_weight.shape
    blocks = grad_modulation.reshape(slots, wide_count, columns).transpose(1, 0, 2)
    held = jnp.concatenate(
        [grad.reshape(wide_count, -1) for grad in bias_grads], axis=1
    ).astype(jnp.bfloat16)
    lines = -(-held.shape[1] // columns)
    held_rows = jnp.pad(held, ((0, 0), (0, lines * columns - held.shape[1])))
    held_rows = held_rows.reshape(wide_count, lines, columns)
    gap = jnp.zeros((wide_count, 4 - slots, columns), jnp.bfloat16)
    end = jnp.zeros((wide_count, 4 - lines, columns), jnp.bfloat16)
    gift = jnp.concatenate([blocks, gap, held_rows, end], axis=1)
    ada, misc, cond = pl.pallas_call(
        partial(tail_kernel, narrow_count, wide_count),
        out_shape=(
            jax.ShapeDtypeStruct((model_width, columns), jnp.float32),
            jax.ShapeDtypeStruct((8, columns), jnp.float32),
            jax.ShapeDtypeStruct((8, model_width), jnp.float32),
        ),
        in_specs=in_vmem(3),
        out_specs=tuple(in_vmem(3)),
        scratch_shapes=[
            pltpu.VMEM((total, 8, columns), jnp.bfloat16),
            pltpu.VMEM((wide_count, 8, model_width), jnp.bfloat16),
            pltpu.VMEM((wide_count, 8, model_width), jnp.bfloat16),
        ]
        + dmas(total, total, wide_count, wide_count),
        compiler_params=pltpu.CompilerParams(collective_id=3, has_side_effects=True),
        name="tail",
    )(gift, gathered, ada_weight)
    flat = misc[4:].reshape(-1)
    grads, at = [], 0
    for grad in bias_grads:
        width = grad.shape[0] // wide_count
        grads.append(flat[at : at + width])
        at += width
    return ada, misc[:slots].sum(axis=0), cond[:slots], grads


def head_parts(ref, head, width, count):
    at = head * width
    span = width * HEADS
    return [ref[0, :, number * span + at : number * span + at + width] for number in range(count)]


def attend_kernel(projected_ref, out_ref, lse_ref):
    width = out_ref.shape[2] // HEADS
    scale = width ** (-0.5)
    for head in range(HEADS):
        query, key, value = head_parts(projected_ref, head, width, 3)
        scores = matmul_back(query, key) * scale
        top = jnp.max(scores, axis=-1, keepdims=True)
        lse = top + jnp.log(jnp.sum(jnp.exp(scores - top), axis=-1, keepdims=True))
        probs = jnp.exp(scores - lse).astype(jnp.bfloat16)
        out_ref[0, :, head * width : head * width + width] = matmul_rows(probs, value).astype(
            jnp.bfloat16
        )
        lse_ref[0, :, head : head + 1] = lse


def attend_back_kernel(projected_ref, grad_ref, lse_ref, out_ref):
    model_width = grad_ref.shape[2]
    width = model_width // HEADS
    scale = width ** (-0.5)
    for head in range(HEADS):
        query, key, value = head_parts(projected_ref, head, width, 3)
        (grad,) = head_parts(grad_ref, head, width, 1)
        scores = matmul_back(query, key) * scale
        probs = jnp.exp(scores - lse_ref[0, :, head : head + 1])
        grad_value = matmul_outer(probs.astype(jnp.bfloat16), grad)
        grad_probs = matmul_back(grad, value)
        row_dot = jnp.sum(grad_probs * probs, axis=-1, keepdims=True)
        grad_scores = (probs * (grad_probs - row_dot)).astype(jnp.bfloat16)
        grad_query = matmul_rows(grad_scores, key) * scale
        grad_key = matmul_outer(grad_scores, query) * scale
        for number, part in enumerate((grad_query, grad_key, grad_value)):
            at = number * model_width + head * width
            out_ref[0, :, at : at + width] = part.astype(jnp.bfloat16)


def by_image(shape):
    return pl.BlockSpec((1,) + shape[1:], lambda image: (image, 0, 0))


def attend_call(kernel, operands, shapes, name):
    slots, seq_len = operands[0].shape[:2]
    work = slots * seq_len * seq_len
    return pl.pallas_call(
        kernel,
        grid=(slots,),
        out_shape=shapes,
        in_specs=[by_image(operand.shape) for operand in operands],
        out_specs=jax.tree.map(lambda shape: by_image(shape.shape), shapes),
        cost_estimate=pl.CostEstimate(
            flops=8 * work * operands[0].shape[2] // 3,
            bytes_accessed=sum(operand.size * 2 for operand in operands) * 2,
            transcendentals=work * HEADS,
        ),
        name=name,
    )(*operands)


def per_device(
    patches,
    condition,
    image_counts,
    ada_weight,
    ada_bias,
    inproj_weight,
    inproj_bias,
    outproj_weight,
    outproj_bias,
    up_weight,
    up_bias,
    down_weight,
    down_bias,
    cotangent,
):
    slots, seq_len, model_width = patches.shape
    row_total = slots * seq_len
    wide_count = lax.axis_size("wide")
    live = (jnp.arange(slots) < image_counts[0]).astype(jnp.float32)[:, None, None]
    cond_act = jax.nn.silu(condition).astype(jnp.bfloat16)
    gathered, mod_blocks, w_inproj, w_outproj, w_up = front(
        cond_act, (inproj_bias, outproj_bias, up_bias, down_bias), ada_weight, ada_bias,
        (inproj_weight, outproj_weight, up_weight),
    )
    down_weight, mod_blocks = lax.optimization_barrier((down_weight, mod_blocks))
    modulation = (
        mod_blocks[:, :slots].transpose(1, 0, 2).reshape(slots, 6 * model_width).astype(jnp.float32)
    )
    group = lax.dynamic_slice_in_dim(
        gathered[:, slots], lax.axis_index("narrow") * wide_count, wide_count
    )
    all_biases, bias_at = [], 0
    for bias in (inproj_bias, outproj_bias, up_bias, down_bias):
        all_biases.append(group[:, bias_at : bias_at + bias.shape[0]].reshape(-1))
        bias_at += bias.shape[0]
    b_inproj, b_outproj, b_up, b_down = all_biases
    segment_list = [
        modulation[:, None, number * model_width : (number + 1) * model_width]
        for number in range(6)
    ]
    (
        selfattn_offset,
        selfattn_scale,
        selfattn_gate,
        perceptron_offset,
        perceptron_scale,
        perceptron_gate,
    ) = segment_list
    w_down = lax.all_gather(down_weight, "wide", axis=0, tiled=True)
    input_rows = patches.astype(jnp.float32)
    normalized_first, inverse_deviation = normalize(input_rows)
    first_input = (
        (normalized_first * (1.0 + selfattn_scale) + selfattn_offset)
        .astype(jnp.bfloat16)
        .reshape(row_total, model_width)
    )
    proj_bias = b_inproj.astype(jnp.float32)
    full_bias = jnp.concatenate(
        [proj_bias[:model_width], jnp.zeros((model_width,), jnp.float32), proj_bias[model_width:]]
    )
    projected = (matmul_rows(first_input, w_inproj) + full_bias).astype(jnp.bfloat16)
    projected = projected.reshape(slots, seq_len, 3 * model_width)
    attended, log_total = attend_call(
        attend_kernel,
        (projected,),
        (
            jax.ShapeDtypeStruct((slots, seq_len, model_width), jnp.bfloat16),
            jax.ShapeDtypeStruct((slots, seq_len, HEADS), jnp.float32),
        ),
        "attend",
    )
    attended = attended.reshape(row_total, model_width)
    residual_branch = (matmul_rows(attended, w_outproj) + b_outproj.astype(jnp.float32)).reshape(
        slots, seq_len, model_width
    )
    between_state = input_rows + selfattn_gate * residual_branch
    normed_b, inv_b = normalize(between_state)
    second_in = (
        (normed_b * (1.0 + perceptron_scale) + perceptron_offset)
        .astype(jnp.bfloat16)
        .reshape(row_total, model_width)
    )
    hidden = matmul_rows(second_in, w_up) + b_up.astype(jnp.float32)
    gelu_value, gelu_pull = jax.vjp(partial(jax.nn.gelu, approximate=True), hidden)
    activated = gelu_value.astype(jnp.bfloat16)
    w_down, activated = lax.optimization_barrier((w_down, activated))
    mlp_out = (matmul_rows(activated, w_down) + b_down.astype(jnp.float32)).reshape(
        slots, seq_len, model_width
    )
    output = ((between_state + perceptron_gate * mlp_out) * live).astype(jnp.bfloat16)
    wb_inproj, wb_outproj, wb_up, wb_down = w_inproj, w_outproj, w_up, w_down
    grad_out = cotangent.astype(jnp.float32) * live
    grad_gate_mlp = jnp.sum(grad_out * mlp_out, axis=1)
    grad_mlp = (grad_out * perceptron_gate).astype(jnp.bfloat16).reshape(row_total, model_width)
    grad_down_bias = jnp.sum(grad_mlp.astype(jnp.float32), axis=0)
    grad_act = matmul_back(grad_mlp, wb_down)
    grad_hidden = gelu_pull(grad_act)[0].astype(jnp.bfloat16)
    grad_up_bias = jnp.sum(grad_hidden.astype(jnp.float32), axis=0)
    grad_second = matmul_back(grad_hidden, wb_up).reshape(slots, seq_len, model_width)
    grad_scale_mlp = jnp.sum(grad_second * normed_b, axis=1)
    grad_shift_mlp = jnp.sum(grad_second, axis=1)
    between_gradient = grad_out + normalize_reverse(
        normed_b, inv_b, grad_second * (1.0 + perceptron_scale)
    )
    selfattn_gate_gradient = jnp.sum(between_gradient * residual_branch, axis=1)
    residual_branch_gradient = (
        (between_gradient * selfattn_gate).astype(jnp.bfloat16).reshape(row_total, model_width)
    )
    grad_outproj_bias = jnp.sum(residual_branch_gradient.astype(jnp.float32), axis=0)
    grad_attended = (
        matmul_back(residual_branch_gradient, wb_outproj)
        .astype(jnp.bfloat16)
        .reshape(slots, seq_len, model_width)
    )
    grad_projected = attend_call(
        attend_back_kernel,
        (projected, grad_attended, log_total),
        jax.ShapeDtypeStruct((slots, seq_len, 3 * model_width), jnp.bfloat16),
        "attend_back",
    ).reshape(row_total, 3 * model_width)
    proj_sums = jnp.sum(grad_projected.astype(jnp.float32), axis=0)
    grad_inproj_bias = jnp.concatenate([proj_sums[:model_width], proj_sums[2 * model_width :]])
    first_gradient = matmul_back(grad_projected, wb_inproj).reshape(slots, seq_len, model_width)
    selfattn_scale_gradient = jnp.sum(first_gradient * normalized_first, axis=1)
    selfattn_offset_gradient = jnp.sum(first_gradient, axis=1)
    grad_patches = (
        between_gradient
        + normalize_reverse(
            normalized_first, inverse_deviation, first_gradient * (1.0 + selfattn_scale)
        )
    ).astype(jnp.bfloat16)
    grad_modulation = jnp.concatenate(
        [
            selfattn_offset_gradient,
            selfattn_scale_gradient,
            selfattn_gate_gradient,
            grad_shift_mlp,
            grad_scale_mlp,
            grad_gate_mlp,
        ],
        axis=1,
    ).astype(jnp.bfloat16)
    grad_ada_weight, grad_ada_bias, grad_cond_act, bias_shares = tail(
        grad_modulation,
        (grad_inproj_bias, grad_outproj_bias, grad_up_bias, grad_down_bias),
        gathered,
        ada_weight,
    )
    _, silu_pull = jax.vjp(jax.nn.silu, condition)
    grad_condition = silu_pull(grad_cond_act)[0]
    ff_width = activated.shape[1]
    input_factors = (
        (first_input, grad_projected, 0),
        (attended, residual_branch_gradient, 3 * model_width),
        (second_in, grad_hidden, 4 * model_width),
    )
    down_factors = ((activated, grad_mlp, 0),)
    input_block = (4 * model_width + ff_width) // 4
    down_block = model_width // 2
    block_jobs = [
        (input_factors, model_width, number * input_block, input_block) for number in range(4)
    ]
    block_jobs = block_jobs + [
        (down_factors, ff_width, number * down_block, down_block) for number in range(2)
    ]

    def reduce_block(factors, rows, first, width):
        return lax.psum_scatter(
            block_term(factors, lax.axis_size("wide") * (rows // wide_count), first, width).astype(
                jnp.bfloat16
            ),
            "wide",
            scatter_dimension=0,
            tiled=True,
        ).astype(jnp.float32)

    if lax.axis_size("narrow") == 2 and wide_count == 16:
        w_grads = weight_grads(
            first_input, attended, second_in, activated,
            grad_projected, residual_branch_gradient, grad_hidden, grad_mlp,
        )
    else:
        shards = [reduce_block(*job) for job in block_jobs]
        input_grads = jnp.concatenate(shards[:4], axis=1)
        w_grads = tuple(
            lax.psum(part.astype(jnp.bfloat16), "narrow").astype(jnp.float32)
            for part in (
                input_grads[:, : 3 * model_width],
                input_grads[:, 3 * model_width : 4 * model_width],
                input_grads[:, 4 * model_width :],
                jnp.concatenate(shards[4:], axis=1),
            )
        )
    return (
        output,
        grad_patches,
        grad_condition,
        grad_ada_weight,
        grad_ada_bias,
        w_grads[0],
        bias_shares[0],
        w_grads[1],
        bias_shares[1],
        w_grads[2],
        bias_shares[2],
        w_grads[3],
        bias_shares[3],
    )


def solution(mesh):
    in_specs = (
        P(("narrow", "wide"), None, None),
        P(("narrow", "wide"), None),
        P(("narrow", "wide")),
        P(None, "wide"),
        P("wide"),
        P("wide", None),
        P("wide"),
        P("wide", None),
        P("wide"),
        P("wide", None),
        P("wide"),
        P("wide", None),
        P("wide"),
        P(("narrow", "wide"), None, None),
    )
    out_specs = (
        P(("narrow", "wide"), None, None),
        P(("narrow", "wide"), None, None),
        P(("narrow", "wide"), None),
        P(None, "wide"),
        P("wide"),
        P("wide", None),
        P("wide"),
        P("wide", None),
        P("wide"),
        P("wide", None),
        P("wide"),
        P("wide", None),
        P("wide"),
    )
    return jax.shard_map(
        per_device, mesh=mesh, in_specs=in_specs, out_specs=out_specs, check_vma=False
    )
```

```python
from functools import partial

import jax
import jax.numpy as jnp
from jax import lax
from jax.sharding import PartitionSpec as P

from jax.experimental import pallas as pl
from jax.experimental.pallas import tpu as pltpu

HEADS = 16
MESH = pl.DeviceIdType.MESH
DEPTH = 4


norm_eps = 1e-06


def normalize(values):
    center = jnp.mean(values, axis=-1, keepdims=True)
    shifted = values - center
    inv_std = lax.rsqrt(jnp.mean(shifted * shifted, axis=-1, keepdims=True) + norm_eps)
    return (shifted * inv_std, inv_std)


def normalize_reverse(normed, inv_std, grad_normed):
    mean_grad = jnp.mean(grad_normed, axis=-1, keepdims=True)
    mean_proj = jnp.mean(grad_normed * normed, axis=-1, keepdims=True)
    return inv_std * (grad_normed - mean_grad - normed * mean_proj)


def matmul_rows(left, right):
    return jnp.dot(left, right, preferred_element_type=jnp.float32)


def matmul_back(left, right):
    return lax.dot_general(
        left, right, (((1,), (1,)), ((), ())), preferred_element_type=jnp.float32
    )


def matmul_outer(left, right):
    return lax.dot_general(
        left, right, (((0,), (0,)), ((), ())), preferred_element_type=jnp.float32
    )


def block_term(factors, count, first, width):
    pieces = []
    for left, right, base in factors:
        lower = max(first, base)
        upper = min(first + width, base + right.shape[1])
        if lower < upper:
            rows_part = lax.slice_in_dim(left, 0, count, axis=1)
            pieces.append(matmul_outer(rows_part, right[:, lower - base : upper - base]))
    return jnp.concatenate(pieces, axis=1)

LANES = 384
PER_HALF = 18


def reduce_kernel(
    a_in, a_out, a_up, a_down, b_in, b_out, b_up, b_down, out_ref,
    abuf, bbuf, gbuf, sbuf, tbuf, ubuf, fbuf, core_in, one_in, two_in, z_in, far_in,
    asem, bsem, core_sem, one_sem, two_sem, zs_sem, zr_sem, far_sem,
):
    narrow = lax.axis_index("narrow")
    wide = lax.axis_index("wide")
    core = wide % 2
    row = (wide // 2) % 2
    deep = wide // 4
    core_peer = (narrow, wide + 1 - 2 * core)
    x_peer = (1 - narrow, wide)
    y_peer = (narrow, wide + 2 - 4 * row)
    z_to = [(narrow, (deep + o) % 4 * 4 + wide % 4) for o in (1, 2, 3)]

    barrier = pltpu.get_barrier_semaphore()
    for peer in [core_peer, x_peer, y_peer] + z_to:
        pl.semaphore_signal(barrier, inc=1, device_id=peer, device_id_type=MESH)
    pl.semaphore_wait(barrier, 6)

    def copies(left, right, column, half):
        column = pl.multiple_of(column * LANES, LANES)
        return (
            pltpu.make_async_copy(left, abuf.at[half], asem.at[half]),
            pltpu.make_async_copy(right.at[:, pl.ds(column, LANES)], bbuf.at[half], bsem.at[half]),
        )

    def fetch(chunk, half):
        number = chunk + half * PER_HALF
        regions = ((0, 9, a_in, b_in), (9, 12, a_out, b_out), (12, 24, a_up, b_up))
        for lower, upper, left, right in regions:
            if half * PER_HALF < upper and lower < (half + 1) * PER_HALF:

                @pl.when(jnp.logical_and(number >= lower, number < upper))
                def _(lower=lower, left=left, right=right):
                    for copy in copies(left.at[0], right, number - lower, half):
                        copy.start()

        if half:

            @pl.when(number >= 24)
            def _():
                for copy in copies(a_down.at[(number - 24) // 3], b_down, (number - 24) % 3, half):
                    copy.start()

    def send(src, dst, sems, chunk, peer):
        return pltpu.make_async_remote_copy(
            src_ref=src, dst_ref=dst, send_sem=sems.at[0, chunk], recv_sem=sems.at[1, chunk],
            device_id=peer, device_id_type=MESH,
        )

    def core_copy(chunk):
        return send(gbuf.at[1 - core], core_in.at[chunk], core_sem, chunk, core_peer)

    def one_copy(chunk, even):
        slot = chunk % DEPTH
        if even:
            return send(sbuf.at[slot, 1 - narrow], one_in.at[chunk], one_sem, chunk, x_peer)
        return send(sbuf.at[slot, 1 - row], one_in.at[chunk], one_sem, chunk, y_peer)

    def two_copy(chunk, even):
        slot = chunk % DEPTH
        if even:
            return send(tbuf.at[slot, 1 - row], two_in.at[chunk], two_sem, chunk, y_peer)
        return send(tbuf.at[slot, 1 - narrow], two_in.at[chunk], two_sem, chunk, x_peer)

    def z_copies(chunk):
        slot = chunk % DEPTH
        return [
            pltpu.make_async_remote_copy(
                src_ref=ubuf.at[slot, (deep + o) % 4], dst_ref=z_in.at[chunk, o - 1],
                send_sem=zs_sem.at[chunk, o - 1], recv_sem=zr_sem.at[chunk, o - 1],
                device_id=z_to[o - 1], device_id_type=MESH,
            )
            for o in (1, 2, 3)
        ]

    def far_copy(chunk):
        return send(fbuf.at[chunk], far_in.at[chunk], far_sem, chunk, x_peer)

    def add(left, right):
        return left.astype(jnp.float32) + right.astype(jnp.float32)

    def make(chunk):
        for half in range(2):
            for copy in copies(a_in.at[0], b_in, 0, half):
                copy.wait()
            for side in range(2):
                product = jnp.dot(
                    abuf[half, side], bbuf[half], preferred_element_type=jnp.float32
                )
                for unit in range(8):
                    gbuf[side, half, unit] = product[unit * 72 : unit * 72 + 72].astype(jnp.bfloat16)

            @pl.when(chunk + 1 < PER_HALF)
            def _():
                fetch(chunk + 1, half)

        core_copy(chunk).start()

    def pair(chunk, even):
        core_copy(chunk).wait()
        slot = chunk % DEPTH

        def body(step, carry):
            half, unit = step // 8, step % 8
            value = add(gbuf[core, half, unit], core_in[chunk, half, unit]).astype(jnp.bfloat16)
            deep_at, row_at = unit // 2, unit % 2
            if even:
                sbuf[slot, half, row_at, deep_at] = value
            else:
                sbuf[slot, row_at, half, deep_at] = value
            return carry

        lax.fori_loop(0, 16, body, 0)
        one_copy(chunk, even).start()

    def first(chunk, even):
        one_copy(chunk, even).wait()
        slot = chunk % DEPTH
        mine = narrow if even else row

        def body(step, carry):
            outer, inner = step // 4, step % 4
            tbuf[slot, outer, inner] = add(
                sbuf[slot, mine, outer, inner], one_in[chunk, outer, inner]
            ).astype(jnp.bfloat16)
            return carry

        lax.fori_loop(0, 8, body, 0)
        two_copy(chunk, even).start()

    def second(chunk, even):
        two_copy(chunk, even).wait()
        slot = chunk % DEPTH
        mine = row if even else narrow

        def body(step, carry):
            ubuf[slot, step] = add(tbuf[slot, mine, step], two_in[chunk, step]).astype(jnp.bfloat16)
            return carry

        lax.fori_loop(0, 4, body, 0)
        for copy in z_copies(chunk):
            copy.start()

    def third(chunk):
        for copy in z_copies(chunk):
            copy.wait()
        total = add(ubuf[chunk % DEPTH, deep], z_in[chunk, 0])
        total = total + add(z_in[chunk, 1], z_in[chunk, 2])
        out_ref[narrow * PER_HALF + chunk] = total
        fbuf[chunk] = total.astype(jnp.bfloat16)
        far_copy(chunk).start()

    for half in range(2):
        fetch(0, half)

    def turn(step, carry):
        for parity in range(2):
            now = step * 2 + parity
            for lag, action, fixed in (
                (1 + 3 * DEPTH, third, False),
                (1 + 2 * DEPTH, second, True),
                (1 + DEPTH, first, True),
                (1, pair, True),
                (0, make, False),
            ):
                chunk = now - lag
                even = (parity - lag) % 2 == 0

                @pl.when(jnp.logical_and(chunk >= 0, chunk < PER_HALF))
                def _(action=action, fixed=fixed, chunk=chunk, even=even):
                    action(chunk, even) if fixed else action(chunk)

        return carry

    lax.fori_loop(0, (PER_HALF + 3 * DEPTH + 2) // 2, turn, 0)

    def finish(chunk, carry):
        far_copy(chunk).wait()
        out_ref[(1 - narrow) * PER_HALF + chunk] = far_in[chunk].astype(jnp.float32)
        return carry

    lax.fori_loop(0, PER_HALF, finish, 0)


def reduce_weights(*operands):
    bf = jnp.bfloat16
    dma = pltpu.SemaphoreType.DMA
    unit = (72, LANES)
    n = PER_HALF
    return pl.pallas_call(
        reduce_kernel,
        out_shape=jax.ShapeDtypeStruct((2 * n,) + unit, jnp.float32),
        in_specs=[pl.BlockSpec(memory_space=pl.ANY)] * 8,
        out_specs=pl.BlockSpec(memory_space=pltpu.VMEM),
        scratch_shapes=[
            pltpu.VMEM((2,) + operands[0].shape[1:], bf),
            pltpu.VMEM((2, operands[4].shape[0], LANES), bf),
            pltpu.VMEM((2, 2, 8) + unit, bf),
            pltpu.VMEM((DEPTH, 2, 2, 4) + unit, bf),
            pltpu.VMEM((DEPTH, 2, 4) + unit, bf),
            pltpu.VMEM((DEPTH, 4) + unit, bf),
            pltpu.VMEM((n,) + unit, bf),
            pltpu.VMEM((n, 2, 8) + unit, bf),
            pltpu.VMEM((n, 2, 4) + unit, bf),
            pltpu.VMEM((n, 4) + unit, bf),
            pltpu.VMEM((n, 3) + unit, bf),
            pltpu.VMEM((n,) + unit, bf),
            dma((2,)),
            dma((2,)),
            dma((2, n)),
            dma((2, n)),
            dma((2, n)),
            dma((n, 3)),
            dma((n, 3)),
            dma((2, n)),
        ],
        compiler_params=pltpu.CompilerParams(
            collective_id=1, has_side_effects=True, vmem_limit_bytes=66_000_000
        ),
        name="reduce_weights",
    )(*operands)


def by_holder(left, parts):
    tokens = left.shape[0]
    rows = left.T.reshape(8, 2, parts, 72, tokens)
    return rows.transpose(2, 1, 0, 3, 4).reshape(parts, 2, 576, tokens)


def weight_grads(first_input, attended, second_in, activated, grad_projected, grad_branch, grad_hidden, grad_mlp):
    done = reduce_weights(
        by_holder(first_input, 1), by_holder(attended, 1), by_holder(second_in, 1),
        by_holder(activated, 4), grad_projected, grad_branch, grad_hidden, grad_mlp,
    )

    def flat(lower, upper):
        return done[lower:upper].transpose(1, 0, 2).reshape(72, (upper - lower) * LANES)

    down = done[24:].reshape(4, 3, 72, LANES).transpose(0, 2, 1, 3).reshape(288, 3 * LANES)
    return flat(0, 9), flat(9, 12), flat(12, 24), down


def place(index, wide_count):
    return (index // wide_count, index % wide_count)


def meet(total, me, wide_count):
    barrier = pltpu.get_barrier_semaphore()

    def greet(step, carry):
        pl.semaphore_signal(
            barrier, inc=1, device_id=place((me + step) % total, wide_count), device_id_type=MESH
        )
        return carry

    lax.fori_loop(1, total, greet, 0)
    pl.semaphore_wait(barrier, total - 1)


def exchange(step, source, landing, send_sems, recv_sems, peer):
    return pltpu.make_async_remote_copy(
        src_ref=source, dst_ref=landing, send_sem=send_sems.at[step], recv_sem=recv_sems.at[step],
        device_id=peer, device_id_type=MESH,
    )


def loop(count, action):
    def body(step, carry):
        action(step)
        return carry

    lax.fori_loop(1, count, body, 0)


def gather_steps(shard_ref, full_ref, own_sem, zs_sem, zr_sem, one_sem, two_sem, core_sem):
    narrow, wide = lax.axis_index("narrow"), lax.axis_index("wide")
    core, row, deep = wide % 2, (wide // 2) % 2, wide // 4
    core_peer = (narrow, wide + 1 - 2 * core)
    x_peer = (1 - narrow, wide)
    y_peer = (narrow, wide + 2 - 4 * row)
    chunks = shard_ref.shape[1] // (2 * LANES)

    def span(chunk, half):
        return pl.ds(pl.multiple_of((chunk + half * chunks) * LANES, LANES), LANES)

    def send(view, sems, chunk, number, peer):
        return pltpu.make_async_remote_copy(
            src_ref=view, dst_ref=view, send_sem=sems.at[0, chunk, number],
            recv_sem=sems.at[1, chunk, number], device_id=peer, device_id_type=MESH,
        )

    def own(chunk):
        return pltpu.make_async_copy(
            shard_ref.at[:, span(chunk, narrow)],
            full_ref.at[deep, row, core, :, span(chunk, narrow)],
            own_sem.at[chunk],
        )

    def along_z(chunk):
        return [
            pltpu.make_async_remote_copy(
                src_ref=shard_ref.at[:, span(chunk, narrow)],
                dst_ref=full_ref.at[deep, row, core, :, span(chunk, narrow)],
                send_sem=zs_sem.at[chunk, o - 1], recv_sem=zr_sem.at[chunk, o - 1],
                device_id=(narrow, (deep + o) % 4 * 4 + wide % 4), device_id_type=MESH,
            )
            for o in (1, 2, 3)
        ]

    def one(chunk):
        view = full_ref.at[:, row, core, :, span(chunk, narrow)]
        return [send(view, one_sem, chunk, 0, x_peer if chunk % 2 else y_peer)]

    def two(chunk):
        if chunk % 2:
            return [
                send(full_ref.at[:, row, core, :, span(chunk, half)], two_sem, chunk, half, y_peer)
                for half in range(2)
            ]
        return [
            send(full_ref.at[:, side, core, :, span(chunk, narrow)], two_sem, chunk, side, x_peer)
            for side in range(2)
        ]

    def across(chunk):
        return [
            send(full_ref.at[:, :, core, :, span(chunk, half)], core_sem, chunk, half, core_peer)
            for half in range(2)
        ]

    def begin():
        for chunk in range(chunks):
            own(chunk).start()
            for copy in along_z(chunk):
                copy.start()

    def run():
        stages = (lambda chunk: [own(chunk)] + along_z(chunk), one, two, across)
        for turn in range(chunks + 4):
            for stage in (2, 1, 0):
                chunk = turn - 2 * stage
                if 0 <= chunk < chunks:
                    for copy in stages[stage](chunk):
                        copy.wait()
                    for copy in stages[stage + 1](chunk):
                        copy.start()
        for chunk in range(chunks):
            for copy in across(chunk):
                copy.wait()

    return begin, run


def front_kernel(narrow_count, wide_count, with_weights, *refs):
    if with_weights:
        pack_ref, weight_ref, bias_ref, shard_ref, all_ref, mod_ref, full_ref = refs[:7]
        part, send_sem, recv_sem, send_two, recv_two = refs[7:12]
        begin, run = gather_steps(shard_ref, full_ref, *refs[12:])
    else:
        pack_ref, weight_ref, bias_ref, all_ref, mod_ref = refs[:5]
        part, send_sem, recv_sem, send_two, recv_two = refs[5:]
    total = narrow_count * wide_count
    narrow, wide = lax.axis_index("narrow"), lax.axis_index("wide")
    me = narrow * wide_count + wide
    base = narrow * wide_count
    meet(total, me, wide_count)

    def spread(step):
        return exchange(
            step, pack_ref, all_ref.at[me], send_sem, recv_sem, place((me + step) % total, wide_count)
        )

    loop(total, lambda step: spread(step).start())
    if with_weights:
        begin()
    all_ref[me] = pack_ref[...]
    loop(total, lambda step: spread(step).wait())
    rows = all_ref[pl.ds(base, wide_count)].astype(jnp.float32)
    rows = rows.reshape(wide_count * 8, rows.shape[2]).astype(jnp.bfloat16)
    product = jnp.dot(rows, weight_ref[...], preferred_element_type=jnp.float32)
    product = product + bias_ref[...].astype(jnp.float32)
    part[...] = product.reshape(part.shape).astype(jnp.bfloat16)

    def deal(step):
        to = (wide + step) % wide_count
        return exchange(step, part.at[to], mod_ref.at[wide], send_two, recv_two, (narrow, to))

    loop(wide_count, lambda step: deal(step).start())
    mod_ref[wide] = part[wide]
    if with_weights:
        run()
    loop(wide_count, lambda step: deal(step).wait())


def tail_kernel(narrow_count, wide_count, *refs):
    mod_refs, (in_ref, out_ref, up_ref, down_ref, all_ref, weight_ref) = refs[:6], refs[6:12]
    ada_ref, misc_ref, cond_ref, wide_mod, layout, gift_ref = refs[12:18]
    gifts, part, shares, send_sem, recv_sem, send_two, recv_two = refs[18:]
    total = narrow_count * wide_count
    narrow, wide = lax.axis_index("narrow"), lax.axis_index("wide")
    me = narrow * wide_count + wide
    base = narrow * wide_count
    slots, model_width = mod_refs[0].shape
    columns = layout.shape[2]
    for number, ref in enumerate(mod_refs):
        wide_mod[:slots, number * model_width : (number + 1) * model_width] = ref[...]
    layout[...] = jnp.zeros_like(layout)
    for holder in range(wide_count):
        layout[holder, :slots] = wide_mod[:slots, holder * columns : (holder + 1) * columns]
        span = 2 * model_width // wide_count
        at = holder * span
        at = at if at < model_width else at + model_width
        layout[holder, 4:5, :span] = in_ref[:, at : at + span]
        for row, ref in ((5, out_ref), (6, up_ref), (7, down_ref)):
            span = ref.shape[1] // wide_count
            layout[holder, row : row + 1, :span] = ref[:, holder * span : (holder + 1) * span]
    gift_ref[...] = layout[...].astype(jnp.bfloat16)
    meet(total, me, wide_count)

    def spread(step):
        to = (me + step) % total
        return exchange(
            step, gift_ref.at[to % wide_count], gifts.at[me], send_sem, recv_sem, place(to, wide_count)
        )

    loop(total, lambda step: spread(step).start())
    gifts[me] = gift_ref[wide]
    loop(total, lambda step: spread(step).wait())
    mine = gifts[pl.ds(base, wide_count)].astype(jnp.float32)
    mine = mine.reshape(wide_count * 8, mine.shape[2]).astype(jnp.bfloat16)
    share = matmul_back(mine, weight_ref[...])
    part[...] = share.reshape(part.shape).astype(jnp.bfloat16)

    def deal(step):
        to = (wide + step) % wide_count
        return exchange(step, part.at[to], shares.at[wide], send_two, recv_two, (narrow, to))

    loop(wide_count, lambda step: deal(step).start())
    shares[wide] = part[wide]
    every = gifts[...].astype(jnp.float32)
    misc_ref[...] = jnp.sum(every, axis=0)
    grads = every.reshape(total * 8, every.shape[2]).astype(jnp.bfloat16)
    conds = all_ref[...].astype(jnp.float32)
    conds = conds.reshape(total * 8, conds.shape[2]).astype(jnp.bfloat16)
    ada_ref[...] = matmul_outer(conds, grads)
    loop(wide_count, lambda step: deal(step).wait())
    cond_ref[...] = jnp.sum(shares[...].astype(jnp.float32), axis=0)


def in_vmem(count):
    return [pl.BlockSpec(memory_space=pltpu.VMEM)] * count


def dmas(*counts):
    return [pltpu.SemaphoreType.DMA((count,)) for count in counts]


def front(cond_act, biases, ada_weight, ada_bias, shards):
    narrow_count, wide_count = lax.axis_size("narrow"), lax.axis_size("wide")
    total = narrow_count * wide_count
    slots, model_width = cond_act.shape
    columns = ada_weight.shape[1]
    bias_row = jnp.concatenate(biases)
    bias_row = jnp.pad(bias_row, (0, model_width - bias_row.shape[0]))[None]
    pack = jnp.concatenate(
        [cond_act, bias_row, jnp.zeros((7 - slots, model_width), jnp.bfloat16)]
    )
    with_weights = narrow_count == 2 and wide_count == 16
    operands = [pack, ada_weight, ada_bias[None]]
    shapes = [
        jax.ShapeDtypeStruct((total, 8, model_width), jnp.bfloat16),
        jax.ShapeDtypeStruct((wide_count, 8, columns), jnp.bfloat16),
    ]
    out_specs = in_vmem(2)
    scratch = [pltpu.VMEM((wide_count, 8, columns), jnp.bfloat16)]
    scratch += dmas(total, total, wide_count, wide_count)
    if with_weights:
        shard = jnp.concatenate(shards, axis=1)
        operands.append(shard)
        shapes.append(jax.ShapeDtypeStruct((4, 2, 2) + shard.shape, jnp.bfloat16))
        out_specs.append(pl.BlockSpec(memory_space=pl.ANY))
        n = shard.shape[1] // (2 * LANES)
        for dims in ((n,), (n, 3), (n, 3), (2, n, 1), (2, n, 2), (2, n, 2)):
            scratch.append(pltpu.SemaphoreType.DMA(dims))
    results = pl.pallas_call(
        partial(front_kernel, narrow_count, wide_count, with_weights),
        out_shape=tuple(shapes),
        in_specs=in_vmem(len(operands)),
        out_specs=tuple(out_specs),
        scratch_shapes=scratch,
        compiler_params=pltpu.CompilerParams(collective_id=2, has_side_effects=True),
        name="front",
    )(*operands)
    if not with_weights:
        return tuple(results) + tuple(lax.all_gather(shard, "wide", axis=0, tiled=True) for shard in shards)
    full = results[2].reshape(wide_count * shard.shape[0], shard.shape[1])
    weights, at = [], 0
    for piece in shards:
        weights.append(full[:, at : at + piece.shape[1]])
        at += piece.shape[1]
    return tuple(results[:2]) + tuple(weights)


def tail(mod_grads, bias_sums, gathered, ada_weight):
    narrow_count, wide_count = lax.axis_size("narrow"), lax.axis_size("wide")
    total = narrow_count * wide_count
    slots = mod_grads[0].shape[0]
    model_width, columns = ada_weight.shape
    operands = list(mod_grads) + [sums[None] for sums in bias_sums] + [gathered, ada_weight]
    ada, misc, cond = pl.pallas_call(
        partial(tail_kernel, narrow_count, wide_count),
        out_shape=(
            jax.ShapeDtypeStruct((model_width, columns), jnp.float32),
            jax.ShapeDtypeStruct((8, columns), jnp.float32),
            jax.ShapeDtypeStruct((8, model_width), jnp.float32),
        ),
        in_specs=in_vmem(len(operands)),
        out_specs=tuple(in_vmem(3)),
        scratch_shapes=[
            pltpu.VMEM((8, 6 * model_width), jnp.float32),
            pltpu.VMEM((wide_count, 8, columns), jnp.float32),
            pltpu.VMEM((wide_count, 8, columns), jnp.bfloat16),
            pltpu.VMEM((total, 8, columns), jnp.bfloat16),
            pltpu.VMEM((wide_count, 8, model_width), jnp.bfloat16),
            pltpu.VMEM((wide_count, 8, model_width), jnp.bfloat16),
        ]
        + dmas(total, total, wide_count, wide_count),
        compiler_params=pltpu.CompilerParams(collective_id=3, has_side_effects=True),
        name="tail",
    )(*operands)
    spans = [2 * model_width // wide_count] + [sums.shape[0] // wide_count for sums in bias_sums[1:]]
    grads = [misc[4 + number, :span] for number, span in enumerate(spans)]
    return ada, misc[:slots].sum(axis=0), cond[:slots], grads


def head_parts(ref, head, width, count):
    at = head * width
    span = width * HEADS
    return [ref[0, :, number * span + at : number * span + at + width] for number in range(count)]


def attend_kernel(projected_ref, out_ref, lse_ref):
    width = out_ref.shape[2] // HEADS
    scale = width ** (-0.5)
    for head in range(HEADS):
        query, key, value = head_parts(projected_ref, head, width, 3)
        scores = matmul_back(query, key) * scale
        top = jnp.max(scores, axis=-1, keepdims=True)
        lse = top + jnp.log(jnp.sum(jnp.exp(scores - top), axis=-1, keepdims=True))
        probs = jnp.exp(scores - lse).astype(jnp.bfloat16)
        out_ref[0, :, head * width : head * width + width] = matmul_rows(probs, value).astype(
            jnp.bfloat16
        )
        lse_ref[0, :, head : head + 1] = lse


def attend_back_kernel(projected_ref, grad_ref, lse_ref, out_ref):
    model_width = grad_ref.shape[2]
    width = model_width // HEADS
    scale = width ** (-0.5)
    for head in range(HEADS):
        query, key, value = head_parts(projected_ref, head, width, 3)
        (grad,) = head_parts(grad_ref, head, width, 1)
        scores = matmul_back(query, key) * scale
        probs = jnp.exp(scores - lse_ref[0, :, head : head + 1])
        grad_value = matmul_outer(probs.astype(jnp.bfloat16), grad)
        grad_probs = matmul_back(grad, value)
        row_dot = jnp.sum(grad_probs * probs, axis=-1, keepdims=True)
        grad_scores = (probs * (grad_probs - row_dot)).astype(jnp.bfloat16)
        grad_query = matmul_rows(grad_scores, key) * scale
        grad_key = matmul_outer(grad_scores, query) * scale
        for number, part in enumerate((grad_query, grad_key, grad_value)):
            at = number * model_width + head * width
            out_ref[0, :, at : at + width] = part.astype(jnp.bfloat16)


def by_image(shape):
    return pl.BlockSpec((1,) + shape[1:], lambda image: (image, 0, 0))


def attend_call(kernel, operands, shapes, name):
    slots, seq_len = operands[0].shape[:2]
    work = slots * seq_len * seq_len
    return pl.pallas_call(
        kernel,
        grid=(slots,),
        out_shape=shapes,
        in_specs=[by_image(operand.shape) for operand in operands],
        out_specs=jax.tree.map(lambda shape: by_image(shape.shape), shapes),
        cost_estimate=pl.CostEstimate(
            flops=8 * work * operands[0].shape[2] // 3,
            bytes_accessed=sum(operand.size * 2 for operand in operands) * 2,
            transcendentals=work * HEADS,
        ),
        name=name,
    )(*operands)


def per_device(
    patches,
    condition,
    image_counts,
    ada_weight,
    ada_bias,
    inproj_weight,
    inproj_bias,
    outproj_weight,
    outproj_bias,
    up_weight,
    up_bias,
    down_weight,
    down_bias,
    cotangent,
):
    slots, seq_len, model_width = patches.shape
    row_total = slots * seq_len
    wide_count = lax.axis_size("wide")
    live = (jnp.arange(slots) < image_counts[0]).astype(jnp.float32)[:, None, None]
    cond_act = jax.nn.silu(condition).astype(jnp.bfloat16)
    gathered, mod_blocks, w_inproj, w_outproj, w_up = front(
        cond_act, (inproj_bias, outproj_bias, up_bias, down_bias), ada_weight, ada_bias,
        (inproj_weight, outproj_weight, up_weight),
    )
    down_weight, mod_blocks = lax.optimization_barrier((down_weight, mod_blocks))
    modulation = (
        mod_blocks[:, :slots].transpose(1, 0, 2).reshape(slots, 6 * model_width).astype(jnp.float32)
    )
    group = lax.dynamic_slice_in_dim(
        gathered[:, slots], lax.axis_index("narrow") * wide_count, wide_count
    )
    all_biases, bias_at = [], 0
    for bias in (inproj_bias, outproj_bias, up_bias, down_bias):
        all_biases.append(group[:, bias_at : bias_at + bias.shape[0]].reshape(-1))
        bias_at += bias.shape[0]
    b_inproj, b_outproj, b_up, b_down = all_biases
    segment_list = [
        modulation[:, None, number * model_width : (number + 1) * model_width]
        for number in range(6)
    ]
    (
        selfattn_offset,
        selfattn_scale,
        selfattn_gate,
        perceptron_offset,
        perceptron_scale,
        perceptron_gate,
    ) = segment_list
    w_down = lax.all_gather(down_weight, "wide", axis=0, tiled=True)
    input_rows = patches.astype(jnp.float32)
    normalized_first, inverse_deviation = normalize(input_rows)
    first_input = (
        (normalized_first * (1.0 + selfattn_scale) + selfattn_offset)
        .astype(jnp.bfloat16)
        .reshape(row_total, model_width)
    )
    proj_bias = b_inproj.astype(jnp.float32)
    full_bias = jnp.concatenate(
        [proj_bias[:model_width], jnp.zeros((model_width,), jnp.float32), proj_bias[model_width:]]
    )
    projected = (matmul_rows(first_input, w_inproj) + full_bias).astype(jnp.bfloat16)
    projected = projected.reshape(slots, seq_len, 3 * model_width)
    attended, log_total = attend_call(
        attend_kernel,
        (projected,),
        (
            jax.ShapeDtypeStruct((slots, seq_len, model_width), jnp.bfloat16),
            jax.ShapeDtypeStruct((slots, seq_len, HEADS), jnp.float32),
        ),
        "attend",
    )
    attended = attended.reshape(row_total, model_width)
    residual_branch = (matmul_rows(attended, w_outproj) + b_outproj.astype(jnp.float32)).reshape(
        slots, seq_len, model_width
    )
    between_state = input_rows + selfattn_gate * residual_branch
    normed_b, inv_b = normalize(between_state)
    second_in = (
        (normed_b * (1.0 + perceptron_scale) + perceptron_offset)
        .astype(jnp.bfloat16)
        .reshape(row_total, model_width)
    )
    hidden = matmul_rows(second_in, w_up) + b_up.astype(jnp.float32)
    gelu_value, gelu_pull = jax.vjp(partial(jax.nn.gelu, approximate=True), hidden)
    activated = gelu_value.astype(jnp.bfloat16)
    w_down, activated = lax.optimization_barrier((w_down, activated))
    mlp_out = (matmul_rows(activated, w_down) + b_down.astype(jnp.float32)).reshape(
        slots, seq_len, model_width
    )
    output = ((between_state + perceptron_gate * mlp_out) * live).astype(jnp.bfloat16)
    wb_inproj, wb_outproj, wb_up, wb_down = w_inproj, w_outproj, w_up, w_down
    grad_out = cotangent.astype(jnp.float32) * live
    grad_gate_mlp = jnp.sum(grad_out * mlp_out, axis=1)
    grad_mlp = (grad_out * perceptron_gate).astype(jnp.bfloat16).reshape(row_total, model_width)
    grad_down_bias = jnp.sum(grad_mlp.astype(jnp.float32), axis=0)
    grad_act = matmul_back(grad_mlp, wb_down)
    grad_hidden = gelu_pull(grad_act)[0].astype(jnp.bfloat16)
    grad_up_bias = jnp.sum(grad_hidden.astype(jnp.float32), axis=0)
    grad_second = matmul_back(grad_hidden, wb_up).reshape(slots, seq_len, model_width)
    grad_scale_mlp = jnp.sum(grad_second * normed_b, axis=1)
    grad_shift_mlp = jnp.sum(grad_second, axis=1)
    between_gradient = grad_out + normalize_reverse(
        normed_b, inv_b, grad_second * (1.0 + perceptron_scale)
    )
    selfattn_gate_gradient = jnp.sum(between_gradient * residual_branch, axis=1)
    residual_branch_gradient = (
        (between_gradient * selfattn_gate).astype(jnp.bfloat16).reshape(row_total, model_width)
    )
    grad_outproj_bias = jnp.sum(residual_branch_gradient.astype(jnp.float32), axis=0)
    grad_attended = (
        matmul_back(residual_branch_gradient, wb_outproj)
        .astype(jnp.bfloat16)
        .reshape(slots, seq_len, model_width)
    )
    grad_projected = attend_call(
        attend_back_kernel,
        (projected, grad_attended, log_total),
        jax.ShapeDtypeStruct((slots, seq_len, 3 * model_width), jnp.bfloat16),
        "attend_back",
    ).reshape(row_total, 3 * model_width)
    proj_sums = jnp.sum(grad_projected.astype(jnp.float32), axis=0)
    first_gradient = matmul_back(grad_projected, wb_inproj).reshape(slots, seq_len, model_width)
    selfattn_scale_gradient = jnp.sum(first_gradient * normalized_first, axis=1)
    selfattn_offset_gradient = jnp.sum(first_gradient, axis=1)
    grad_patches = (
        between_gradient
        + normalize_reverse(
            normalized_first, inverse_deviation, first_gradient * (1.0 + selfattn_scale)
        )
    ).astype(jnp.bfloat16)
    mod_grads = (
        selfattn_offset_gradient,
        selfattn_scale_gradient,
        selfattn_gate_gradient,
        grad_shift_mlp,
        grad_scale_mlp,
        grad_gate_mlp,
    )
    grad_ada_weight, grad_ada_bias, grad_cond_act, bias_shares = tail(
        mod_grads,
        (proj_sums, grad_outproj_bias, grad_up_bias, grad_down_bias),
        gathered,
        ada_weight,
    )
    _, silu_pull = jax.vjp(jax.nn.silu, condition)
    grad_condition = silu_pull(grad_cond_act)[0]
    ff_width = activated.shape[1]
    input_factors = (
        (first_input, grad_projected, 0),
        (attended, residual_branch_gradient, 3 * model_width),
        (second_in, grad_hidden, 4 * model_width),
    )
    down_factors = ((activated, grad_mlp, 0),)
    input_block = (4 * model_width + ff_width) // 4
    down_block = model_width // 2
    block_jobs = [
        (input_factors, model_width, number * input_block, input_block) for number in range(4)
    ]
    block_jobs = block_jobs + [
        (down_factors, ff_width, number * down_block, down_block) for number in range(2)
    ]

    def reduce_block(factors, rows, first, width):
        return lax.psum_scatter(
            block_term(factors, lax.axis_size("wide") * (rows // wide_count), first, width).astype(
                jnp.bfloat16
            ),
            "wide",
            scatter_dimension=0,
            tiled=True,
        ).astype(jnp.float32)

    if lax.axis_size("narrow") == 2 and wide_count == 16:
        w_grads = weight_grads(
            first_input, attended, second_in, activated,
            grad_projected, residual_branch_gradient, grad_hidden, grad_mlp,
        )
    else:
        shards = [reduce_block(*job) for job in block_jobs]
        input_grads = jnp.concatenate(shards[:4], axis=1)
        w_grads = tuple(
            lax.psum(part.astype(jnp.bfloat16), "narrow").astype(jnp.float32)
            for part in (
                input_grads[:, : 3 * model_width],
                input_grads[:, 3 * model_width : 4 * model_width],
                input_grads[:, 4 * model_width :],
                jnp.concatenate(shards[4:], axis=1),
            )
        )
    return (
        output,
        grad_patches,
        grad_condition,
        grad_ada_weight,
        grad_ada_bias,
        w_grads[0],
        bias_shares[0],
        w_grads[1],
        bias_shares[1],
        w_grads[2],
        bias_shares[2],
        w_grads[3],
        bias_shares[3],
    )


def solution(mesh):
    in_specs = (
        P(("narrow", "wide"), None, None),
        P(("narrow", "wide"), None),
        P(("narrow", "wide")),
        P(None, "wide"),
        P("wide"),
        P("wide", None),
        P("wide"),
        P("wide", None),
        P("wide"),
        P("wide", None),
        P("wide"),
        P("wide", None),
        P("wide"),
        P(("narrow", "wide"), None, None),
    )
    out_specs = (
        P(("narrow", "wide"), None, None),
        P(("narrow", "wide"), None, None),
        P(("narrow", "wide"), None),
        P(None, "wide"),
        P("wide"),
        P("wide", None),
        P("wide"),
        P("wide", None),
        P("wide"),
        P("wide", None),
        P("wide"),
        P("wide", None),
        P("wide"),
    )
    return jax.shard_map(
        per_device, mesh=mesh, in_specs=in_specs, out_specs=out_specs, check_vma=False
    )
```

```python
from functools import partial

import jax
import jax.numpy as jnp
from jax import lax
from jax.sharding import PartitionSpec as P

from jax.experimental import pallas as pl
from jax.experimental.pallas import tpu as pltpu

HEADS = 16
MESH = pl.DeviceIdType.MESH
DEPTH = 4


norm_eps = 1e-06


def normalize(values):
    center = jnp.mean(values, axis=-1, keepdims=True)
    shifted = values - center
    inv_std = lax.rsqrt(jnp.mean(shifted * shifted, axis=-1, keepdims=True) + norm_eps)
    return (shifted * inv_std, inv_std)


def normalize_reverse(normed, inv_std, grad_normed):
    mean_grad = jnp.mean(grad_normed, axis=-1, keepdims=True)
    mean_proj = jnp.mean(grad_normed * normed, axis=-1, keepdims=True)
    return inv_std * (grad_normed - mean_grad - normed * mean_proj)


def matmul_rows(left, right):
    return jnp.dot(left, right, preferred_element_type=jnp.float32)


def matmul_back(left, right):
    return lax.dot_general(
        left, right, (((1,), (1,)), ((), ())), preferred_element_type=jnp.float32
    )


def matmul_outer(left, right):
    return lax.dot_general(
        left, right, (((0,), (0,)), ((), ())), preferred_element_type=jnp.float32
    )


def block_term(factors, count, first, width):
    pieces = []
    for left, right, base in factors:
        lower = max(first, base)
        upper = min(first + width, base + right.shape[1])
        if lower < upper:
            rows_part = lax.slice_in_dim(left, 0, count, axis=1)
            pieces.append(matmul_outer(rows_part, right[:, lower - base : upper - base]))
    return jnp.concatenate(pieces, axis=1)

LANES = 384
PER_HALF = 18


def reduce_kernel(
    projected_ref, grad_ref, lse_ref, a_in, a_out, a_up, a_down, b_out, b_up, b_down, out_ref, b_in,
    abuf, bbuf, gbuf, sbuf, tbuf, ubuf, fbuf, core_in, one_in, two_in, z_in, far_in,
    asem, bsem, core_sem, one_sem, two_sem, zs_sem, zr_sem, far_sem,
):
    narrow = lax.axis_index("narrow")
    wide = lax.axis_index("wide")
    core = wide % 2
    row = (wide // 2) % 2
    deep = wide // 4
    core_peer = (narrow, wide + 1 - 2 * core)
    x_peer = (1 - narrow, wide)
    y_peer = (narrow, wide + 2 - 4 * row)
    z_to = [(narrow, (deep + o) % 4 * 4 + wide % 4) for o in (1, 2, 3)]

    barrier = pltpu.get_barrier_semaphore()
    for peer in [core_peer, x_peer, y_peer] + z_to:
        pl.semaphore_signal(barrier, inc=1, device_id=peer, device_id_type=MESH)
    pl.semaphore_wait(barrier, 6)

    def copies(left, right, column, half):
        column = pl.multiple_of(column * LANES, LANES)
        return (
            pltpu.make_async_copy(left, abuf.at[half], asem.at[half]),
            pltpu.make_async_copy(right.at[:, pl.ds(column, LANES)], bbuf.at[half], bsem.at[half]),
        )

    def fetch(chunk, half):
        if half:
            regions = ((0, 12, None, b_down, 0), (12, 18, a_in, b_in, 3))
        else:
            regions = ((0, 12, a_up, b_up, 0), (12, 15, a_out, b_out, 0), (15, 18, a_in, b_in, 0))
        for lower, upper, left, right, offset in regions:

            @pl.when(jnp.logical_and(chunk >= lower, chunk < upper))
            def _(lower=lower, left=left, right=right, offset=offset):
                if left is None:
                    pieces = copies(a_down.at[chunk // 3], right, chunk % 3, half)
                else:
                    pieces = copies(left.at[0], right, chunk - lower + offset, half)
                for copy in pieces:
                    copy.start()

    def send(src, dst, sems, chunk, peer):
        return pltpu.make_async_remote_copy(
            src_ref=src, dst_ref=dst, send_sem=sems.at[0, chunk], recv_sem=sems.at[1, chunk],
            device_id=peer, device_id_type=MESH,
        )

    def core_copy(chunk):
        return send(gbuf.at[1 - core], core_in.at[chunk], core_sem, chunk, core_peer)

    def one_copy(chunk, even):
        slot = chunk % DEPTH
        if even:
            return send(sbuf.at[slot, 1 - narrow], one_in.at[chunk], one_sem, chunk, x_peer)
        return send(sbuf.at[slot, 1 - row], one_in.at[chunk], one_sem, chunk, y_peer)

    def two_copy(chunk, even):
        slot = chunk % DEPTH
        if even:
            return send(tbuf.at[slot, 1 - row], two_in.at[chunk], two_sem, chunk, y_peer)
        return send(tbuf.at[slot, 1 - narrow], two_in.at[chunk], two_sem, chunk, x_peer)

    def z_copies(chunk):
        slot = chunk % DEPTH
        return [
            pltpu.make_async_remote_copy(
                src_ref=ubuf.at[slot, (deep + o) % 4], dst_ref=z_in.at[chunk, o - 1],
                send_sem=zs_sem.at[chunk, o - 1], recv_sem=zr_sem.at[chunk, o - 1],
                device_id=z_to[o - 1], device_id_type=MESH,
            )
            for o in (1, 2, 3)
        ]

    def far_copy(chunk):
        return send(fbuf.at[chunk], far_in.at[chunk], far_sem, chunk, x_peer)

    def add(left, right):
        return left.astype(jnp.float32) + right.astype(jnp.float32)

    def make(chunk):
        for half in range(2):
            for copy in copies(a_in.at[0], b_up, 0, half):
                copy.wait()
            for side in range(2):
                product = jnp.dot(
                    abuf[half, side], bbuf[half], preferred_element_type=jnp.float32
                )
                for unit in range(8):
                    gbuf[side, half, unit] = product[unit * 72 : unit * 72 + 72].astype(jnp.bfloat16)

            @pl.when(chunk + 1 < PER_HALF)
            def _():
                fetch(chunk + 1, half)

        core_copy(chunk).start()

    def pair(chunk, even):
        core_copy(chunk).wait()
        slot = chunk % DEPTH

        def body(step, carry):
            half, unit = step // 8, step % 8
            value = add(gbuf[core, half, unit], core_in[chunk, half, unit]).astype(jnp.bfloat16)
            deep_at, row_at = unit // 2, unit % 2
            if even:
                sbuf[slot, half, row_at, deep_at] = value
            else:
                sbuf[slot, row_at, half, deep_at] = value
            return carry

        lax.fori_loop(0, 16, body, 0)
        one_copy(chunk, even).start()

    def first(chunk, even):
        one_copy(chunk, even).wait()
        slot = chunk % DEPTH
        mine = narrow if even else row

        def body(step, carry):
            outer, inner = step // 4, step % 4
            tbuf[slot, outer, inner] = add(
                sbuf[slot, mine, outer, inner], one_in[chunk, outer, inner]
            ).astype(jnp.bfloat16)
            return carry

        lax.fori_loop(0, 8, body, 0)
        two_copy(chunk, even).start()

    def second(chunk, even):
        two_copy(chunk, even).wait()
        slot = chunk % DEPTH
        mine = row if even else narrow

        def body(step, carry):
            ubuf[slot, step] = add(tbuf[slot, mine, step], two_in[chunk, step]).astype(jnp.bfloat16)
            return carry

        lax.fori_loop(0, 4, body, 0)
        for copy in z_copies(chunk):
            copy.start()

    def third(chunk):
        for copy in z_copies(chunk):
            copy.wait()
        total = add(ubuf[chunk % DEPTH, deep], z_in[chunk, 0])
        total = total + add(z_in[chunk, 1], z_in[chunk, 2])
        out_ref[narrow * PER_HALF + chunk] = total
        fbuf[chunk] = total.astype(jnp.bfloat16)
        far_copy(chunk).start()

    for half in range(2):
        fetch(0, half)

    def turn(now, carry):
        for lag, action, fixed in (
            (1 + 3 * DEPTH, third, False),
            (1 + 2 * DEPTH, second, True),
            (1 + DEPTH, first, True),
            (1, pair, True),
            (0, make, False),
        ):
            chunk = now - lag
            valid = jnp.logical_and(chunk >= 0, chunk < PER_HALF)
            if fixed:
                even = (2 * chunk + 10 * PER_HALF) % 5 < 2

                @pl.when(jnp.logical_and(valid, even))
                def _(action=action, chunk=chunk):
                    action(chunk, True)

                @pl.when(jnp.logical_and(valid, jnp.logical_not(even)))
                def _(action=action, chunk=chunk):
                    action(chunk, False)

            else:

                @pl.when(valid)
                def _(action=action, chunk=chunk):
                    action(chunk)

        seq_len = projected_ref.shape[0] // 2
        for group in range(4):

            @pl.when(jnp.logical_and(now < 8, now % 4 == group))
            def _(group=group):
                rows = pl.ds(pl.multiple_of(now // 4 * seq_len, seq_len), seq_len)
                for head in range(4 * group, 4 * group + 4):
                    attend_back_head(
                        head, projected_ref.at[rows], grad_ref.at[rows], lse_ref.at[rows], b_in.at[rows]
                    )

        return carry

    lax.fori_loop(0, PER_HALF + 3 * DEPTH + 1, turn, 0)

    def finish(chunk, carry):
        far_copy(chunk).wait()
        out_ref[(1 - narrow) * PER_HALF + chunk] = far_in[chunk].astype(jnp.float32)
        return carry

    lax.fori_loop(0, PER_HALF, finish, 0)


def reduce_weights(*operands):
    bf = jnp.bfloat16
    dma = pltpu.SemaphoreType.DMA
    unit = (72, LANES)
    n = PER_HALF
    return pl.pallas_call(
        reduce_kernel,
        out_shape=(
            jax.ShapeDtypeStruct((2 * n,) + unit, jnp.float32),
            jax.ShapeDtypeStruct(operands[0].shape, bf),
        ),
        in_specs=in_vmem(3) + [pl.BlockSpec(memory_space=pl.ANY)] * 7,
        out_specs=tuple(in_vmem(2)),
        scratch_shapes=[
            pltpu.VMEM((2,) + operands[3].shape[1:], bf),
            pltpu.VMEM((2, operands[0].shape[0], LANES), bf),
            pltpu.VMEM((2, 2, 8) + unit, bf),
            pltpu.VMEM((DEPTH, 2, 2, 4) + unit, bf),
            pltpu.VMEM((DEPTH, 2, 4) + unit, bf),
            pltpu.VMEM((DEPTH, 4) + unit, bf),
            pltpu.VMEM((n,) + unit, bf),
            pltpu.VMEM((n, 2, 8) + unit, bf),
            pltpu.VMEM((n, 2, 4) + unit, bf),
            pltpu.VMEM((n, 4) + unit, bf),
            pltpu.VMEM((n, 3) + unit, bf),
            pltpu.VMEM((n,) + unit, bf),
            dma((2,)),
            dma((2,)),
            dma((2, n)),
            dma((2, n)),
            dma((2, n)),
            dma((n, 3)),
            dma((n, 3)),
            dma((2, n)),
        ],
        compiler_params=pltpu.CompilerParams(
            collective_id=1, has_side_effects=True, vmem_limit_bytes=66_000_000
        ),
        name="reduce_weights",
    )(*operands)


def by_holder(left, parts):
    tokens = left.shape[0]
    rows = left.T.reshape(8, 2, parts, 72, tokens)
    return rows.transpose(2, 1, 0, 3, 4).reshape(parts, 2, 576, tokens)


def weight_grads(
    projected, grad_attended, log_total, first_input, attended, second_in, activated,
    grad_branch, grad_hidden, grad_mlp,
):
    done, grad_projected = reduce_weights(
        projected, grad_attended, log_total, by_holder(first_input, 1), by_holder(attended, 1),
        by_holder(second_in, 1), by_holder(activated, 4), grad_branch, grad_hidden, grad_mlp,
    )

    def flat(*pieces):
        part = jnp.concatenate(pieces) if len(pieces) > 1 else pieces[0]
        return part.transpose(1, 0, 2).reshape(72, part.shape[0] * LANES)

    down = done[18:30].reshape(4, 3, 72, LANES).transpose(0, 2, 1, 3).reshape(288, 3 * LANES)
    return grad_projected, (flat(done[15:18], done[30:]), flat(done[12:15]), flat(done[:12]), down)


def place(index, wide_count):
    return (index // wide_count, index % wide_count)


def meet(total, me, wide_count):
    barrier = pltpu.get_barrier_semaphore()

    def greet(step, carry):
        pl.semaphore_signal(
            barrier, inc=1, device_id=place((me + step) % total, wide_count), device_id_type=MESH
        )
        return carry

    lax.fori_loop(1, total, greet, 0)
    pl.semaphore_wait(barrier, total - 1)


def exchange(step, source, landing, send_sems, recv_sems, peer):
    return pltpu.make_async_remote_copy(
        src_ref=source, dst_ref=landing, send_sem=send_sems.at[step], recv_sem=recv_sems.at[step],
        device_id=peer, device_id_type=MESH,
    )


def loop(count, action):
    def body(step, carry):
        action(step)
        return carry

    lax.fori_loop(1, count, body, 0)


def gather_steps(shard_ref, full_ref, own_sem, zs_sem, zr_sem, one_sem, two_sem, core_sem):
    narrow, wide = lax.axis_index("narrow"), lax.axis_index("wide")
    core, row, deep = wide % 2, (wide // 2) % 2, wide // 4
    core_peer = (narrow, wide + 1 - 2 * core)
    x_peer = (1 - narrow, wide)
    y_peer = (narrow, wide + 2 - 4 * row)
    chunks = shard_ref.shape[1] // (2 * LANES)

    def span(chunk, half):
        return pl.ds(pl.multiple_of((chunk + half * chunks) * LANES, LANES), LANES)

    def send(view, sems, chunk, number, peer):
        return pltpu.make_async_remote_copy(
            src_ref=view, dst_ref=view, send_sem=sems.at[0, chunk, number],
            recv_sem=sems.at[1, chunk, number], device_id=peer, device_id_type=MESH,
        )

    def own(chunk):
        return pltpu.make_async_copy(
            shard_ref.at[:, span(chunk, narrow)],
            full_ref.at[deep, row, core, :, span(chunk, narrow)],
            own_sem.at[chunk],
        )

    def along_z(chunk):
        return [
            pltpu.make_async_remote_copy(
                src_ref=shard_ref.at[:, span(chunk, narrow)],
                dst_ref=full_ref.at[deep, row, core, :, span(chunk, narrow)],
                send_sem=zs_sem.at[chunk, o - 1], recv_sem=zr_sem.at[chunk, o - 1],
                device_id=(narrow, (deep + o) % 4 * 4 + wide % 4), device_id_type=MESH,
            )
            for o in (1, 2, 3)
        ]

    def one(chunk):
        view = full_ref.at[:, row, core, :, span(chunk, narrow)]
        return [send(view, one_sem, chunk, 0, x_peer if chunk % 2 else y_peer)]

    def two(chunk):
        if chunk % 2:
            return [
                send(full_ref.at[:, row, core, :, span(chunk, half)], two_sem, chunk, half, y_peer)
                for half in range(2)
            ]
        return [
            send(full_ref.at[:, side, core, :, span(chunk, narrow)], two_sem, chunk, side, x_peer)
            for side in range(2)
        ]

    def across(chunk):
        return [
            send(full_ref.at[:, :, core, :, span(chunk, half)], core_sem, chunk, half, core_peer)
            for half in range(2)
        ]

    def begin():
        for chunk in range(chunks):
            own(chunk).start()
            for copy in along_z(chunk):
                copy.start()

    def run():
        stages = (lambda chunk: [own(chunk)] + along_z(chunk), one, two, across)
        for turn in range(chunks + 4):
            for stage in (2, 1, 0):
                chunk = turn - 2 * stage
                if 0 <= chunk < chunks:
                    for copy in stages[stage](chunk):
                        copy.wait()
                    for copy in stages[stage + 1](chunk):
                        copy.start()
        for chunk in range(chunks):
            for copy in across(chunk):
                copy.wait()

    return begin, run


def front_kernel(narrow_count, wide_count, with_weights, *refs):
    if with_weights:
        pack_ref, weight_ref, bias_ref, shard_ref, all_ref, mod_ref, full_ref = refs[:7]
        part, send_sem, recv_sem, send_two, recv_two = refs[7:12]
        begin, run = gather_steps(shard_ref, full_ref, *refs[12:])
    else:
        pack_ref, weight_ref, bias_ref, all_ref, mod_ref = refs[:5]
        part, send_sem, recv_sem, send_two, recv_two = refs[5:]
    total = narrow_count * wide_count
    narrow, wide = lax.axis_index("narrow"), lax.axis_index("wide")
    me = narrow * wide_count + wide
    base = narrow * wide_count
    meet(total, me, wide_count)

    def spread(step):
        return exchange(
            step, pack_ref, all_ref.at[me], send_sem, recv_sem, place((me + step) % total, wide_count)
        )

    loop(total, lambda step: spread(step).start())
    if with_weights:
        begin()
    all_ref[me] = pack_ref[...]
    loop(total, lambda step: spread(step).wait())
    rows = all_ref[pl.ds(base, wide_count)].astype(jnp.float32)
    rows = rows.reshape(wide_count * 8, rows.shape[2]).astype(jnp.bfloat16)
    product = jnp.dot(rows, weight_ref[...], preferred_element_type=jnp.float32)
    product = product + bias_ref[...].astype(jnp.float32)
    part[...] = product.reshape(part.shape).astype(jnp.bfloat16)

    def deal(step):
        to = (wide + step) % wide_count
        return exchange(step, part.at[to], mod_ref.at[wide], send_two, recv_two, (narrow, to))

    loop(wide_count, lambda step: deal(step).start())
    mod_ref[wide] = part[wide]
    if with_weights:
        run()
    loop(wide_count, lambda step: deal(step).wait())


def tail_kernel(narrow_count, wide_count, *refs):
    mod_refs, (in_ref, out_ref, up_ref, down_ref, all_ref, weight_ref) = refs[:6], refs[6:12]
    ada_ref, misc_ref, cond_ref, wide_mod, layout, gift_ref = refs[12:18]
    gifts, part, shares, send_sem, recv_sem, send_two, recv_two = refs[18:]
    total = narrow_count * wide_count
    narrow, wide = lax.axis_index("narrow"), lax.axis_index("wide")
    me = narrow * wide_count + wide
    base = narrow * wide_count
    slots, model_width = mod_refs[0].shape
    columns = layout.shape[2]
    for number, ref in enumerate(mod_refs):
        wide_mod[:slots, number * model_width : (number + 1) * model_width] = ref[...]
    layout[...] = jnp.zeros_like(layout)
    for holder in range(wide_count):
        layout[holder, :slots] = wide_mod[:slots, holder * columns : (holder + 1) * columns]
        span = 2 * model_width // wide_count
        at = holder * span
        at = at if at < model_width else at + model_width
        layout[holder, 4:5, :span] = in_ref[:, at : at + span]
        for row, ref in ((5, out_ref), (6, up_ref), (7, down_ref)):
            span = ref.shape[1] // wide_count
            layout[holder, row : row + 1, :span] = ref[:, holder * span : (holder + 1) * span]
    gift_ref[...] = layout[...].astype(jnp.bfloat16)
    meet(total, me, wide_count)

    def spread(step):
        to = (me + step) % total
        return exchange(
            step, gift_ref.at[to % wide_count], gifts.at[me], send_sem, recv_sem, place(to, wide_count)
        )

    loop(total, lambda step: spread(step).start())
    gifts[me] = gift_ref[wide]
    loop(total, lambda step: spread(step).wait())
    mine = gifts[pl.ds(base, wide_count)].astype(jnp.float32)
    mine = mine.reshape(wide_count * 8, mine.shape[2]).astype(jnp.bfloat16)
    share = matmul_back(mine, weight_ref[...])
    part[...] = share.reshape(part.shape).astype(jnp.bfloat16)

    def deal(step):
        to = (wide + step) % wide_count
        return exchange(step, part.at[to], shares.at[wide], send_two, recv_two, (narrow, to))

    loop(wide_count, lambda step: deal(step).start())
    shares[wide] = part[wide]
    every = gifts[...].astype(jnp.float32)
    misc_ref[...] = jnp.sum(every, axis=0)
    grads = every.reshape(total * 8, every.shape[2]).astype(jnp.bfloat16)
    conds = all_ref[...].astype(jnp.float32)
    conds = conds.reshape(total * 8, conds.shape[2]).astype(jnp.bfloat16)
    ada_ref[...] = matmul_outer(conds, grads)
    loop(wide_count, lambda step: deal(step).wait())
    cond_ref[...] = jnp.sum(shares[...].astype(jnp.float32), axis=0)


def in_vmem(count):
    return [pl.BlockSpec(memory_space=pltpu.VMEM)] * count


def dmas(*counts):
    return [pltpu.SemaphoreType.DMA((count,)) for count in counts]


def front(cond_act, biases, ada_weight, ada_bias, shards):
    narrow_count, wide_count = lax.axis_size("narrow"), lax.axis_size("wide")
    total = narrow_count * wide_count
    slots, model_width = cond_act.shape
    columns = ada_weight.shape[1]
    bias_row = jnp.concatenate(biases)
    bias_row = jnp.pad(bias_row, (0, model_width - bias_row.shape[0]))[None]
    pack = jnp.concatenate(
        [cond_act, bias_row, jnp.zeros((7 - slots, model_width), jnp.bfloat16)]
    )
    with_weights = narrow_count == 2 and wide_count == 16
    operands = [pack, ada_weight, ada_bias[None]]
    shapes = [
        jax.ShapeDtypeStruct((total, 8, model_width), jnp.bfloat16),
        jax.ShapeDtypeStruct((wide_count, 8, columns), jnp.bfloat16),
    ]
    out_specs = in_vmem(2)
    scratch = [pltpu.VMEM((wide_count, 8, columns), jnp.bfloat16)]
    scratch += dmas(total, total, wide_count, wide_count)
    if with_weights:
        shard = jnp.concatenate(shards, axis=1)
        operands.append(shard)
        shapes.append(jax.ShapeDtypeStruct((4, 2, 2) + shard.shape, jnp.bfloat16))
        out_specs.append(pl.BlockSpec(memory_space=pl.ANY))
        n = shard.shape[1] // (2 * LANES)
        for dims in ((n,), (n, 3), (n, 3), (2, n, 1), (2, n, 2), (2, n, 2)):
            scratch.append(pltpu.SemaphoreType.DMA(dims))
    results = pl.pallas_call(
        partial(front_kernel, narrow_count, wide_count, with_weights),
        out_shape=tuple(shapes),
        in_specs=in_vmem(len(operands)),
        out_specs=tuple(out_specs),
        scratch_shapes=scratch,
        compiler_params=pltpu.CompilerParams(collective_id=2, has_side_effects=True),
        name="front",
    )(*operands)
    if not with_weights:
        return tuple(results) + tuple(lax.all_gather(shard, "wide", axis=0, tiled=True) for shard in shards)
    full = results[2].reshape(wide_count * shard.shape[0], shard.shape[1])
    weights, at = [], 0
    for piece in shards:
        weights.append(full[:, at : at + piece.shape[1]])
        at += piece.shape[1]
    return tuple(results[:2]) + tuple(weights)


def tail(mod_grads, bias_sums, gathered, ada_weight):
    narrow_count, wide_count = lax.axis_size("narrow"), lax.axis_size("wide")
    total = narrow_count * wide_count
    slots = mod_grads[0].shape[0]
    model_width, columns = ada_weight.shape
    operands = list(mod_grads) + [sums[None] for sums in bias_sums] + [gathered, ada_weight]
    ada, misc, cond = pl.pallas_call(
        partial(tail_kernel, narrow_count, wide_count),
        out_shape=(
            jax.ShapeDtypeStruct((model_width, columns), jnp.float32),
            jax.ShapeDtypeStruct((8, columns), jnp.float32),
            jax.ShapeDtypeStruct((8, model_width), jnp.float32),
        ),
        in_specs=in_vmem(len(operands)),
        out_specs=tuple(in_vmem(3)),
        scratch_shapes=[
            pltpu.VMEM((8, 6 * model_width), jnp.float32),
            pltpu.VMEM((wide_count, 8, columns), jnp.float32),
            pltpu.VMEM((wide_count, 8, columns), jnp.bfloat16),
            pltpu.VMEM((total, 8, columns), jnp.bfloat16),
            pltpu.VMEM((wide_count, 8, model_width), jnp.bfloat16),
            pltpu.VMEM((wide_count, 8, model_width), jnp.bfloat16),
        ]
        + dmas(total, total, wide_count, wide_count),
        compiler_params=pltpu.CompilerParams(collective_id=3, has_side_effects=True),
        name="tail",
    )(*operands)
    spans = [2 * model_width // wide_count] + [sums.shape[0] // wide_count for sums in bias_sums[1:]]
    grads = [misc[4 + number, :span] for number, span in enumerate(spans)]
    return ada, misc[:slots].sum(axis=0), cond[:slots], grads


def head_parts(ref, head, width, count):
    at = head * width
    span = width * HEADS
    return [ref[:, number * span + at : number * span + at + width] for number in range(count)]


def attend_kernel(projected_ref, out_ref, lse_ref):
    width = out_ref.shape[2] // HEADS
    scale = width ** (-0.5)
    for head in range(HEADS):
        query, key, value = head_parts(projected_ref.at[0], head, width, 3)
        scores = matmul_back(query, key) * scale
        top = jnp.max(scores, axis=-1, keepdims=True)
        lse = top + jnp.log(jnp.sum(jnp.exp(scores - top), axis=-1, keepdims=True))
        probs = jnp.exp(scores - lse).astype(jnp.bfloat16)
        out_ref[0, :, head * width : head * width + width] = matmul_rows(probs, value).astype(
            jnp.bfloat16
        )
        lse_ref[0, :, head : head + 1] = lse


def attend_back_head(head, projected_ref, grad_ref, lse_ref, out_ref):
    model_width = grad_ref.shape[1]
    width = model_width // HEADS
    scale = width ** (-0.5)
    query, key, value = head_parts(projected_ref, head, width, 3)
    (grad,) = head_parts(grad_ref, head, width, 1)
    scores = matmul_back(query, key) * scale
    probs = jnp.exp(scores - lse_ref[:, head : head + 1])
    grad_value = matmul_outer(probs.astype(jnp.bfloat16), grad)
    grad_probs = matmul_back(grad, value)
    row_dot = jnp.sum(grad_probs * probs, axis=-1, keepdims=True)
    grad_scores = (probs * (grad_probs - row_dot)).astype(jnp.bfloat16)
    grad_query = matmul_rows(grad_scores, key) * scale
    grad_key = matmul_outer(grad_scores, query) * scale
    for number, part in enumerate((grad_query, grad_key, grad_value)):
        at = number * model_width + head * width
        out_ref[:, at : at + width] = part.astype(jnp.bfloat16)


def attend_back_kernel(*refs):
    for head in range(HEADS):
        attend_back_head(head, *[ref.at[0] for ref in refs])


def by_image(shape):
    return pl.BlockSpec((1,) + shape[1:], lambda image: (image, 0, 0))


def attend_call(kernel, operands, shapes, name):
    slots, seq_len = operands[0].shape[:2]
    work = slots * seq_len * seq_len
    return pl.pallas_call(
        kernel,
        grid=(slots,),
        out_shape=shapes,
        in_specs=[by_image(operand.shape) for operand in operands],
        out_specs=jax.tree.map(lambda shape: by_image(shape.shape), shapes),
        cost_estimate=pl.CostEstimate(
            flops=8 * work * operands[0].shape[2] // 3,
            bytes_accessed=sum(operand.size * 2 for operand in operands) * 2,
            transcendentals=work * HEADS,
        ),
        name=name,
    )(*operands)


def per_device(
    patches,
    condition,
    image_counts,
    ada_weight,
    ada_bias,
    inproj_weight,
    inproj_bias,
    outproj_weight,
    outproj_bias,
    up_weight,
    up_bias,
    down_weight,
    down_bias,
    cotangent,
):
    slots, seq_len, model_width = patches.shape
    row_total = slots * seq_len
    wide_count = lax.axis_size("wide")
    live = (jnp.arange(slots) < image_counts[0]).astype(jnp.float32)[:, None, None]
    cond_act = jax.nn.silu(condition).astype(jnp.bfloat16)
    gathered, mod_blocks, w_inproj, w_outproj, w_up = front(
        cond_act, (inproj_bias, outproj_bias, up_bias, down_bias), ada_weight, ada_bias,
        (inproj_weight, outproj_weight, up_weight),
    )
    down_weight, mod_blocks = lax.optimization_barrier((down_weight, mod_blocks))
    modulation = (
        mod_blocks[:, :slots].transpose(1, 0, 2).reshape(slots, 6 * model_width).astype(jnp.float32)
    )
    group = lax.dynamic_slice_in_dim(
        gathered[:, slots], lax.axis_index("narrow") * wide_count, wide_count
    )
    all_biases, bias_at = [], 0
    for bias in (inproj_bias, outproj_bias, up_bias, down_bias):
        all_biases.append(group[:, bias_at : bias_at + bias.shape[0]].reshape(-1))
        bias_at += bias.shape[0]
    b_inproj, b_outproj, b_up, b_down = all_biases
    segment_list = [
        modulation[:, None, number * model_width : (number + 1) * model_width]
        for number in range(6)
    ]
    (
        selfattn_offset,
        selfattn_scale,
        selfattn_gate,
        perceptron_offset,
        perceptron_scale,
        perceptron_gate,
    ) = segment_list
    w_down = lax.all_gather(down_weight, "wide", axis=0, tiled=True)
    input_rows = patches.astype(jnp.float32)
    normalized_first, inverse_deviation = normalize(input_rows)
    first_input = (
        (normalized_first * (1.0 + selfattn_scale) + selfattn_offset)
        .astype(jnp.bfloat16)
        .reshape(row_total, model_width)
    )
    proj_bias = b_inproj.astype(jnp.float32)
    full_bias = jnp.concatenate(
        [proj_bias[:model_width], jnp.zeros((model_width,), jnp.float32), proj_bias[model_width:]]
    )
    projected = (matmul_rows(first_input, w_inproj) + full_bias).astype(jnp.bfloat16)
    projected = projected.reshape(slots, seq_len, 3 * model_width)
    attended, log_total = attend_call(
        attend_kernel,
        (projected,),
        (
            jax.ShapeDtypeStruct((slots, seq_len, model_width), jnp.bfloat16),
            jax.ShapeDtypeStruct((slots, seq_len, HEADS), jnp.float32),
        ),
        "attend",
    )
    attended = attended.reshape(row_total, model_width)
    residual_branch = (matmul_rows(attended, w_outproj) + b_outproj.astype(jnp.float32)).reshape(
        slots, seq_len, model_width
    )
    between_state = input_rows + selfattn_gate * residual_branch
    normed_b, inv_b = normalize(between_state)
    second_in = (
        (normed_b * (1.0 + perceptron_scale) + perceptron_offset)
        .astype(jnp.bfloat16)
        .reshape(row_total, model_width)
    )
    hidden = matmul_rows(second_in, w_up) + b_up.astype(jnp.float32)
    gelu_value, gelu_pull = jax.vjp(partial(jax.nn.gelu, approximate=True), hidden)
    activated = gelu_value.astype(jnp.bfloat16)
    w_down, activated = lax.optimization_barrier((w_down, activated))
    mlp_out = (matmul_rows(activated, w_down) + b_down.astype(jnp.float32)).reshape(
        slots, seq_len, model_width
    )
    output = ((between_state + perceptron_gate * mlp_out) * live).astype(jnp.bfloat16)
    wb_inproj, wb_outproj, wb_up, wb_down = w_inproj, w_outproj, w_up, w_down
    grad_out = cotangent.astype(jnp.float32) * live
    grad_gate_mlp = jnp.sum(grad_out * mlp_out, axis=1)
    grad_mlp = (grad_out * perceptron_gate).astype(jnp.bfloat16).reshape(row_total, model_width)
    grad_down_bias = jnp.sum(grad_mlp.astype(jnp.float32), axis=0)
    grad_act = matmul_back(grad_mlp, wb_down)
    grad_hidden = gelu_pull(grad_act)[0].astype(jnp.bfloat16)
    grad_up_bias = jnp.sum(grad_hidden.astype(jnp.float32), axis=0)
    grad_second = matmul_back(grad_hidden, wb_up).reshape(slots, seq_len, model_width)
    grad_scale_mlp = jnp.sum(grad_second * normed_b, axis=1)
    grad_shift_mlp = jnp.sum(grad_second, axis=1)
    between_gradient = grad_out + normalize_reverse(
        normed_b, inv_b, grad_second * (1.0 + perceptron_scale)
    )
    selfattn_gate_gradient = jnp.sum(between_gradient * residual_branch, axis=1)
    residual_branch_gradient = (
        (between_gradient * selfattn_gate).astype(jnp.bfloat16).reshape(row_total, model_width)
    )
    grad_outproj_bias = jnp.sum(residual_branch_gradient.astype(jnp.float32), axis=0)
    grad_attended = (
        matmul_back(residual_branch_gradient, wb_outproj)
        .astype(jnp.bfloat16)
        .reshape(slots, seq_len, model_width)
    )
    fast = lax.axis_size("narrow") == 2 and wide_count == 16
    if fast:
        grad_projected, w_grads = weight_grads(
            projected.reshape(row_total, 3 * model_width),
            grad_attended.reshape(row_total, model_width),
            log_total.reshape(row_total, HEADS),
            first_input, attended, second_in, activated,
            residual_branch_gradient, grad_hidden, grad_mlp,
        )
    else:
        grad_projected = attend_call(
            attend_back_kernel,
            (projected, grad_attended, log_total),
            jax.ShapeDtypeStruct((slots, seq_len, 3 * model_width), jnp.bfloat16),
            "attend_back",
        ).reshape(row_total, 3 * model_width)
    proj_sums = jnp.sum(grad_projected.astype(jnp.float32), axis=0)
    first_gradient = matmul_back(grad_projected, wb_inproj).reshape(slots, seq_len, model_width)
    selfattn_scale_gradient = jnp.sum(first_gradient * normalized_first, axis=1)
    selfattn_offset_gradient = jnp.sum(first_gradient, axis=1)
    grad_patches = (
        between_gradient
        + normalize_reverse(
            normalized_first, inverse_deviation, first_gradient * (1.0 + selfattn_scale)
        )
    ).astype(jnp.bfloat16)
    mod_grads = (
        selfattn_offset_gradient,
        selfattn_scale_gradient,
        selfattn_gate_gradient,
        grad_shift_mlp,
        grad_scale_mlp,
        grad_gate_mlp,
    )
    grad_ada_weight, grad_ada_bias, grad_cond_act, bias_shares = tail(
        mod_grads,
        (proj_sums, grad_outproj_bias, grad_up_bias, grad_down_bias),
        gathered,
        ada_weight,
    )
    _, silu_pull = jax.vjp(jax.nn.silu, condition)
    grad_condition = silu_pull(grad_cond_act)[0]
    ff_width = activated.shape[1]
    input_factors = (
        (first_input, grad_projected, 0),
        (attended, residual_branch_gradient, 3 * model_width),
        (second_in, grad_hidden, 4 * model_width),
    )
    down_factors = ((activated, grad_mlp, 0),)
    input_block = (4 * model_width + ff_width) // 4
    down_block = model_width // 2
    block_jobs = [
        (input_factors, model_width, number * input_block, input_block) for number in range(4)
    ]
    block_jobs = block_jobs + [
        (down_factors, ff_width, number * down_block, down_block) for number in range(2)
    ]

    def reduce_block(factors, rows, first, width):
        return lax.psum_scatter(
            block_term(factors, lax.axis_size("wide") * (rows // wide_count), first, width).astype(
                jnp.bfloat16
            ),
            "wide",
            scatter_dimension=0,
            tiled=True,
        ).astype(jnp.float32)

    if not fast:
        shards = [reduce_block(*job) for job in block_jobs]
        input_grads = jnp.concatenate(shards[:4], axis=1)
        w_grads = tuple(
            lax.psum(part.astype(jnp.bfloat16), "narrow").astype(jnp.float32)
            for part in (
                input_grads[:, : 3 * model_width],
                input_grads[:, 3 * model_width : 4 * model_width],
                input_grads[:, 4 * model_width :],
                jnp.concatenate(shards[4:], axis=1),
            )
        )
    return (
        output,
        grad_patches,
        grad_condition,
        grad_ada_weight,
        grad_ada_bias,
        w_grads[0],
        bias_shares[0],
        w_grads[1],
        bias_shares[1],
        w_grads[2],
        bias_shares[2],
        w_grads[3],
        bias_shares[3],
    )


def solution(mesh):
    in_specs = (
        P(("narrow", "wide"), None, None),
        P(("narrow", "wide"), None),
        P(("narrow", "wide")),
        P(None, "wide"),
        P("wide"),
        P("wide", None),
        P("wide"),
        P("wide", None),
        P("wide"),
        P("wide", None),
        P("wide"),
        P("wide", None),
        P("wide"),
        P(("narrow", "wide"), None, None),
    )
    out_specs = (
        P(("narrow", "wide"), None, None),
        P(("narrow", "wide"), None, None),
        P(("narrow", "wide"), None),
        P(None, "wide"),
        P("wide"),
        P("wide", None),
        P("wide"),
        P("wide", None),
        P("wide"),
        P("wide", None),
        P("wide"),
        P("wide", None),
        P("wide"),
    )
    return jax.shard_map(
        per_device, mesh=mesh, in_specs=in_specs, out_specs=out_specs, check_vma=False
    )
```

```python
from functools import partial

import jax
import jax.numpy as jnp
from jax import lax
from jax.sharding import PartitionSpec as P

from jax.experimental import pallas as pl
from jax.experimental.pallas import tpu as pltpu

HEADS = 16
MESH = pl.DeviceIdType.MESH
DEPTH = 4
AHEAD = 3


norm_eps = 1e-06


def normalize(values):
    center = jnp.mean(values, axis=-1, keepdims=True)
    shifted = values - center
    inv_std = lax.rsqrt(jnp.mean(shifted * shifted, axis=-1, keepdims=True) + norm_eps)
    return (shifted * inv_std, inv_std)


def normalize_reverse(normed, inv_std, grad_normed):
    mean_grad = jnp.mean(grad_normed, axis=-1, keepdims=True)
    mean_proj = jnp.mean(grad_normed * normed, axis=-1, keepdims=True)
    return inv_std * (grad_normed - mean_grad - normed * mean_proj)


def matmul_rows(left, right):
    return jnp.dot(left, right, preferred_element_type=jnp.float32)


def matmul_back(left, right):
    return lax.dot_general(
        left, right, (((1,), (1,)), ((), ())), preferred_element_type=jnp.float32
    )


def matmul_outer(left, right):
    return lax.dot_general(
        left, right, (((0,), (0,)), ((), ())), preferred_element_type=jnp.float32
    )


def block_term(factors, count, first, width):
    pieces = []
    for left, right, base in factors:
        lower = max(first, base)
        upper = min(first + width, base + right.shape[1])
        if lower < upper:
            rows_part = lax.slice_in_dim(left, 0, count, axis=1)
            pieces.append(matmul_outer(rows_part, right[:, lower - base : upper - base]))
    return jnp.concatenate(pieces, axis=1)

LANES = 384
PER_HALF = 18


def reduce_kernel(
    projected_ref, grad_ref, lse_ref, a_in, a_out, a_up, a_down, b_out, b_up, b_down, out_ref, b_in,
    abuf, bbuf, gbuf, sbuf, tbuf, ubuf, fbuf, core_in, one_in, two_in, z_in, far_in,
    asem, bsem, core_sem, one_sem, two_sem, zs_sem, zr_sem, far_sem,
):
    narrow = lax.axis_index("narrow")
    wide = lax.axis_index("wide")
    core = wide % 2
    row = (wide // 2) % 2
    deep = wide // 4
    core_peer = (narrow, wide + 1 - 2 * core)
    x_peer = (1 - narrow, wide)
    y_peer = (narrow, wide + 2 - 4 * row)
    z_to = [(narrow, (deep + o) % 4 * 4 + wide % 4) for o in (1, 2, 3)]

    barrier = pltpu.get_barrier_semaphore()
    for peer in [core_peer, x_peer, y_peer] + z_to:
        pl.semaphore_signal(barrier, inc=1, device_id=peer, device_id_type=MESH)
    pl.semaphore_wait(barrier, 6)

    def copies(left, right, column, half):
        column = pl.multiple_of(column * LANES, LANES)
        return (
            pltpu.make_async_copy(left, abuf.at[half], asem.at[half]),
            pltpu.make_async_copy(right.at[:, pl.ds(column, LANES)], bbuf.at[half], bsem.at[half]),
        )

    def fetch(chunk, half):
        if half:
            regions = ((0, 12, None, b_down, 0), (12, 18, a_in, b_in, 3))
        else:
            regions = ((0, 12, a_up, b_up, 0), (12, 15, a_out, b_out, 0), (15, 18, a_in, b_in, 0))
        for lower, upper, left, right, offset in regions:

            @pl.when(jnp.logical_and(chunk >= lower, chunk < upper))
            def _(lower=lower, left=left, right=right, offset=offset):
                if left is None:
                    pieces = copies(a_down.at[chunk // 3], right, chunk % 3, half)
                else:
                    pieces = copies(left.at[0], right, chunk - lower + offset, half)
                for copy in pieces:
                    copy.start()

    def send(src, dst, sems, chunk, peer):
        return pltpu.make_async_remote_copy(
            src_ref=src, dst_ref=dst, send_sem=sems.at[0, chunk], recv_sem=sems.at[1, chunk],
            device_id=peer, device_id_type=MESH,
        )

    def core_copy(chunk):
        return send(gbuf.at[1 - core], core_in.at[chunk], core_sem, chunk, core_peer)

    def one_copy(chunk, even):
        slot = chunk % DEPTH
        if even:
            return send(sbuf.at[slot, 1 - narrow], one_in.at[chunk], one_sem, chunk, x_peer)
        return send(sbuf.at[slot, 1 - row], one_in.at[chunk], one_sem, chunk, y_peer)

    def two_copy(chunk, even):
        slot = chunk % DEPTH
        if even:
            return send(tbuf.at[slot, 1 - row], two_in.at[chunk], two_sem, chunk, y_peer)
        return send(tbuf.at[slot, 1 - narrow], two_in.at[chunk], two_sem, chunk, x_peer)

    def z_copies(chunk):
        slot = chunk % DEPTH
        return [
            pltpu.make_async_remote_copy(
                src_ref=ubuf.at[slot, (deep + o) % 4], dst_ref=z_in.at[chunk, o - 1],
                send_sem=zs_sem.at[chunk, o - 1], recv_sem=zr_sem.at[chunk, o - 1],
                device_id=z_to[o - 1], device_id_type=MESH,
            )
            for o in (1, 2, 3)
        ]

    def far_copy(chunk):
        return send(fbuf.at[chunk], far_in.at[chunk], far_sem, chunk, x_peer)

    def add(left, right):
        return left.astype(jnp.float32) + right.astype(jnp.float32)

    def make(chunk):
        for half in range(2):
            for copy in copies(a_in.at[0], b_up, 0, half):
                copy.wait()
            for side in range(2):
                product = jnp.dot(
                    abuf[half, side], bbuf[half], preferred_element_type=jnp.float32
                )
                for unit in range(8):
                    gbuf[side, half, unit] = product[unit * 72 : unit * 72 + 72].astype(jnp.bfloat16)

            @pl.when(chunk + 1 < PER_HALF)
            def _():
                fetch(chunk + 1, half)

        core_copy(chunk).start()

    def pair(chunk, even):
        core_copy(chunk).wait()
        slot = chunk % DEPTH

        def body(step, carry):
            half, unit = step // 8, step % 8
            value = add(gbuf[core, half, unit], core_in[chunk, half, unit]).astype(jnp.bfloat16)
            deep_at, row_at = unit // 2, unit % 2
            if even:
                sbuf[slot, half, row_at, deep_at] = value
            else:
                sbuf[slot, row_at, half, deep_at] = value
            return carry

        lax.fori_loop(0, 16, body, 0)
        one_copy(chunk, even).start()

    def first(chunk, even):
        one_copy(chunk, even).wait()
        slot = chunk % DEPTH
        mine = narrow if even else row

        def body(step, carry):
            outer, inner = step // 4, step % 4
            tbuf[slot, outer, inner] = add(
                sbuf[slot, mine, outer, inner], one_in[chunk, outer, inner]
            ).astype(jnp.bfloat16)
            return carry

        lax.fori_loop(0, 8, body, 0)
        two_copy(chunk, even).start()

    def second(chunk, even):
        two_copy(chunk, even).wait()
        slot = chunk % DEPTH
        mine = row if even else narrow

        def body(step, carry):
            ubuf[slot, step] = add(tbuf[slot, mine, step], two_in[chunk, step]).astype(jnp.bfloat16)
            return carry

        lax.fori_loop(0, 4, body, 0)
        for copy in z_copies(chunk):
            copy.start()

    def third(chunk):
        for copy in z_copies(chunk):
            copy.wait()
        total = add(ubuf[chunk % DEPTH, deep], z_in[chunk, 0])
        total = total + add(z_in[chunk, 1], z_in[chunk, 2])
        out_ref[narrow * PER_HALF + chunk] = total
        fbuf[chunk] = total.astype(jnp.bfloat16)
        far_copy(chunk).start()

    for half in range(2):
        fetch(0, half)

    seq_len = projected_ref.shape[0] // 2

    def turn(now, carry):
        for lag, action, fixed in (
            (1 + 3 * DEPTH, third, False),
            (1 + 2 * DEPTH, second, True),
            (1 + DEPTH, first, True),
            (1, pair, True),
        ):
            chunk = now - lag
            valid = jnp.logical_and(chunk >= 0, chunk < PER_HALF)
            if fixed:
                even = (2 * chunk + 10 * PER_HALF) % 5 < 2

                @pl.when(jnp.logical_and(valid, even))
                def _(action=action, chunk=chunk):
                    action(chunk, True)

                @pl.when(jnp.logical_and(valid, jnp.logical_not(even)))
                def _(action=action, chunk=chunk):
                    action(chunk, False)

            else:

                @pl.when(valid)
                def _(action=action, chunk=chunk):
                    action(chunk)

        for group in range(6):

            @pl.when(jnp.logical_and(now < 12, now % 6 == group))
            def _(group=group):
                rows = pl.ds(pl.multiple_of(now // 6 * seq_len, seq_len), seq_len)
                for head in range(HEADS * group // 6, HEADS * (group + 1) // 6):
                    attend_back_head(
                        head, projected_ref.at[rows], grad_ref.at[rows], lse_ref.at[rows], b_in.at[rows]
                    )

        @pl.when(now < PER_HALF)
        def _():
            make(now)

        return carry

    lax.fori_loop(0, PER_HALF + 3 * DEPTH + 1, turn, 0)

    def finish(chunk, carry):
        far_copy(chunk).wait()
        out_ref[(1 - narrow) * PER_HALF + chunk] = far_in[chunk].astype(jnp.float32)
        return carry

    lax.fori_loop(0, PER_HALF, finish, 0)


def reduce_weights(*operands):
    bf = jnp.bfloat16
    dma = pltpu.SemaphoreType.DMA
    unit = (72, LANES)
    n = PER_HALF
    return pl.pallas_call(
        reduce_kernel,
        out_shape=(
            jax.ShapeDtypeStruct((2 * n,) + unit, jnp.float32),
            jax.ShapeDtypeStruct(operands[0].shape, bf),
        ),
        in_specs=in_vmem(3) + [pl.BlockSpec(memory_space=pl.ANY)] * 7,
        out_specs=tuple(in_vmem(2)),
        scratch_shapes=[
            pltpu.VMEM((2,) + operands[3].shape[1:], bf),
            pltpu.VMEM((2, operands[0].shape[0], LANES), bf),
            pltpu.VMEM((2, 2, 8) + unit, bf),
            pltpu.VMEM((DEPTH, 2, 2, 4) + unit, bf),
            pltpu.VMEM((DEPTH, 2, 4) + unit, bf),
            pltpu.VMEM((DEPTH, 4) + unit, bf),
            pltpu.VMEM((n,) + unit, bf),
            pltpu.VMEM((n, 2, 8) + unit, bf),
            pltpu.VMEM((n, 2, 4) + unit, bf),
            pltpu.VMEM((n, 4) + unit, bf),
            pltpu.VMEM((n, 3) + unit, bf),
            pltpu.VMEM((n,) + unit, bf),
            dma((2,)),
            dma((2,)),
            dma((2, n)),
            dma((2, n)),
            dma((2, n)),
            dma((n, 3)),
            dma((n, 3)),
            dma((2, n)),
        ],
        compiler_params=pltpu.CompilerParams(
            collective_id=1, has_side_effects=True, vmem_limit_bytes=66_000_000
        ),
        name="reduce_weights",
    )(*operands)


def by_holder(left, parts):
    tokens = left.shape[0]
    rows = left.T.reshape(8, 2, parts, 72, tokens)
    return rows.transpose(2, 1, 0, 3, 4).reshape(parts, 2, 576, tokens)


def weight_grads(
    projected, grad_attended, log_total, first_input, attended, second_in, activated,
    grad_branch, grad_hidden, grad_mlp,
):
    done, grad_projected = reduce_weights(
        projected, grad_attended, log_total, by_holder(first_input, 1), by_holder(attended, 1),
        by_holder(second_in, 1), activated, grad_branch, grad_hidden, grad_mlp,
    )

    def flat(*pieces):
        part = jnp.concatenate(pieces) if len(pieces) > 1 else pieces[0]
        return part.transpose(1, 0, 2).reshape(72, part.shape[0] * LANES)

    down = done[18:30].reshape(4, 3, 72, LANES).transpose(0, 2, 1, 3).reshape(288, 3 * LANES)
    return grad_projected, (flat(done[15:18], done[30:]), flat(done[12:15]), flat(done[:12]), down)


def place(index, wide_count):
    return (index // wide_count, index % wide_count)


def meet(total, me, wide_count):
    barrier = pltpu.get_barrier_semaphore()

    def greet(step, carry):
        pl.semaphore_signal(
            barrier, inc=1, device_id=place((me + step) % total, wide_count), device_id_type=MESH
        )
        return carry

    lax.fori_loop(1, total, greet, 0)
    pl.semaphore_wait(barrier, total - 1)


def exchange(step, source, landing, send_sems, recv_sems, peer):
    return pltpu.make_async_remote_copy(
        src_ref=source, dst_ref=landing, send_sem=send_sems.at[step], recv_sem=recv_sems.at[step],
        device_id=peer, device_id_type=MESH,
    )


def loop(count, action):
    def body(step, carry):
        action(step)
        return carry

    lax.fori_loop(1, count, body, 0)


def gather_steps(shard_ref, full_ref, own_sem, zs_sem, zr_sem, one_sem, two_sem, core_sem):
    narrow, wide = lax.axis_index("narrow"), lax.axis_index("wide")
    core, row, deep = wide % 2, (wide // 2) % 2, wide // 4
    core_peer = (narrow, wide + 1 - 2 * core)
    x_peer = (1 - narrow, wide)
    y_peer = (narrow, wide + 2 - 4 * row)
    chunks = shard_ref.shape[1] // (2 * LANES)

    def span(chunk, half):
        return pl.ds(pl.multiple_of((chunk + half * chunks) * LANES, LANES), LANES)

    def send(view, sems, chunk, number, peer):
        return pltpu.make_async_remote_copy(
            src_ref=view, dst_ref=view, send_sem=sems.at[0, chunk, number],
            recv_sem=sems.at[1, chunk, number], device_id=peer, device_id_type=MESH,
        )

    def own(chunk):
        return pltpu.make_async_copy(
            shard_ref.at[:, span(chunk, narrow)],
            full_ref.at[deep, row, core, :, span(chunk, narrow)],
            own_sem.at[chunk],
        )

    def along_z(chunk):
        return [
            pltpu.make_async_remote_copy(
                src_ref=shard_ref.at[:, span(chunk, narrow)],
                dst_ref=full_ref.at[deep, row, core, :, span(chunk, narrow)],
                send_sem=zs_sem.at[chunk, o - 1], recv_sem=zr_sem.at[chunk, o - 1],
                device_id=(narrow, (deep + o) % 4 * 4 + wide % 4), device_id_type=MESH,
            )
            for o in (1, 2, 3)
        ]

    def one(chunk):
        view = full_ref.at[:, row, core, :, span(chunk, narrow)]
        return [send(view, one_sem, chunk, 0, x_peer if chunk % 2 else y_peer)]

    def two(chunk):
        if chunk % 2:
            return [
                send(full_ref.at[:, row, core, :, span(chunk, half)], two_sem, chunk, half, y_peer)
                for half in range(2)
            ]
        return [
            send(full_ref.at[:, side, core, :, span(chunk, narrow)], two_sem, chunk, side, x_peer)
            for side in range(2)
        ]

    def across(chunk):
        return [
            send(full_ref.at[:, :, core, :, span(chunk, half)], core_sem, chunk, half, core_peer)
            for half in range(2)
        ]

    def begin():
        for chunk in range(chunks):
            own(chunk).start()
        for chunk in range(AHEAD):
            for copy in along_z(chunk):
                copy.start()

    def run():
        stages = (lambda chunk: [own(chunk)] + along_z(chunk), one, two, across)
        for turn in range(chunks + 4):
            if turn + AHEAD < chunks:
                for copy in along_z(turn + AHEAD):
                    copy.start()
            for stage in (2, 1, 0):
                chunk = turn - 2 * stage
                if 0 <= chunk < chunks:
                    for copy in stages[stage](chunk):
                        copy.wait()
                    for copy in stages[stage + 1](chunk):
                        copy.start()
        for chunk in range(chunks):
            for copy in across(chunk):
                copy.wait()

    return begin, run


def front_kernel(narrow_count, wide_count, with_weights, *refs):
    if with_weights:
        pack_ref, weight_ref, bias_ref, shard_ref, all_ref, mod_ref, full_ref = refs[:7]
        part, send_sem, recv_sem, send_two, recv_two = refs[7:12]
        begin, run = gather_steps(shard_ref, full_ref, *refs[12:])
    else:
        pack_ref, weight_ref, bias_ref, all_ref, mod_ref = refs[:5]
        part, send_sem, recv_sem, send_two, recv_two = refs[5:]
    total = narrow_count * wide_count
    narrow, wide = lax.axis_index("narrow"), lax.axis_index("wide")
    me = narrow * wide_count + wide
    base = narrow * wide_count
    meet(total, me, wide_count)

    def spread(step):
        return exchange(
            step, pack_ref, all_ref.at[me], send_sem, recv_sem, place((me + step) % total, wide_count)
        )

    loop(total, lambda step: spread(step).start())
    if with_weights:
        begin()
    all_ref[me] = pack_ref[...]
    loop(total, lambda step: spread(step).wait())
    rows = all_ref[pl.ds(base, wide_count)].astype(jnp.float32)
    rows = rows.reshape(wide_count * 8, rows.shape[2]).astype(jnp.bfloat16)
    product = jnp.dot(rows, weight_ref[...], preferred_element_type=jnp.float32)
    product = product + bias_ref[...].astype(jnp.float32)
    part[...] = product.reshape(part.shape).astype(jnp.bfloat16)

    def deal(step):
        to = (wide + step) % wide_count
        return exchange(step, part.at[to], mod_ref.at[wide], send_two, recv_two, (narrow, to))

    loop(wide_count, lambda step: deal(step).start())
    mod_ref[wide] = part[wide]
    if with_weights:
        run()
    loop(wide_count, lambda step: deal(step).wait())


def tail_kernel(narrow_count, wide_count, *refs):
    mod_refs, (in_ref, out_ref, up_ref, down_ref, all_ref, weight_ref) = refs[:6], refs[6:12]
    ada_ref, misc_ref, cond_ref, wide_mod, layout, gift_ref = refs[12:18]
    gifts, part, shares, send_sem, recv_sem, send_two, recv_two = refs[18:]
    total = narrow_count * wide_count
    narrow, wide = lax.axis_index("narrow"), lax.axis_index("wide")
    me = narrow * wide_count + wide
    base = narrow * wide_count
    slots, model_width = mod_refs[0].shape
    columns = layout.shape[2]
    for number, ref in enumerate(mod_refs):
        wide_mod[:slots, number * model_width : (number + 1) * model_width] = ref[...]
    layout[...] = jnp.zeros_like(layout)
    for holder in range(wide_count):
        layout[holder, :slots] = wide_mod[:slots, holder * columns : (holder + 1) * columns]
        span = 2 * model_width // wide_count
        at = holder * span
        at = at if at < model_width else at + model_width
        layout[holder, 4:5, :span] = in_ref[:, at : at + span]
        for row, ref in ((5, out_ref), (6, up_ref), (7, down_ref)):
            span = ref.shape[1] // wide_count
            layout[holder, row : row + 1, :span] = ref[:, holder * span : (holder + 1) * span]
    gift_ref[...] = layout[...].astype(jnp.bfloat16)
    meet(total, me, wide_count)

    def spread(step):
        to = (me + step) % total
        return exchange(
            step, gift_ref.at[to % wide_count], gifts.at[me], send_sem, recv_sem, place(to, wide_count)
        )

    loop(total, lambda step: spread(step).start())
    gifts[me] = gift_ref[wide]
    loop(total, lambda step: spread(step).wait())
    mine = gifts[pl.ds(base, wide_count)].astype(jnp.float32)
    mine = mine.reshape(wide_count * 8, mine.shape[2]).astype(jnp.bfloat16)
    share = matmul_back(mine, weight_ref[...])
    part[...] = share.reshape(part.shape).astype(jnp.bfloat16)

    def deal(step):
        to = (wide + step) % wide_count
        return exchange(step, part.at[to], shares.at[wide], send_two, recv_two, (narrow, to))

    loop(wide_count, lambda step: deal(step).start())
    shares[wide] = part[wide]
    every = gifts[...].astype(jnp.float32)
    misc_ref[...] = jnp.sum(every, axis=0)
    grads = every.reshape(total * 8, every.shape[2]).astype(jnp.bfloat16)
    conds = all_ref[...].astype(jnp.float32)
    conds = conds.reshape(total * 8, conds.shape[2]).astype(jnp.bfloat16)
    ada_ref[...] = matmul_outer(conds, grads)
    loop(wide_count, lambda step: deal(step).wait())
    cond_ref[...] = jnp.sum(shares[...].astype(jnp.float32), axis=0)


def in_vmem(count):
    return [pl.BlockSpec(memory_space=pltpu.VMEM)] * count


def dmas(*counts):
    return [pltpu.SemaphoreType.DMA((count,)) for count in counts]


def front(cond_act, biases, ada_weight, ada_bias, shards):
    narrow_count, wide_count = lax.axis_size("narrow"), lax.axis_size("wide")
    total = narrow_count * wide_count
    slots, model_width = cond_act.shape
    columns = ada_weight.shape[1]
    bias_row = jnp.concatenate(biases)
    bias_row = jnp.pad(bias_row, (0, model_width - bias_row.shape[0]))[None]
    pack = jnp.concatenate(
        [cond_act, bias_row, jnp.zeros((7 - slots, model_width), jnp.bfloat16)]
    )
    with_weights = narrow_count == 2 and wide_count == 16
    operands = [pack, ada_weight, ada_bias[None]]
    shapes = [
        jax.ShapeDtypeStruct((total, 8, model_width), jnp.bfloat16),
        jax.ShapeDtypeStruct((wide_count, 8, columns), jnp.bfloat16),
    ]
    out_specs = in_vmem(2)
    scratch = [pltpu.VMEM((wide_count, 8, columns), jnp.bfloat16)]
    scratch += dmas(total, total, wide_count, wide_count)
    if with_weights:
        shard = jnp.concatenate(shards, axis=1)
        operands.append(shard)
        shapes.append(jax.ShapeDtypeStruct((4, 2, 2) + shard.shape, jnp.bfloat16))
        out_specs.append(pl.BlockSpec(memory_space=pl.ANY))
        n = shard.shape[1] // (2 * LANES)
        for dims in ((n,), (n, 3), (n, 3), (2, n, 1), (2, n, 2), (2, n, 2)):
            scratch.append(pltpu.SemaphoreType.DMA(dims))
    results = pl.pallas_call(
        partial(front_kernel, narrow_count, wide_count, with_weights),
        out_shape=tuple(shapes),
        in_specs=in_vmem(len(operands)),
        out_specs=tuple(out_specs),
        scratch_shapes=scratch,
        compiler_params=pltpu.CompilerParams(collective_id=2, has_side_effects=True),
        name="front",
    )(*operands)
    if not with_weights:
        return tuple(results) + tuple(lax.all_gather(shard, "wide", axis=0, tiled=True) for shard in shards)
    full = results[2].reshape(wide_count * shard.shape[0], shard.shape[1])
    weights, at = [], 0
    for piece in shards:
        weights.append(full[:, at : at + piece.shape[1]])
        at += piece.shape[1]
    return tuple(results[:2]) + tuple(weights)


def tail(mod_grads, bias_sums, gathered, ada_weight):
    narrow_count, wide_count = lax.axis_size("narrow"), lax.axis_size("wide")
    total = narrow_count * wide_count
    slots = mod_grads[0].shape[0]
    model_width, columns = ada_weight.shape
    operands = list(mod_grads) + [sums[None] for sums in bias_sums] + [gathered, ada_weight]
    ada, misc, cond = pl.pallas_call(
        partial(tail_kernel, narrow_count, wide_count),
        out_shape=(
            jax.ShapeDtypeStruct((model_width, columns), jnp.float32),
            jax.ShapeDtypeStruct((8, columns), jnp.float32),
            jax.ShapeDtypeStruct((8, model_width), jnp.float32),
        ),
        in_specs=in_vmem(len(operands)),
        out_specs=tuple(in_vmem(3)),
        scratch_shapes=[
            pltpu.VMEM((8, 6 * model_width), jnp.float32),
            pltpu.VMEM((wide_count, 8, columns), jnp.float32),
            pltpu.VMEM((wide_count, 8, columns), jnp.bfloat16),
            pltpu.VMEM((total, 8, columns), jnp.bfloat16),
            pltpu.VMEM((wide_count, 8, model_width), jnp.bfloat16),
            pltpu.VMEM((wide_count, 8, model_width), jnp.bfloat16),
        ]
        + dmas(total, total, wide_count, wide_count),
        compiler_params=pltpu.CompilerParams(collective_id=3, has_side_effects=True),
        name="tail",
    )(*operands)
    spans = [2 * model_width // wide_count] + [sums.shape[0] // wide_count for sums in bias_sums[1:]]
    grads = [misc[4 + number, :span] for number, span in enumerate(spans)]
    return ada, misc[:slots].sum(axis=0), cond[:slots], grads


def head_parts(ref, head, width, count):
    at = head * width
    span = width * HEADS
    return [ref[:, number * span + at : number * span + at + width] for number in range(count)]


def attend_kernel(projected_ref, out_ref, lse_ref):
    width = out_ref.shape[2] // HEADS
    scale = width ** (-0.5)
    for head in range(HEADS):
        query, key, value = head_parts(projected_ref.at[0], head, width, 3)
        scores = matmul_back(query, key) * scale
        top = jnp.max(scores, axis=-1, keepdims=True)
        lse = top + jnp.log(jnp.sum(jnp.exp(scores - top), axis=-1, keepdims=True))
        probs = jnp.exp(scores - lse).astype(jnp.bfloat16)
        out_ref[0, :, head * width : head * width + width] = matmul_rows(probs, value).astype(
            jnp.bfloat16
        )
        lse_ref[0, :, head : head + 1] = lse


def attend_back_head(head, projected_ref, grad_ref, lse_ref, out_ref):
    model_width = grad_ref.shape[1]
    width = model_width // HEADS
    scale = width ** (-0.5)
    query, key, value = head_parts(projected_ref, head, width, 3)
    (grad,) = head_parts(grad_ref, head, width, 1)
    scores = matmul_back(query, key) * scale
    probs = jnp.exp(scores - lse_ref[:, head : head + 1])
    grad_value = matmul_outer(probs.astype(jnp.bfloat16), grad)
    grad_probs = matmul_back(grad, value)
    row_dot = jnp.sum(grad_probs * probs, axis=-1, keepdims=True)
    grad_scores = (probs * (grad_probs - row_dot)).astype(jnp.bfloat16)
    grad_query = matmul_rows(grad_scores, key) * scale
    grad_key = matmul_outer(grad_scores, query) * scale
    for number, part in enumerate((grad_query, grad_key, grad_value)):
        at = number * model_width + head * width
        out_ref[:, at : at + width] = part.astype(jnp.bfloat16)


def attend_back_kernel(*refs):
    for head in range(HEADS):
        attend_back_head(head, *[ref.at[0] for ref in refs])


def by_image(shape):
    return pl.BlockSpec((1,) + shape[1:], lambda image: (image, 0, 0))


def attend_call(kernel, operands, shapes, name):
    slots, seq_len = operands[0].shape[:2]
    work = slots * seq_len * seq_len
    return pl.pallas_call(
        kernel,
        grid=(slots,),
        out_shape=shapes,
        in_specs=[by_image(operand.shape) for operand in operands],
        out_specs=jax.tree.map(lambda shape: by_image(shape.shape), shapes),
        cost_estimate=pl.CostEstimate(
            flops=8 * work * operands[0].shape[2] // 3,
            bytes_accessed=sum(operand.size * 2 for operand in operands) * 2,
            transcendentals=work * HEADS,
        ),
        name=name,
    )(*operands)


def per_device(
    patches,
    condition,
    image_counts,
    ada_weight,
    ada_bias,
    inproj_weight,
    inproj_bias,
    outproj_weight,
    outproj_bias,
    up_weight,
    up_bias,
    down_weight,
    down_bias,
    cotangent,
):
    slots, seq_len, model_width = patches.shape
    row_total = slots * seq_len
    wide_count = lax.axis_size("wide")
    live = (jnp.arange(slots) < image_counts[0]).astype(jnp.float32)[:, None, None]
    cond_act = jax.nn.silu(condition).astype(jnp.bfloat16)
    gathered, mod_blocks, w_inproj, w_outproj, w_up = front(
        cond_act, (inproj_bias, outproj_bias, up_bias, down_bias), ada_weight, ada_bias,
        (inproj_weight, outproj_weight, up_weight),
    )
    down_weight, mod_blocks = lax.optimization_barrier((down_weight, mod_blocks))
    modulation = (
        mod_blocks[:, :slots].transpose(1, 0, 2).reshape(slots, 6 * model_width).astype(jnp.float32)
    )
    group = lax.dynamic_slice_in_dim(
        gathered[:, slots], lax.axis_index("narrow") * wide_count, wide_count
    )
    all_biases, bias_at = [], 0
    for bias in (inproj_bias, outproj_bias, up_bias, down_bias):
        all_biases.append(group[:, bias_at : bias_at + bias.shape[0]].reshape(-1))
        bias_at += bias.shape[0]
    b_inproj, b_outproj, b_up, b_down = all_biases
    segment_list = [
        modulation[:, None, number * model_width : (number + 1) * model_width]
        for number in range(6)
    ]
    (
        selfattn_offset,
        selfattn_scale,
        selfattn_gate,
        perceptron_offset,
        perceptron_scale,
        perceptron_gate,
    ) = segment_list
    w_down = lax.all_gather(down_weight, "wide", axis=0, tiled=True)
    input_rows = patches.astype(jnp.float32)
    normalized_first, inverse_deviation = normalize(input_rows)
    first_input = (
        (normalized_first * (1.0 + selfattn_scale) + selfattn_offset)
        .astype(jnp.bfloat16)
        .reshape(row_total, model_width)
    )
    proj_bias = b_inproj.astype(jnp.float32)
    full_bias = jnp.concatenate(
        [proj_bias[:model_width], jnp.zeros((model_width,), jnp.float32), proj_bias[model_width:]]
    )
    projected = (matmul_rows(first_input, w_inproj) + full_bias).astype(jnp.bfloat16)
    projected = projected.reshape(slots, seq_len, 3 * model_width)
    attended, log_total = attend_call(
        attend_kernel,
        (projected,),
        (
            jax.ShapeDtypeStruct((slots, seq_len, model_width), jnp.bfloat16),
            jax.ShapeDtypeStruct((slots, seq_len, HEADS), jnp.float32),
        ),
        "attend",
    )
    attended = attended.reshape(row_total, model_width)
    residual_branch = (matmul_rows(attended, w_outproj) + b_outproj.astype(jnp.float32)).reshape(
        slots, seq_len, model_width
    )
    between_state = input_rows + selfattn_gate * residual_branch
    normed_b, inv_b = normalize(between_state)
    second_in = (
        (normed_b * (1.0 + perceptron_scale) + perceptron_offset)
        .astype(jnp.bfloat16)
        .reshape(row_total, model_width)
    )
    hidden = matmul_rows(second_in, w_up) + b_up.astype(jnp.float32)
    gelu_value, gelu_pull = jax.vjp(partial(jax.nn.gelu, approximate=True), hidden)
    activated = gelu_value.astype(jnp.bfloat16)
    fast = lax.axis_size("narrow") == 2 and wide_count == 16
    if fast:
        held_activated = by_holder(activated, 4)
        w_down, activated, held_activated = lax.optimization_barrier(
            (w_down, activated, held_activated)
        )
    mlp_out = (matmul_rows(activated, w_down) + b_down.astype(jnp.float32)).reshape(
        slots, seq_len, model_width
    )
    output = ((between_state + perceptron_gate * mlp_out) * live).astype(jnp.bfloat16)
    wb_inproj, wb_outproj, wb_up, wb_down = w_inproj, w_outproj, w_up, w_down
    grad_out = cotangent.astype(jnp.float32) * live
    grad_gate_mlp = jnp.sum(grad_out * mlp_out, axis=1)
    grad_mlp = (grad_out * perceptron_gate).astype(jnp.bfloat16).reshape(row_total, model_width)
    grad_down_bias = jnp.sum(grad_mlp.astype(jnp.float32), axis=0)
    grad_act = matmul_back(grad_mlp, wb_down)
    grad_hidden = gelu_pull(grad_act)[0].astype(jnp.bfloat16)
    grad_up_bias = jnp.sum(grad_hidden.astype(jnp.float32), axis=0)
    grad_second = matmul_back(grad_hidden, wb_up).reshape(slots, seq_len, model_width)
    grad_scale_mlp = jnp.sum(grad_second * normed_b, axis=1)
    grad_shift_mlp = jnp.sum(grad_second, axis=1)
    between_gradient = grad_out + normalize_reverse(
        normed_b, inv_b, grad_second * (1.0 + perceptron_scale)
    )
    selfattn_gate_gradient = jnp.sum(between_gradient * residual_branch, axis=1)
    residual_branch_gradient = (
        (between_gradient * selfattn_gate).astype(jnp.bfloat16).reshape(row_total, model_width)
    )
    grad_outproj_bias = jnp.sum(residual_branch_gradient.astype(jnp.float32), axis=0)
    grad_attended = (
        matmul_back(residual_branch_gradient, wb_outproj)
        .astype(jnp.bfloat16)
        .reshape(slots, seq_len, model_width)
    )
    if fast:
        grad_projected, w_grads = weight_grads(
            projected.reshape(row_total, 3 * model_width),
            grad_attended.reshape(row_total, model_width),
            log_total.reshape(row_total, HEADS),
            first_input, attended, second_in, held_activated,
            residual_branch_gradient, grad_hidden, grad_mlp,
        )
    else:
        grad_projected = attend_call(
            attend_back_kernel,
            (projected, grad_attended, log_total),
            jax.ShapeDtypeStruct((slots, seq_len, 3 * model_width), jnp.bfloat16),
            "attend_back",
        ).reshape(row_total, 3 * model_width)
    proj_sums = jnp.sum(grad_projected.astype(jnp.float32), axis=0)
    first_gradient = matmul_back(grad_projected, wb_inproj).reshape(slots, seq_len, model_width)
    selfattn_scale_gradient = jnp.sum(first_gradient * normalized_first, axis=1)
    selfattn_offset_gradient = jnp.sum(first_gradient, axis=1)
    grad_patches = (
        between_gradient
        + normalize_reverse(
            normalized_first, inverse_deviation, first_gradient * (1.0 + selfattn_scale)
        )
    ).astype(jnp.bfloat16)
    mod_grads = (
        selfattn_offset_gradient,
        selfattn_scale_gradient,
        selfattn_gate_gradient,
        grad_shift_mlp,
        grad_scale_mlp,
        grad_gate_mlp,
    )
    grad_ada_weight, grad_ada_bias, grad_cond_act, bias_shares = tail(
        mod_grads,
        (proj_sums, grad_outproj_bias, grad_up_bias, grad_down_bias),
        gathered,
        ada_weight,
    )
    _, silu_pull = jax.vjp(jax.nn.silu, condition)
    grad_condition = silu_pull(grad_cond_act)[0]
    ff_width = activated.shape[1]
    input_factors = (
        (first_input, grad_projected, 0),
        (attended, residual_branch_gradient, 3 * model_width),
        (second_in, grad_hidden, 4 * model_width),
    )
    down_factors = ((activated, grad_mlp, 0),)
    input_block = (4 * model_width + ff_width) // 4
    down_block = model_width // 2
    block_jobs = [
        (input_factors, model_width, number * input_block, input_block) for number in range(4)
    ]
    block_jobs = block_jobs + [
        (down_factors, ff_width, number * down_block, down_block) for number in range(2)
    ]

    def reduce_block(factors, rows, first, width):
        return lax.psum_scatter(
            block_term(factors, lax.axis_size("wide") * (rows // wide_count), first, width).astype(
                jnp.bfloat16
            ),
            "wide",
            scatter_dimension=0,
            tiled=True,
        ).astype(jnp.float32)

    if not fast:
        shards = [reduce_block(*job) for job in block_jobs]
        input_grads = jnp.concatenate(shards[:4], axis=1)
        w_grads = tuple(
            lax.psum(part.astype(jnp.bfloat16), "narrow").astype(jnp.float32)
            for part in (
                input_grads[:, : 3 * model_width],
                input_grads[:, 3 * model_width : 4 * model_width],
                input_grads[:, 4 * model_width :],
                jnp.concatenate(shards[4:], axis=1),
            )
        )
    return (
        output,
        grad_patches,
        grad_condition,
        grad_ada_weight,
        grad_ada_bias,
        w_grads[0],
        bias_shares[0],
        w_grads[1],
        bias_shares[1],
        w_grads[2],
        bias_shares[2],
        w_grads[3],
        bias_shares[3],
    )


def solution(mesh):
    in_specs = (
        P(("narrow", "wide"), None, None),
        P(("narrow", "wide"), None),
        P(("narrow", "wide")),
        P(None, "wide"),
        P("wide"),
        P("wide", None),
        P("wide"),
        P("wide", None),
        P("wide"),
        P("wide", None),
        P("wide"),
        P("wide", None),
        P("wide"),
        P(("narrow", "wide"), None, None),
    )
    out_specs = (
        P(("narrow", "wide"), None, None),
        P(("narrow", "wide"), None, None),
        P(("narrow", "wide"), None),
        P(None, "wide"),
        P("wide"),
        P("wide", None),
        P("wide"),
        P("wide", None),
        P("wide"),
        P("wide", None),
        P("wide"),
        P("wide", None),
        P("wide"),
    )
    return jax.shard_map(
        per_device, mesh=mesh, in_specs=in_specs, out_specs=out_specs, check_vma=False
    )
```

```python
from functools import partial

import jax
import jax.numpy as jnp
from jax import lax
from jax.sharding import PartitionSpec as P

from jax.experimental import pallas as pl
from jax.experimental.pallas import tpu as pltpu

HEADS = 16
MESH = pl.DeviceIdType.MESH
DEPTH = 4
AHEAD = 4
EARLY = 4
GATHER_LANES = 256


norm_eps = 1e-06


def normalize(values):
    center = jnp.mean(values, axis=-1, keepdims=True)
    shifted = values - center
    inv_std = lax.rsqrt(jnp.mean(shifted * shifted, axis=-1, keepdims=True) + norm_eps)
    return (shifted * inv_std, inv_std)


def normalize_reverse(normed, inv_std, grad_normed):
    mean_grad = jnp.mean(grad_normed, axis=-1, keepdims=True)
    mean_proj = jnp.mean(grad_normed * normed, axis=-1, keepdims=True)
    return inv_std * (grad_normed - mean_grad - normed * mean_proj)


def matmul_rows(left, right):
    return jnp.dot(left, right, preferred_element_type=jnp.float32)


def matmul_back(left, right):
    return lax.dot_general(
        left, right, (((1,), (1,)), ((), ())), preferred_element_type=jnp.float32
    )


def matmul_outer(left, right):
    return lax.dot_general(
        left, right, (((0,), (0,)), ((), ())), preferred_element_type=jnp.float32
    )


def block_term(factors, count, first, width):
    pieces = []
    for left, right, base in factors:
        lower = max(first, base)
        upper = min(first + width, base + right.shape[1])
        if lower < upper:
            rows_part = lax.slice_in_dim(left, 0, count, axis=1)
            pieces.append(matmul_outer(rows_part, right[:, lower - base : upper - base]))
    return jnp.concatenate(pieces, axis=1)

LANES = 384
PER_HALF = 18


def reduce_kernel(
    projected_ref, grad_ref, lse_ref, a_in, a_out, a_up, a_down, b_out, b_up, b_down, out_ref, b_in,
    abuf, bbuf, gbuf, sbuf, tbuf, ubuf, fbuf, core_in, one_in, two_in, z_in, far_in,
    asem, bsem, core_sem, one_sem, two_sem, zs_sem, zr_sem, far_sem,
):
    narrow = lax.axis_index("narrow")
    wide = lax.axis_index("wide")
    core = wide % 2
    row = (wide // 2) % 2
    deep = wide // 4
    core_peer = (narrow, wide + 1 - 2 * core)
    x_peer = (1 - narrow, wide)
    y_peer = (narrow, wide + 2 - 4 * row)
    z_to = [(narrow, (deep + o) % 4 * 4 + wide % 4) for o in (1, 2, 3)]

    barrier = pltpu.get_barrier_semaphore()
    for peer in [core_peer, x_peer, y_peer] + z_to:
        pl.semaphore_signal(barrier, inc=1, device_id=peer, device_id_type=MESH)
    pl.semaphore_wait(barrier, 6)

    def copies(left, right, column, half):
        column = pl.multiple_of(column * LANES, LANES)
        return (
            pltpu.make_async_copy(left, abuf.at[half], asem.at[half]),
            pltpu.make_async_copy(right.at[:, pl.ds(column, LANES)], bbuf.at[half], bsem.at[half]),
        )

    def fetch(chunk, half):
        if half:
            regions = ((0, 12, None, b_down, 0), (12, 18, a_in, b_in, 3))
        else:
            regions = ((0, 12, a_up, b_up, 0), (12, 15, a_out, b_out, 0), (15, 18, a_in, b_in, 0))
        for lower, upper, left, right, offset in regions:

            @pl.when(jnp.logical_and(chunk >= lower, chunk < upper))
            def _(lower=lower, left=left, right=right, offset=offset):
                if left is None:
                    pieces = copies(a_down.at[chunk // 3], right, chunk % 3, half)
                else:
                    pieces = copies(left.at[0], right, chunk - lower + offset, half)
                for copy in pieces:
                    copy.start()

    def send(src, dst, sems, chunk, peer):
        return pltpu.make_async_remote_copy(
            src_ref=src, dst_ref=dst, send_sem=sems.at[0, chunk], recv_sem=sems.at[1, chunk],
            device_id=peer, device_id_type=MESH,
        )

    def core_copy(chunk):
        return send(gbuf.at[1 - core], core_in.at[chunk], core_sem, chunk, core_peer)

    def one_copy(chunk, even):
        slot = chunk % DEPTH
        if even:
            return send(sbuf.at[slot, 1 - narrow], one_in.at[chunk], one_sem, chunk, x_peer)
        return send(sbuf.at[slot, 1 - row], one_in.at[chunk], one_sem, chunk, y_peer)

    def two_copy(chunk, even):
        slot = chunk % DEPTH
        if even:
            return send(tbuf.at[slot, 1 - row], two_in.at[chunk], two_sem, chunk, y_peer)
        return send(tbuf.at[slot, 1 - narrow], two_in.at[chunk], two_sem, chunk, x_peer)

    def z_copies(chunk):
        slot = chunk % DEPTH
        return [
            pltpu.make_async_remote_copy(
                src_ref=ubuf.at[slot, (deep + o) % 4], dst_ref=z_in.at[chunk, o - 1],
                send_sem=zs_sem.at[chunk, o - 1], recv_sem=zr_sem.at[chunk, o - 1],
                device_id=z_to[o - 1], device_id_type=MESH,
            )
            for o in (1, 2, 3)
        ]

    def far_copy(chunk):
        return send(fbuf.at[chunk], far_in.at[chunk], far_sem, chunk, x_peer)

    def add(left, right):
        return left.astype(jnp.float32) + right.astype(jnp.float32)

    def make(chunk):
        for half in range(2):
            for copy in copies(a_in.at[0], b_up, 0, half):
                copy.wait()
            for side in range(2):
                product = jnp.dot(
                    abuf[half, side], bbuf[half], preferred_element_type=jnp.float32
                )
                for unit in range(8):
                    gbuf[side, half, unit] = product[unit * 72 : unit * 72 + 72].astype(jnp.bfloat16)

            @pl.when(chunk + 1 < PER_HALF)
            def _():
                fetch(chunk + 1, half)

        core_copy(chunk).start()

    def pair(chunk, even):
        core_copy(chunk).wait()
        slot = chunk % DEPTH

        def body(step, carry):
            half, unit = step // 8, step % 8
            value = add(gbuf[core, half, unit], core_in[chunk, half, unit]).astype(jnp.bfloat16)
            deep_at, row_at = unit // 2, unit % 2
            if even:
                sbuf[slot, half, row_at, deep_at] = value
            else:
                sbuf[slot, row_at, half, deep_at] = value
            return carry

        lax.fori_loop(0, 16, body, 0)
        one_copy(chunk, even).start()

    def first(chunk, even):
        one_copy(chunk, even).wait()
        slot = chunk % DEPTH
        mine = narrow if even else row

        def body(step, carry):
            outer, inner = step // 4, step % 4
            tbuf[slot, outer, inner] = add(
                sbuf[slot, mine, outer, inner], one_in[chunk, outer, inner]
            ).astype(jnp.bfloat16)
            return carry

        lax.fori_loop(0, 8, body, 0)
        two_copy(chunk, even).start()

    def second(chunk, even):
        two_copy(chunk, even).wait()
        slot = chunk % DEPTH
        mine = row if even else narrow

        def body(step, carry):
            ubuf[slot, step] = add(tbuf[slot, mine, step], two_in[chunk, step]).astype(jnp.bfloat16)
            return carry

        lax.fori_loop(0, 4, body, 0)
        for copy in z_copies(chunk):
            copy.start()

    def third(chunk):
        for copy in z_copies(chunk):
            copy.wait()
        total = add(ubuf[chunk % DEPTH, deep], z_in[chunk, 0])
        total = total + add(z_in[chunk, 1], z_in[chunk, 2])
        out_ref[narrow * PER_HALF + chunk] = total
        fbuf[chunk] = total.astype(jnp.bfloat16)
        far_copy(chunk).start()

    for half in range(2):
        fetch(0, half)

    seq_len = projected_ref.shape[0] // 2

    def turn(now, carry):
        for lag, action, fixed in (
            (1 + 3 * DEPTH, third, False),
            (1 + 2 * DEPTH, second, True),
            (1 + DEPTH, first, True),
            (1, pair, True),
        ):
            chunk = now - lag
            valid = jnp.logical_and(chunk >= 0, chunk < PER_HALF)
            if fixed:
                even = (2 * chunk + 10 * PER_HALF) % 5 < 2

                @pl.when(jnp.logical_and(valid, even))
                def _(action=action, chunk=chunk):
                    action(chunk, True)

                @pl.when(jnp.logical_and(valid, jnp.logical_not(even)))
                def _(action=action, chunk=chunk):
                    action(chunk, False)

            else:

                @pl.when(valid)
                def _(action=action, chunk=chunk):
                    action(chunk)

        for group in range(6):

            @pl.when(jnp.logical_and(now < 12, now % 6 == group))
            def _(group=group):
                rows = pl.ds(pl.multiple_of(now // 6 * seq_len, seq_len), seq_len)
                for head in range(HEADS * group // 6, HEADS * (group + 1) // 6):
                    attend_back_head(
                        head, projected_ref.at[rows], grad_ref.at[rows], lse_ref.at[rows], b_in.at[rows]
                    )

        @pl.when(now < PER_HALF)
        def _():
            make(now)

        return carry

    lax.fori_loop(0, PER_HALF + 3 * DEPTH + 1, turn, 0)

    def finish(chunk, carry):
        far_copy(chunk).wait()
        out_ref[(1 - narrow) * PER_HALF + chunk] = far_in[chunk].astype(jnp.float32)
        return carry

    lax.fori_loop(0, PER_HALF, finish, 0)


def reduce_weights(*operands):
    bf = jnp.bfloat16
    dma = pltpu.SemaphoreType.DMA
    unit = (72, LANES)
    n = PER_HALF
    return pl.pallas_call(
        reduce_kernel,
        out_shape=(
            jax.ShapeDtypeStruct((2 * n,) + unit, jnp.float32),
            jax.ShapeDtypeStruct(operands[0].shape, bf),
        ),
        in_specs=in_vmem(3) + [pl.BlockSpec(memory_space=pl.ANY)] * 7,
        out_specs=tuple(in_vmem(2)),
        scratch_shapes=[
            pltpu.VMEM((2,) + operands[3].shape[1:], bf),
            pltpu.VMEM((2, operands[0].shape[0], LANES), bf),
            pltpu.VMEM((2, 2, 8) + unit, bf),
            pltpu.VMEM((DEPTH, 2, 2, 4) + unit, bf),
            pltpu.VMEM((DEPTH, 2, 4) + unit, bf),
            pltpu.VMEM((DEPTH, 4) + unit, bf),
            pltpu.VMEM((n,) + unit, bf),
            pltpu.VMEM((n, 2, 8) + unit, bf),
            pltpu.VMEM((n, 2, 4) + unit, bf),
            pltpu.VMEM((n, 4) + unit, bf),
            pltpu.VMEM((n, 3) + unit, bf),
            pltpu.VMEM((n,) + unit, bf),
            dma((2,)),
            dma((2,)),
            dma((2, n)),
            dma((2, n)),
            dma((2, n)),
            dma((n, 3)),
            dma((n, 3)),
            dma((2, n)),
        ],
        compiler_params=pltpu.CompilerParams(
            collective_id=1, has_side_effects=True, vmem_limit_bytes=66_000_000
        ),
        name="reduce_weights",
    )(*operands)


def by_holder(left, parts):
    tokens = left.shape[0]
    rows = left.T.reshape(8, 2, parts, 72, tokens)
    return rows.transpose(2, 1, 0, 3, 4).reshape(parts, 2, 576, tokens)


def weight_grads(
    projected, grad_attended, log_total, first_input, attended, second_in, activated,
    grad_branch, grad_hidden, grad_mlp,
):
    done, grad_projected = reduce_weights(
        projected, grad_attended, log_total, by_holder(first_input, 1), by_holder(attended, 1),
        by_holder(second_in, 1), activated, grad_branch, grad_hidden, grad_mlp,
    )

    def flat(*pieces):
        part = jnp.concatenate(pieces) if len(pieces) > 1 else pieces[0]
        return part.transpose(1, 0, 2).reshape(72, part.shape[0] * LANES)

    down = done[18:30].reshape(4, 3, 72, LANES).transpose(0, 2, 1, 3).reshape(288, 3 * LANES)
    return grad_projected, (flat(done[15:18], done[30:]), flat(done[12:15]), flat(done[:12]), down)


def place(index, wide_count):
    return (index // wide_count, index % wide_count)


def meet(total, me, wide_count):
    barrier = pltpu.get_barrier_semaphore()

    def greet(step, carry):
        pl.semaphore_signal(
            barrier, inc=1, device_id=place((me + step) % total, wide_count), device_id_type=MESH
        )
        return carry

    lax.fori_loop(1, total, greet, 0)
    pl.semaphore_wait(barrier, total - 1)


def exchange(step, source, landing, send_sems, recv_sems, peer):
    return pltpu.make_async_remote_copy(
        src_ref=source, dst_ref=landing, send_sem=send_sems.at[step], recv_sem=recv_sems.at[step],
        device_id=peer, device_id_type=MESH,
    )


def loop(count, action):
    def body(step, carry):
        action(step)
        return carry

    lax.fori_loop(1, count, body, 0)


def gather_steps(shard_ref, full_ref, own_sem, zs_sem, zr_sem, one_sem, two_sem, core_sem):
    narrow, wide = lax.axis_index("narrow"), lax.axis_index("wide")
    core, row, deep = wide % 2, (wide // 2) % 2, wide // 4
    core_peer = (narrow, wide + 1 - 2 * core)
    x_peer = (1 - narrow, wide)
    y_peer = (narrow, wide + 2 - 4 * row)
    chunks = shard_ref.shape[1] // (2 * GATHER_LANES)

    def span(chunk, half):
        at = pl.multiple_of((chunk + half * chunks) * GATHER_LANES, GATHER_LANES)
        return pl.ds(at, GATHER_LANES)

    def send(view, sems, chunk, number, peer):
        return pltpu.make_async_remote_copy(
            src_ref=view, dst_ref=view, send_sem=sems.at[0, chunk, number],
            recv_sem=sems.at[1, chunk, number], device_id=peer, device_id_type=MESH,
        )

    def own(chunk):
        return pltpu.make_async_copy(
            shard_ref.at[:, span(chunk, narrow)],
            full_ref.at[deep, row, core, :, span(chunk, narrow)],
            own_sem.at[chunk],
        )

    def along_z(chunk):
        return [
            pltpu.make_async_remote_copy(
                src_ref=shard_ref.at[:, span(chunk, narrow)],
                dst_ref=full_ref.at[deep, row, core, :, span(chunk, narrow)],
                send_sem=zs_sem.at[chunk, o - 1], recv_sem=zr_sem.at[chunk, o - 1],
                device_id=(narrow, (deep + o) % 4 * 4 + wide % 4), device_id_type=MESH,
            )
            for o in (1, 2, 3)
        ]

    def one(chunk):
        view = full_ref.at[:, row, core, :, span(chunk, narrow)]
        return [send(view, one_sem, chunk, 0, x_peer if chunk % 2 else y_peer)]

    def two(chunk):
        if chunk % 2:
            return [
                send(full_ref.at[:, row, core, :, span(chunk, half)], two_sem, chunk, half, y_peer)
                for half in range(2)
            ]
        return [
            send(full_ref.at[:, side, core, :, span(chunk, narrow)], two_sem, chunk, side, x_peer)
            for side in range(2)
        ]

    def across(chunk):
        return [
            send(full_ref.at[:, :, core, :, span(chunk, half)], core_sem, chunk, half, core_peer)
            for half in range(2)
        ]

    def begin():
        for chunk in range(chunks):
            own(chunk).start()
        for chunk in range(AHEAD):
            for copy in along_z(chunk):
                copy.start()

    def run(lower, upper):
        stages = (lambda chunk: [own(chunk)] + along_z(chunk), one, two, across)
        for turn in range(lower, min(upper, chunks + 4)):
            if turn + AHEAD < chunks:
                for copy in along_z(turn + AHEAD):
                    copy.start()
            for stage in (2, 1, 0):
                chunk = turn - 2 * stage
                if 0 <= chunk < chunks:
                    for copy in stages[stage](chunk):
                        copy.wait()
                    for copy in stages[stage + 1](chunk):
                        copy.start()

    def end():
        run(EARLY, chunks + 4)
        for chunk in range(chunks):
            for copy in across(chunk):
                copy.wait()

    return begin, lambda: run(0, EARLY), end


def front_kernel(narrow_count, wide_count, with_weights, *refs):
    if with_weights:
        pack_ref, weight_ref, bias_ref, shard_ref, all_ref, mod_ref, full_ref = refs[:7]
        part, send_sem, recv_sem, send_two, recv_two = refs[7:12]
        begin, early, end = gather_steps(shard_ref, full_ref, *refs[12:])
    else:
        pack_ref, weight_ref, bias_ref, all_ref, mod_ref = refs[:5]
        part, send_sem, recv_sem, send_two, recv_two = refs[5:]
    total = narrow_count * wide_count
    narrow, wide = lax.axis_index("narrow"), lax.axis_index("wide")
    me = narrow * wide_count + wide
    base = narrow * wide_count
    meet(total, me, wide_count)

    def spread(step):
        return exchange(
            step, pack_ref, all_ref.at[me], send_sem, recv_sem, place((me + step) % total, wide_count)
        )

    loop(total, lambda step: spread(step).start())
    all_ref[me] = pack_ref[...]
    if with_weights:
        begin()
        early()
    loop(total, lambda step: spread(step).wait())
    rows = all_ref[pl.ds(base, wide_count)].astype(jnp.float32)
    rows = rows.reshape(wide_count * 8, rows.shape[2]).astype(jnp.bfloat16)
    product = jnp.dot(rows, weight_ref[...], preferred_element_type=jnp.float32)
    product = product + bias_ref[...].astype(jnp.float32)
    part[...] = product.reshape(part.shape).astype(jnp.bfloat16)

    def deal(step):
        to = (wide + step) % wide_count
        return exchange(step, part.at[to], mod_ref.at[wide], send_two, recv_two, (narrow, to))

    loop(wide_count, lambda step: deal(step).start())
    mod_ref[wide] = part[wide]
    if with_weights:
        end()
    loop(wide_count, lambda step: deal(step).wait())


def tail_kernel(narrow_count, wide_count, *refs):
    mod_refs, (in_ref, out_ref, up_ref, down_ref, all_ref, weight_ref) = refs[:6], refs[6:12]
    ada_ref, misc_ref, cond_ref, wide_mod, layout, gift_ref = refs[12:18]
    gifts, part, shares, send_sem, recv_sem, send_two, recv_two = refs[18:]
    total = narrow_count * wide_count
    narrow, wide = lax.axis_index("narrow"), lax.axis_index("wide")
    me = narrow * wide_count + wide
    base = narrow * wide_count
    slots, model_width = mod_refs[0].shape
    columns = layout.shape[2]
    for number, ref in enumerate(mod_refs):
        wide_mod[:slots, number * model_width : (number + 1) * model_width] = ref[...]
    layout[...] = jnp.zeros_like(layout)
    for holder in range(wide_count):
        layout[holder, :slots] = wide_mod[:slots, holder * columns : (holder + 1) * columns]
        span = 2 * model_width // wide_count
        at = holder * span
        at = at if at < model_width else at + model_width
        layout[holder, 4:5, :span] = in_ref[:, at : at + span]
        for row, ref in ((5, out_ref), (6, up_ref), (7, down_ref)):
            span = ref.shape[1] // wide_count
            layout[holder, row : row + 1, :span] = ref[:, holder * span : (holder + 1) * span]
    gift_ref[...] = layout[...].astype(jnp.bfloat16)
    meet(total, me, wide_count)

    def spread(step):
        to = (me + step) % total
        return exchange(
            step, gift_ref.at[to % wide_count], gifts.at[me], send_sem, recv_sem, place(to, wide_count)
        )

    loop(total, lambda step: spread(step).start())
    gifts[me] = gift_ref[wide]
    loop(total, lambda step: spread(step).wait())
    mine = gifts[pl.ds(base, wide_count)].astype(jnp.float32)
    mine = mine.reshape(wide_count * 8, mine.shape[2]).astype(jnp.bfloat16)
    share = matmul_back(mine, weight_ref[...])
    part[...] = share.reshape(part.shape).astype(jnp.bfloat16)

    def deal(step):
        to = (wide + step) % wide_count
        return exchange(step, part.at[to], shares.at[wide], send_two, recv_two, (narrow, to))

    loop(wide_count, lambda step: deal(step).start())
    shares[wide] = part[wide]
    every = gifts[...].astype(jnp.float32)
    misc_ref[...] = jnp.sum(every, axis=0)
    grads = every.reshape(total * 8, every.shape[2]).astype(jnp.bfloat16)
    conds = all_ref[...].astype(jnp.float32)
    conds = conds.reshape(total * 8, conds.shape[2]).astype(jnp.bfloat16)
    ada_ref[...] = matmul_outer(conds, grads)
    loop(wide_count, lambda step: deal(step).wait())
    cond_ref[...] = jnp.sum(shares[...].astype(jnp.float32), axis=0)


def in_vmem(count):
    return [pl.BlockSpec(memory_space=pltpu.VMEM)] * count


def dmas(*counts):
    return [pltpu.SemaphoreType.DMA((count,)) for count in counts]


def front(cond_act, biases, ada_weight, ada_bias, shards):
    narrow_count, wide_count = lax.axis_size("narrow"), lax.axis_size("wide")
    total = narrow_count * wide_count
    slots, model_width = cond_act.shape
    columns = ada_weight.shape[1]
    bias_row = jnp.concatenate(biases)
    bias_row = jnp.pad(bias_row, (0, model_width - bias_row.shape[0]))[None]
    pack = jnp.concatenate(
        [cond_act, bias_row, jnp.zeros((7 - slots, model_width), jnp.bfloat16)]
    )
    with_weights = narrow_count == 2 and wide_count == 16
    operands = [pack, ada_weight, ada_bias[None]]
    shapes = [
        jax.ShapeDtypeStruct((total, 8, model_width), jnp.bfloat16),
        jax.ShapeDtypeStruct((wide_count, 8, columns), jnp.bfloat16),
    ]
    out_specs = in_vmem(2)
    scratch = [pltpu.VMEM((wide_count, 8, columns), jnp.bfloat16)]
    scratch += dmas(total, total, wide_count, wide_count)
    if with_weights:
        shard = jnp.concatenate(shards, axis=1)
        operands.append(shard)
        shapes.append(jax.ShapeDtypeStruct((4, 2, 2) + shard.shape, jnp.bfloat16))
        out_specs.append(pl.BlockSpec(memory_space=pl.ANY))
        n = shard.shape[1] // (2 * GATHER_LANES)
        for dims in ((n,), (n, 3), (n, 3), (2, n, 1), (2, n, 2), (2, n, 2)):
            scratch.append(pltpu.SemaphoreType.DMA(dims))
    results = pl.pallas_call(
        partial(front_kernel, narrow_count, wide_count, with_weights),
        out_shape=tuple(shapes),
        in_specs=in_vmem(len(operands)),
        out_specs=tuple(out_specs),
        scratch_shapes=scratch,
        compiler_params=pltpu.CompilerParams(collective_id=2, has_side_effects=True),
        name="front",
    )(*operands)
    if not with_weights:
        return tuple(results) + tuple(lax.all_gather(shard, "wide", axis=0, tiled=True) for shard in shards)
    full = results[2].reshape(wide_count * shard.shape[0], shard.shape[1])
    weights, at = [], 0
    for piece in shards:
        weights.append(full[:, at : at + piece.shape[1]])
        at += piece.shape[1]
    return tuple(results[:2]) + tuple(weights)


def tail(mod_grads, bias_sums, gathered, ada_weight):
    narrow_count, wide_count = lax.axis_size("narrow"), lax.axis_size("wide")
    total = narrow_count * wide_count
    slots = mod_grads[0].shape[0]
    model_width, columns = ada_weight.shape
    operands = list(mod_grads) + [sums[None] for sums in bias_sums] + [gathered, ada_weight]
    ada, misc, cond = pl.pallas_call(
        partial(tail_kernel, narrow_count, wide_count),
        out_shape=(
            jax.ShapeDtypeStruct((model_width, columns), jnp.float32),
            jax.ShapeDtypeStruct((8, columns), jnp.float32),
            jax.ShapeDtypeStruct((8, model_width), jnp.float32),
        ),
        in_specs=in_vmem(len(operands)),
        out_specs=tuple(in_vmem(3)),
        scratch_shapes=[
            pltpu.VMEM((8, 6 * model_width), jnp.float32),
            pltpu.VMEM((wide_count, 8, columns), jnp.float32),
            pltpu.VMEM((wide_count, 8, columns), jnp.bfloat16),
            pltpu.VMEM((total, 8, columns), jnp.bfloat16),
            pltpu.VMEM((wide_count, 8, model_width), jnp.bfloat16),
            pltpu.VMEM((wide_count, 8, model_width), jnp.bfloat16),
        ]
        + dmas(total, total, wide_count, wide_count),
        compiler_params=pltpu.CompilerParams(collective_id=3, has_side_effects=True),
        name="tail",
    )(*operands)
    spans = [2 * model_width // wide_count] + [sums.shape[0] // wide_count for sums in bias_sums[1:]]
    grads = [misc[4 + number, :span] for number, span in enumerate(spans)]
    return ada, misc[:slots].sum(axis=0), cond[:slots], grads


def head_parts(ref, head, width, count):
    at = head * width
    span = width * HEADS
    return [ref[:, number * span + at : number * span + at + width] for number in range(count)]


def attend_kernel(projected_ref, out_ref, lse_ref):
    width = out_ref.shape[2] // HEADS
    scale = width ** (-0.5)
    for head in range(HEADS):
        query, key, value = head_parts(projected_ref.at[0], head, width, 3)
        scores = matmul_back(query, key) * scale
        top = jnp.max(scores, axis=-1, keepdims=True)
        lse = top + jnp.log(jnp.sum(jnp.exp(scores - top), axis=-1, keepdims=True))
        probs = jnp.exp(scores - lse).astype(jnp.bfloat16)
        out_ref[0, :, head * width : head * width + width] = matmul_rows(probs, value).astype(
            jnp.bfloat16
        )
        lse_ref[0, :, head : head + 1] = lse


def attend_back_head(head, projected_ref, grad_ref, lse_ref, out_ref):
    model_width = grad_ref.shape[1]
    width = model_width // HEADS
    scale = width ** (-0.5)
    query, key, value = head_parts(projected_ref, head, width, 3)
    (grad,) = head_parts(grad_ref, head, width, 1)
    scores = matmul_back(query, key) * scale
    probs = jnp.exp(scores - lse_ref[:, head : head + 1])
    grad_value = matmul_outer(probs.astype(jnp.bfloat16), grad)
    grad_probs = matmul_back(grad, value)
    row_dot = jnp.sum(grad_probs * probs, axis=-1, keepdims=True)
    grad_scores = (probs * (grad_probs - row_dot)).astype(jnp.bfloat16)
    grad_query = matmul_rows(grad_scores, key) * scale
    grad_key = matmul_outer(grad_scores, query) * scale
    for number, part in enumerate((grad_query, grad_key, grad_value)):
        at = number * model_width + head * width
        out_ref[:, at : at + width] = part.astype(jnp.bfloat16)


def attend_back_kernel(*refs):
    for head in range(HEADS):
        attend_back_head(head, *[ref.at[0] for ref in refs])


def by_image(shape):
    return pl.BlockSpec((1,) + shape[1:], lambda image: (image, 0, 0))


def attend_call(kernel, operands, shapes, name):
    slots, seq_len = operands[0].shape[:2]
    work = slots * seq_len * seq_len
    return pl.pallas_call(
        kernel,
        grid=(slots,),
        out_shape=shapes,
        in_specs=[by_image(operand.shape) for operand in operands],
        out_specs=jax.tree.map(lambda shape: by_image(shape.shape), shapes),
        cost_estimate=pl.CostEstimate(
            flops=8 * work * operands[0].shape[2] // 3,
            bytes_accessed=sum(operand.size * 2 for operand in operands) * 2,
            transcendentals=work * HEADS,
        ),
        name=name,
    )(*operands)


def per_device(
    patches,
    condition,
    image_counts,
    ada_weight,
    ada_bias,
    inproj_weight,
    inproj_bias,
    outproj_weight,
    outproj_bias,
    up_weight,
    up_bias,
    down_weight,
    down_bias,
    cotangent,
):
    slots, seq_len, model_width = patches.shape
    row_total = slots * seq_len
    wide_count = lax.axis_size("wide")
    live = (jnp.arange(slots) < image_counts[0]).astype(jnp.float32)[:, None, None]
    cond_act = jax.nn.silu(condition).astype(jnp.bfloat16)
    gathered, mod_blocks, w_inproj, w_outproj, w_up = front(
        cond_act, (inproj_bias, outproj_bias, up_bias, down_bias), ada_weight, ada_bias,
        (inproj_weight, outproj_weight, up_weight),
    )
    down_weight, mod_blocks = lax.optimization_barrier((down_weight, mod_blocks))
    modulation = (
        mod_blocks[:, :slots].transpose(1, 0, 2).reshape(slots, 6 * model_width).astype(jnp.float32)
    )
    group = lax.dynamic_slice_in_dim(
        gathered[:, slots], lax.axis_index("narrow") * wide_count, wide_count
    )
    all_biases, bias_at = [], 0
    for bias in (inproj_bias, outproj_bias, up_bias, down_bias):
        all_biases.append(group[:, bias_at : bias_at + bias.shape[0]].reshape(-1))
        bias_at += bias.shape[0]
    b_inproj, b_outproj, b_up, b_down = all_biases
    segment_list = [
        modulation[:, None, number * model_width : (number + 1) * model_width]
        for number in range(6)
    ]
    (
        selfattn_offset,
        selfattn_scale,
        selfattn_gate,
        perceptron_offset,
        perceptron_scale,
        perceptron_gate,
    ) = segment_list
    w_down = lax.all_gather(down_weight, "wide", axis=0, tiled=True)
    input_rows = patches.astype(jnp.float32)
    normalized_first, inverse_deviation = normalize(input_rows)
    first_input = (
        (normalized_first * (1.0 + selfattn_scale) + selfattn_offset)
        .astype(jnp.bfloat16)
        .reshape(row_total, model_width)
    )
    proj_bias = b_inproj.astype(jnp.float32)
    full_bias = jnp.concatenate(
        [proj_bias[:model_width], jnp.zeros((model_width,), jnp.float32), proj_bias[model_width:]]
    )
    projected = (matmul_rows(first_input, w_inproj) + full_bias).astype(jnp.bfloat16)
    projected = projected.reshape(slots, seq_len, 3 * model_width)
    attended, log_total = attend_call(
        attend_kernel,
        (projected,),
        (
            jax.ShapeDtypeStruct((slots, seq_len, model_width), jnp.bfloat16),
            jax.ShapeDtypeStruct((slots, seq_len, HEADS), jnp.float32),
        ),
        "attend",
    )
    attended = attended.reshape(row_total, model_width)
    residual_branch = (matmul_rows(attended, w_outproj) + b_outproj.astype(jnp.float32)).reshape(
        slots, seq_len, model_width
    )
    between_state = input_rows + selfattn_gate * residual_branch
    normed_b, inv_b = normalize(between_state)
    second_in = (
        (normed_b * (1.0 + perceptron_scale) + perceptron_offset)
        .astype(jnp.bfloat16)
        .reshape(row_total, model_width)
    )
    hidden = matmul_rows(second_in, w_up) + b_up.astype(jnp.float32)
    gelu_value, gelu_pull = jax.vjp(partial(jax.nn.gelu, approximate=True), hidden)
    activated = gelu_value.astype(jnp.bfloat16)
    fast = lax.axis_size("narrow") == 2 and wide_count == 16
    if fast:
        held_activated = by_holder(activated, 4)
        w_down, activated, held_activated = lax.optimization_barrier(
            (w_down, activated, held_activated)
        )
    mlp_out = (matmul_rows(activated, w_down) + b_down.astype(jnp.float32)).reshape(
        slots, seq_len, model_width
    )
    output = ((between_state + perceptron_gate * mlp_out) * live).astype(jnp.bfloat16)
    wb_inproj, wb_outproj, wb_up, wb_down = w_inproj, w_outproj, w_up, w_down
    grad_out = cotangent.astype(jnp.float32) * live
    grad_gate_mlp = jnp.sum(grad_out * mlp_out, axis=1)
    grad_mlp = (grad_out * perceptron_gate).astype(jnp.bfloat16).reshape(row_total, model_width)
    grad_down_bias = jnp.sum(grad_mlp.astype(jnp.float32), axis=0)
    grad_act = matmul_back(grad_mlp, wb_down)
    grad_hidden = gelu_pull(grad_act)[0].astype(jnp.bfloat16)
    grad_up_bias = jnp.sum(grad_hidden.astype(jnp.float32), axis=0)
    grad_second = matmul_back(grad_hidden, wb_up).reshape(slots, seq_len, model_width)
    grad_scale_mlp = jnp.sum(grad_second * normed_b, axis=1)
    grad_shift_mlp = jnp.sum(grad_second, axis=1)
    between_gradient = grad_out + normalize_reverse(
        normed_b, inv_b, grad_second * (1.0 + perceptron_scale)
    )
    selfattn_gate_gradient = jnp.sum(between_gradient * residual_branch, axis=1)
    residual_branch_gradient = (
        (between_gradient * selfattn_gate).astype(jnp.bfloat16).reshape(row_total, model_width)
    )
    grad_outproj_bias = jnp.sum(residual_branch_gradient.astype(jnp.float32), axis=0)
    grad_attended = (
        matmul_back(residual_branch_gradient, wb_outproj)
        .astype(jnp.bfloat16)
        .reshape(slots, seq_len, model_width)
    )
    if fast:
        grad_projected, w_grads = weight_grads(
            projected.reshape(row_total, 3 * model_width),
            grad_attended.reshape(row_total, model_width),
            log_total.reshape(row_total, HEADS),
            first_input, attended, second_in, held_activated,
            residual_branch_gradient, grad_hidden, grad_mlp,
        )
    else:
        grad_projected = attend_call(
            attend_back_kernel,
            (projected, grad_attended, log_total),
            jax.ShapeDtypeStruct((slots, seq_len, 3 * model_width), jnp.bfloat16),
            "attend_back",
        ).reshape(row_total, 3 * model_width)
    proj_sums = jnp.sum(grad_projected.astype(jnp.float32), axis=0)
    first_gradient = matmul_back(grad_projected, wb_inproj).reshape(slots, seq_len, model_width)
    selfattn_scale_gradient = jnp.sum(first_gradient * normalized_first, axis=1)
    selfattn_offset_gradient = jnp.sum(first_gradient, axis=1)
    grad_patches = (
        between_gradient
        + normalize_reverse(
            normalized_first, inverse_deviation, first_gradient * (1.0 + selfattn_scale)
        )
    ).astype(jnp.bfloat16)
    mod_grads = (
        selfattn_offset_gradient,
        selfattn_scale_gradient,
        selfattn_gate_gradient,
        grad_shift_mlp,
        grad_scale_mlp,
        grad_gate_mlp,
    )
    grad_ada_weight, grad_ada_bias, grad_cond_act, bias_shares = tail(
        mod_grads,
        (proj_sums, grad_outproj_bias, grad_up_bias, grad_down_bias),
        gathered,
        ada_weight,
    )
    _, silu_pull = jax.vjp(jax.nn.silu, condition)
    grad_condition = silu_pull(grad_cond_act)[0]
    ff_width = activated.shape[1]
    input_factors = (
        (first_input, grad_projected, 0),
        (attended, residual_branch_gradient, 3 * model_width),
        (second_in, grad_hidden, 4 * model_width),
    )
    down_factors = ((activated, grad_mlp, 0),)
    input_block = (4 * model_width + ff_width) // 4
    down_block = model_width // 2
    block_jobs = [
        (input_factors, model_width, number * input_block, input_block) for number in range(4)
    ]
    block_jobs = block_jobs + [
        (down_factors, ff_width, number * down_block, down_block) for number in range(2)
    ]

    def reduce_block(factors, rows, first, width):
        return lax.psum_scatter(
            block_term(factors, lax.axis_size("wide") * (rows // wide_count), first, width).astype(
                jnp.bfloat16
            ),
            "wide",
            scatter_dimension=0,
            tiled=True,
        ).astype(jnp.float32)

    if not fast:
        shards = [reduce_block(*job) for job in block_jobs]
        input_grads = jnp.concatenate(shards[:4], axis=1)
        w_grads = tuple(
            lax.psum(part.astype(jnp.bfloat16), "narrow").astype(jnp.float32)
            for part in (
                input_grads[:, : 3 * model_width],
                input_grads[:, 3 * model_width : 4 * model_width],
                input_grads[:, 4 * model_width :],
                jnp.concatenate(shards[4:], axis=1),
            )
        )
    return (
        output,
        grad_patches,
        grad_condition,
        grad_ada_weight,
        grad_ada_bias,
        w_grads[0],
        bias_shares[0],
        w_grads[1],
        bias_shares[1],
        w_grads[2],
        bias_shares[2],
        w_grads[3],
        bias_shares[3],
    )


def solution(mesh):
    in_specs = (
        P(("narrow", "wide"), None, None),
        P(("narrow", "wide"), None),
        P(("narrow", "wide")),
        P(None, "wide"),
        P("wide"),
        P("wide", None),
        P("wide"),
        P("wide", None),
        P("wide"),
        P("wide", None),
        P("wide"),
        P("wide", None),
        P("wide"),
        P(("narrow", "wide"), None, None),
    )
    out_specs = (
        P(("narrow", "wide"), None, None),
        P(("narrow", "wide"), None, None),
        P(("narrow", "wide"), None),
        P(None, "wide"),
        P("wide"),
        P("wide", None),
        P("wide"),
        P("wide", None),
        P("wide"),
        P("wide", None),
        P("wide"),
        P("wide", None),
        P("wide"),
    )
    return jax.shard_map(
        per_device, mesh=mesh, in_specs=in_specs, out_specs=out_specs, check_vma=False
    )
```
